32 devices in a mesh: dp: 8 (over y, x, core), rep: 4 (over z).
Axes of the slice: x: 2, y: 2, z: 4, core: 2. Of those that a mesh axis runs over, the one named last changes fastest.
Arguments:
- audio_patches: bfloat16 [2, 64, 228, 256], P(None, ('dp', 'rep')), may hold values from -6 to 6
- clip_lengths: int32 [2, 64], P(None, ('dp', 'rep')), may hold values from 114 to 228, as said below
- video_ids: int32 [2, 64], P(None, ('dp', 'rep')), may hold values from 0 to 31
- image_tokens: bfloat16 [2, 64, 256, 1280], P(None, ('dp', 'rep')), may hold values from -6 to 6
- i_qkv: bfloat16 [1280, 3840], P('dp'), may hold values from -0.15625 to 0.15625
- i_out: bfloat16 [1280, 1280], P('dp'), may hold values from -0.625 to 0.625
- i_up: bfloat16 [1280, 5120], P('dp'), may hold values from -0.15625 to 0.15625
- i_down: bfloat16 [5120, 1280], P('dp'), may hold values from -0.078125 to 0.078125
- i_proj: bfloat16 [1280, 1024], P('dp'), may hold values from -0.15625 to 0.15625
- i_gains: bfloat16 [3, 1280], P(None, 'dp'), may hold values from 0.5 to 1.5
- a_patch: float32 [256, 768], P('dp'), may hold values from -0.375 to 0.375
- a_qkv: float32 [768, 2304], P('dp'), may hold values from -0.21875 to 0.21875
- a_out: float32 [768, 768], P('dp'), may hold values from -0.875 to 0.875
- a_up: float32 [768, 3072], P('dp'), may hold values from -0.21875 to 0.21875
- a_down: float32 [3072, 768], P('dp'), may hold values from -0.109375 to 0.109375
- a_proj: float32 [768, 1024], P('dp'), may hold values from -0.21875 to 0.21875
- a_gains: float32 [3, 768], P(None, 'dp'), may hold values from 0.5 to 1.5
- m_patch: float32 [256, 768], P('dp'), may hold values from -5.722046e-06 to 5.722046e-06
- m_qkv: float32 [768, 2304], P('dp'), may hold values from -5.722046e-06 to 5.722046e-06
- m_out: float32 [768, 768], P('dp'), may hold values from -5.722046e-06 to 5.722046e-06
- m_up: float32 [768, 3072], P('dp'), may hold values from -5.722046e-06 to 5.722046e-06
- m_down: float32 [3072, 768], P('dp'), may hold values from -5.722046e-06 to 5.722046e-06
- m_proj: float32 [768, 1024], P('dp'), may hold values from -5.722046e-06 to 5.722046e-06
- m_gains: float32 [3, 768], P(None, 'dp'), may hold values from -2.2888184e-05 to 2.2888184e-05
- s_patch: float32 [256, 768], P('dp'), may hold values from 1.2405519e-14 to 4.9622077e-14
- s_qkv: float32 [768, 2304], P('dp'), may hold values from 1.2405519e-14 to 4.9622077e-14
- s_out: float32 [768, 768], P('dp'), may hold values from 1.2405519e-14 to 4.9622077e-14
- s_up: float32 [768, 3072], P('dp'), may hold values from 1.2405519e-14 to 4.9622077e-14
- s_down: float32 [3072, 768], P('dp'), may hold values from 1.2405519e-14 to 4.9622077e-14
- s_proj: float32 [768, 1024], P('dp'), may hold values from 1.2405519e-14 to 4.9622077e-14
- s_gains: float32 [3, 768], P(None, 'dp'), may hold values from 1.9848831e-13 to 7.9395323e-13
Outputs:
- loss: float32 [], replicated
- grad_norm: float32 [], replicated
- new_patch: float32 [256, 768], P('dp')
- new_qkv: float32 [768, 2304], P('dp')
- new_out: float32 [768, 768], P('dp')
- new_up: float32 [768, 3072], P('dp')
- new_down: float32 [3072, 768], P('dp')
- new_proj: float32 [768, 1024], P('dp')
- new_gains: float32 [3, 768], P(None, 'dp')
- first_patch: float32 [256, 768], P('dp')
- first_qkv: float32 [768, 2304], P('dp')
- first_out: float32 [768, 768], P('dp')
- first_up: float32 [768, 3072], P('dp')
- first_down: float32 [3072, 768], P('dp')
- first_proj: float32 [768, 1024], P('dp')
- first_gains: float32 [3, 768], P(None, 'dp')
- second_patch: float32 [256, 768], P('dp')
- second_qkv: float32 [768, 2304], P('dp')
- second_out: float32 [768, 768], P('dp')
- second_up: float32 [768, 3072], P('dp')
- second_down: float32 [3072, 768], P('dp')
- second_proj: float32 [768, 1024], P('dp')
- second_gains: float32 [3, 768], P(None, 'dp')
The draws below stay inside these ranges and needn't reach their ends.
Inputs may be any that keep to these rules, and one draw needn't show every extreme that they name: `clip_lengths`: each clip has 228 or 114 patches; in every micro-batch the first clip has 228 and the second 228 // 2.
All inputs are finite; a program needn't handle non-finite values.
Results may differ from the reference program's by a relative error of at most 0.014.
Values may be sent and summed in bfloat16 or wider, within the bound.
No kernel may reach another device: no remote copies, remote signals or barrier semaphores. Data moves between devices by JAX's collectives and lax.ppermute only.
A program may use at most 256 MiB of HBM per device.

```python
import math
import jax
import jax.numpy as jnp
from jax import lax

D_A = 768
HEADS_A = 12
FF_A = 3072
PATCH = 256
PROJ = 1024
D_I = 1280
HEADS_I = 16
FF_I = 5120
LEN = 228
IMG_LEN = 256
MICRO = 2
STEP = 7
CLIPS = 64


def draw_clip_lengths(key, part):
    picks = jax.random.randint(key, (MICRO, CLIPS), 0, 2)
    column = jnp.arange(CLIPS)[None, :]
    picks = jnp.where(column == 0, 1, jnp.where(column == 1, 0, picks))
    return (LEN // 2 * (1 + picks)).astype(jnp.int32)


def plant(drawn, own_key, low, top_value):
    longest = drawn.shape.index(max(drawn.shape))
    spots = []
    for shift in (0, 1):
        where = [jax.random.randint(jax.random.fold_in(own_key, axis), (), 0, length) for axis, length in enumerate(drawn.shape)]
        where[longest] = (where[longest] + shift) % drawn.shape[longest]
        spots.append(tuple(where))
    return drawn.at[spots[0]].set(low).at[spots[1]].set(top_value)


def level_of(rng, dims, split, low, high):
    factor_of, own = 1.0, jax.random.fold_in(rng, 6)
    for position, parts in split:
        draws = jnp.exp(jax.random.uniform(jax.random.fold_in(own, position), (parts,), jnp.float32, low / len(split), high / len(split)))
        factor_of = factor_of * jnp.repeat(draws, dims[position] // parts).reshape([-1 if axis == position else 1 for axis in range(len(dims))])
    return factor_of


def normal_values(rng, dims, width, reach, split=(), kind=jnp.bfloat16):
    level = level_of(rng, dims, split, -0.22, 0.18) if split else 1.0
    drawn = jax.random.normal(rng, dims, jnp.float32) * width * level
    return jnp.minimum(jnp.maximum(drawn, -reach), reach).astype(kind)


def setup_inputs(seed: int = 0) -> dict:
    arg_keys = jax.random.split(jax.random.key(seed), 32)
    return {
        "audio_patches": normal_values(arg_keys[0], (MICRO, CLIPS, LEN, PATCH), 1.0, 6.0, ((1, 32),)),
        "clip_lengths": draw_clip_lengths(jax.random.fold_in(arg_keys[31], 71), 0),
        "video_ids": plant(jax.random.randint(arg_keys[2], (MICRO, CLIPS), 0, CLIPS // 2), jax.random.fold_in(arg_keys[2], 1), 0, (CLIPS // 2) - 1).astype(jnp.int32),
        "image_tokens": normal_values(arg_keys[3], (MICRO, CLIPS, IMG_LEN, D_I), 1.0, 6.0, ((1, 32),)),
        "i_qkv": normal_values(arg_keys[4], (D_I, 3 * D_I), D_I ** -0.5, 0.15625, ((0, 8),)),
        "i_out": normal_values(arg_keys[5], (D_I, D_I), (D_I // 16) ** -0.5, 0.625, ((0, 8),)),
        "i_up": normal_values(arg_keys[6], (D_I, FF_I), D_I ** -0.5, 0.15625, ((0, 8),)),
        "i_down": normal_values(arg_keys[7], (FF_I, D_I), FF_I ** -0.5, 0.078125, ((0, 8),)),
        "i_proj": normal_values(arg_keys[8], (D_I, PROJ), D_I ** -0.5, 0.15625, ((0, 8),)),
        "i_gains": jnp.clip(1.0 + 0.1 * jax.random.normal(arg_keys[9], (3, D_I), jnp.float32), 0.5, 1.5).astype(jnp.bfloat16),
        "a_patch": normal_values(arg_keys[10], (PATCH, D_A), PATCH ** -0.5, 0.375, ((0, 8),), jnp.float32),
        "a_qkv": normal_values(arg_keys[11], (D_A, 3 * D_A), D_A ** -0.5, 0.21875, ((0, 8),), jnp.float32),
        "a_out": normal_values(arg_keys[12], (D_A, D_A), (D_A // 16) ** -0.5, 0.875, ((0, 8),), jnp.float32),
        "a_up": normal_values(arg_keys[13], (D_A, FF_A), D_A ** -0.5, 0.21875, ((0, 8),), jnp.float32),
        "a_down": normal_values(arg_keys[14], (FF_A, D_A), FF_A ** -0.5, 0.109375, ((0, 8),), jnp.float32),
        "a_proj": normal_values(arg_keys[15], (D_A, PROJ), D_A ** -0.5, 0.21875, ((0, 8),), jnp.float32),
        "a_gains": jnp.clip(1.0 + 0.1 * jax.random.normal(arg_keys[16], (3, D_A), jnp.float32), 0.5, 1.5),
        "m_patch": normal_values(arg_keys[17], (PATCH, D_A), (0.0011 * (PATCH * D_A + 4 * D_A * D_A + 2 * D_A * FF_A + D_A * PROJ) ** -0.5), 5.7220458984375e-06, ((0, 8),), jnp.float32),
        "m_qkv": normal_values(arg_keys[18], (D_A, 3 * D_A), (0.0011 * (PATCH * D_A + 4 * D_A * D_A + 2 * D_A * FF_A + D_A * PROJ) ** -0.5), 5.7220458984375e-06, ((0, 8),), jnp.float32),
        "m_out": normal_values(arg_keys[19], (D_A, D_A), (0.0011 * (PATCH * D_A + 4 * D_A * D_A + 2 * D_A * FF_A + D_A * PROJ) ** -0.5), 5.7220458984375e-06, ((0, 8),), jnp.float32),
        "m_up": normal_values(arg_keys[20], (D_A, FF_A), (0.0011 * (PATCH * D_A + 4 * D_A * D_A + 2 * D_A * FF_A + D_A * PROJ) ** -0.5), 5.7220458984375e-06, ((0, 8),), jnp.float32),
        "m_down": normal_values(arg_keys[21], (FF_A, D_A), (0.0011 * (PATCH * D_A + 4 * D_A * D_A + 2 * D_A * FF_A + D_A * PROJ) ** -0.5), 5.7220458984375e-06, ((0, 8),), jnp.float32),
        "m_proj": normal_values(arg_keys[22], (D_A, PROJ), (0.0011 * (PATCH * D_A + 4 * D_A * D_A + 2 * D_A * FF_A + D_A * PROJ) ** -0.5), 5.7220458984375e-06, ((0, 8),), jnp.float32),
        "m_gains": normal_values(arg_keys[23], (3, D_A), (0.0044 * (PATCH * D_A + 4 * D_A * D_A + 2 * D_A * FF_A + D_A * PROJ) ** -0.5), 2.288818359375e-05, ((1, 8),), jnp.float32),
        "s_patch": jnp.clip(jnp.exp(math.log(4.9622076738441157e-14) - 1.3862944 * jax.random.uniform(arg_keys[24], (PATCH, D_A), jnp.float32) ** level_of(arg_keys[24], (PATCH, D_A), ((0, 8),), -0.2, 0.2)), 1.2405519184610289e-14, 4.9622076738441157e-14),
        "s_qkv": jnp.clip(jnp.exp(math.log(4.9622076738441157e-14) - 1.3862944 * jax.random.uniform(arg_keys[25], (D_A, 3 * D_A), jnp.float32) ** level_of(arg_keys[25], (D_A, 3 * D_A), ((0, 8),), -0.2, 0.2)), 1.2405519184610289e-14, 4.9622076738441157e-14),
        "s_out": jnp.clip(jnp.exp(math.log(4.9622076738441157e-14) - 1.3862944 * jax.random.uniform(arg_keys[26], (D_A, D_A), jnp.float32) ** level_of(arg_keys[26], (D_A, D_A), ((0, 8),), -0.2, 0.2)), 1.2405519184610289e-14, 4.9622076738441157e-14),
        "s_up": jnp.clip(jnp.exp(math.log(4.9622076738441157e-14) - 1.3862944 * jax.random.uniform(arg_keys[27], (D_A, FF_A), jnp.float32) ** level_of(arg_keys[27], (D_A, FF_A), ((0, 8),), -0.2, 0.2)), 1.2405519184610289e-14, 4.9622076738441157e-14),
        "s_down": jnp.clip(jnp.exp(math.log(4.9622076738441157e-14) - 1.3862944 * jax.random.uniform(arg_keys[28], (FF_A, D_A), jnp.float32) ** level_of(arg_keys[28], (FF_A, D_A), ((0, 8),), -0.2, 0.2)), 1.2405519184610289e-14, 4.9622076738441157e-14),
        "s_proj": jnp.clip(jnp.exp(math.log(4.9622076738441157e-14) - 1.3862944 * jax.random.uniform(arg_keys[29], (D_A, PROJ), jnp.float32) ** level_of(arg_keys[29], (D_A, PROJ), ((0, 8),), -0.2, 0.2)), 1.2405519184610289e-14, 4.9622076738441157e-14),
        "s_gains": jnp.clip(jnp.exp(math.log(7.939532278150585e-13) - 1.3862944 * jax.random.uniform(arg_keys[30], (3, D_A), jnp.float32) ** level_of(arg_keys[30], (3, D_A), ((1, 8),), -0.2, 0.2)), 1.9848830695376463e-13, 7.939532278150585e-13),
    }


HIGHEST = lax.Precision.HIGHEST
NORM_EPS = 1e-06
LOGIT_SCALE = 50.0
CLIP_NORM = 0.01
BETA_ONE = 0.9
BETA_TWO = 0.999
ADAM_EPS = 1e-08
WEIGHT_DECAY = 0.1
RATE_MATRIX = 0.05
RATE_GAIN = 0.3

@jax.custom_vjp
def low(v):
    return lax.optimization_barrier(v.astype(jnp.bfloat16)).astype(jnp.float32)

@jax.custom_vjp
def low_back(v):
    return v

def low_keep(v):
    return (low(v), None)

def low_pass(kept, grad):
    return (grad,)

def back_keep(v):
    return (v, None)

def back_low(kept, grad):
    return (low(grad),)
low.defvjp(low_keep, low_pass)
low_back.defvjp(back_keep, back_low)

def normed(resid, gain):
    center = resid - lax.optimization_barrier(jnp.mean(resid, axis=-1, keepdims=True))
    spread = lax.optimization_barrier(jnp.mean(center * center, axis=-1, keepdims=True))
    return center * lax.rsqrt(spread + NORM_EPS) * gain

def unit_rows(embed_raw):
    return embed_raw * lax.rsqrt(lax.optimization_barrier(jnp.sum(embed_raw * embed_raw, axis=-1, keepdims=True)) + NORM_EPS)

def matmul(left, right):
    return jnp.einsum('cld,de->cle', left, right, precision=HIGHEST)

def layer(resid_in, weights, norm_gains, valid, heads):
    w_qkv, w_out, w_up, w_down = weights
    clip_count, length, feature = resid_in.shape
    head_dim = feature // heads
    h_one = low(normed(resid_in, norm_gains[0]))
    qkv = low(low_back(matmul(h_one, w_qkv))).reshape(clip_count, length, 3, heads, head_dim)
    scores = low_back(jnp.einsum('clhd,cmhd->chlm', qkv[:, :, 0], qkv[:, :, 1], precision=HIGHEST) * head_dim ** (-0.5))
    scores = jnp.where(valid[:, None, None, :], scores, -1e+30)
    attn_probs = jax.nn.softmax(scores, axis=-1)
    attn_mixed = jnp.einsum('chlm,cmhd->clhd', low(attn_probs), qkv[:, :, 2], precision=HIGHEST)
    attn_mixed = low(low_back(attn_mixed.reshape(clip_count, length, feature)))
    resid_mid = resid_in + low_back(matmul(attn_mixed, w_out))
    h_two = low(normed(resid_mid, norm_gains[1]))
    pre_act = low_back(matmul(h_two, w_up))
    hidden = low(jax.nn.gelu(pre_act))
    return resid_mid + low_back(matmul(hidden, w_down))

def embed(resid_out, gain, pool_weight, w_proj):
    pooled = lax.optimization_barrier(jnp.sum(normed(resid_out, gain) * pool_weight[:, :, None], axis=1))
    embed_raw = low_back(jnp.dot(low(pooled), w_proj, precision=HIGHEST))
    return low(unit_rows(embed_raw))

def contrast(audio, image, ids):
    logits = jnp.dot(audio, image.T, precision=HIGHEST) * LOGIT_SCALE
    count_rows = ids.shape[0]
    same = jnp.arange(count_rows)[:, None] == jnp.arange(count_rows)[None, :]
    allowed = jnp.logical_or(ids[:, None] != ids[None, :], same)
    masked = jnp.where(allowed, logits, -1e+30)
    matched = lax.optimization_barrier(jnp.sum(jnp.where(same, logits, 0.0), axis=1))
    row_lse = jax.nn.logsumexp(masked, axis=1)
    col_lse = jax.nn.logsumexp(masked, axis=0)
    return jnp.sum(row_lse - matched) + jnp.sum(col_lse - matched)

def adam_step(weight, gradient, moment_one, moment_two, step_rate, decay):
    first_new = BETA_ONE * moment_one + (1.0 - BETA_ONE) * gradient
    second_new = BETA_TWO * moment_two + (1.0 - BETA_TWO) * gradient * gradient
    fixed_one = first_new / (1.0 - BETA_ONE ** STEP)
    fixed_two = second_new / (1.0 - BETA_TWO ** STEP)
    update = fixed_one / (jnp.sqrt(fixed_two) + ADAM_EPS) + decay * weight
    return (weight - step_rate * update, first_new, second_new)

def reference(audio_patches, clip_lengths, video_ids, image_tokens, i_qkv, i_out, i_up, i_down, i_proj, i_gains, a_patch, a_qkv, a_out, a_up, a_down, a_proj, a_gains, m_patch, m_qkv, m_out, m_up, m_down, m_proj, m_gains, s_patch, s_qkv, s_out, s_up, s_down, s_proj, s_gains):
    image_w = tuple((w.astype(jnp.float32) for w in (i_qkv, i_out, i_up, i_down, i_proj)))
    image_g = i_gains.astype(jnp.float32)
    masters = (a_patch, a_qkv, a_out, a_up, a_down, a_proj, a_gains)
    firsts = (m_patch, m_qkv, m_out, m_up, m_down, m_proj, m_gains)
    seconds = (s_patch, s_qkv, s_out, s_up, s_down, s_proj, s_gains)
    same = jnp.arange(CLIPS)[:, None] == jnp.arange(CLIPS)[None, :]
    allowed = jnp.logical_or(video_ids[:, :, None] != video_ids[:, None, :], same[None])
    loss_scale = CLIPS / jnp.sum(allowed.astype(jnp.float32))
    image_embeds = []
    image_valid = jnp.ones((CLIPS, IMG_LEN), dtype=bool)
    image_pool = jnp.ones((CLIPS, IMG_LEN), jnp.float32) / IMG_LEN
    for micro in range(MICRO):
        image_out = layer(image_tokens[micro].astype(jnp.float32), image_w[:4], image_g, image_valid, HEADS_I)
        image_embeds.append(embed(image_out, image_g[2], image_pool, image_w[4]))
    positions = jnp.arange(LEN)
    patches = audio_patches.astype(jnp.float32)

    def loss_of(params):
        copies_low = tuple((low(w) for w in params))
        loss_sum = 0.0
        for micro in range(MICRO):
            lengths_now = clip_lengths[micro]
            valid = positions[None, :] < lengths_now[:, None]
            pool_weight = valid.astype(jnp.float32) / lengths_now[:, None].astype(jnp.float32)
            resid_in = low_back(jnp.einsum('clp,pd->cld', patches[micro], copies_low[0], precision=HIGHEST))
            resid_out = layer(resid_in, copies_low[1:5], copies_low[6], valid, HEADS_A)
            audio_embed = embed(resid_out, copies_low[6][2], pool_weight, copies_low[5])
            loss_sum = loss_sum + contrast(audio_embed, image_embeds[micro], video_ids[micro])
        return loss_sum * loss_scale
    loss, loss_back = jax.vjp(loss_of, masters)
    grads = loss_back(jnp.ones_like(loss))[0]
    grad_norm = jnp.sqrt(sum((jnp.sum(g * g) for g in grads)))
    factor = jnp.minimum(1.0, CLIP_NORM / grad_norm)
    results = []
    for index in range(7):
        step_rate = RATE_GAIN if index == 6 else RATE_MATRIX
        decay = 0.0 if index == 6 else WEIGHT_DECAY
        results.append(adam_step(masters[index], grads[index] * factor, firsts[index], seconds[index], step_rate, decay))
    new_w = tuple((r[0] for r in results))
    new_one = tuple((r[1] for r in results))
    new_two = tuple((r[2] for r in results))
    return (loss, grad_norm, new_w[0], new_w[1], new_w[2], new_w[3], new_w[4], new_w[5], new_w[6], new_one[0], new_one[1], new_one[2], new_one[3], new_one[4], new_one[5], new_one[6], new_two[0], new_two[1], new_two[2], new_two[3], new_two[4], new_two[5], new_two[6])
```

```python
import functools

import jax
import jax.numpy as jnp
from jax import lax
from jax.experimental import pallas as pl
from jax.experimental.pallas import tpu as pltpu
from jax.sharding import PartitionSpec as P

HEADS_A = 12
HEADS_I = 16
LEN = 228
IMG_LEN = 256
MICRO = 2
STEP = 7

HIGHEST = lax.Precision.HIGHEST
F32 = jnp.float32
BF16 = jnp.bfloat16
NORM_EPS = 1e-06
LOGIT_SCALE = 50.0
CLIP_NORM = 0.01
BETA_ONE = 0.9
BETA_TWO = 0.999
ADAM_EPS = 1e-08
WEIGHT_DECAY = 0.1
RATE_MATRIX = 0.05
RATE_GAIN = 0.3
PAD_LEN = 240
GELU_C = 0.7978845608028654
GELU_A = 0.044715
MIB = 1 << 20


def to_low(v):
    return v.astype(BF16)


def normed(resid, gain):
    center = resid - jnp.mean(resid, axis=-1, keepdims=True)
    spread = jnp.mean(center * center, axis=-1, keepdims=True)
    return center * lax.rsqrt(spread + NORM_EPS) * gain


def unit_rows(embed_raw):
    return embed_raw * lax.rsqrt(jnp.sum(embed_raw * embed_raw, axis=-1, keepdims=True) + NORM_EPS)


def dot_f32(a, b):
    return lax.dot_general(a, b, (((1,), (0,)), ((), ())), preferred_element_type=F32)


def dot_nt(a, b):
    return lax.dot_general(a, b, (((1,), (1,)), ((), ())), preferred_element_type=F32)


def dot_tn(a, b):
    return lax.dot_general(a, b, (((0,), (0,)), ((), ())), preferred_element_type=F32)


class Group:
    def __init__(self, arrays, index, rows, cols):
        self.arrays, self.index, self.rows, self.cols = arrays, index, rows, cols


class Weight:
    def __init__(self, k, n, segs=None, sub=1, whole=None):
        self.k, self.n, self.segs, self.sub, self.whole = k, n, segs, sub, whole

    def groups(self):
        seen = []
        for seg in self.segs:
            if seg[0] not in seen:
                seen.append(seg[0])
        return seen

    def operands(self):
        if self.whole is not None:
            return [self.whole]
        return [v for g in self.groups() for v in g.arrays]

    def indices(self):
        return [] if self.whole is not None else [g.index for g in self.groups()]

    def entries(self, tn):
        groups, out = self.groups(), []
        for g, col, width, dst, part in self.segs:
            out += [(groups.index(g), col + t * tn, dst + t * tn, part) for t in range(width // tn)]
        return sorted(out, key=lambda e: (e[2], e[3]))


def start_weight(w, tn, refs, idx, wbuf, sem):
    if w.whole is not None:
        for t in range(w.n // tn):
            cols = pl.ds(t * tn, tn)
            pltpu.make_async_copy(refs[0].at[:, cols], wbuf.at[:, cols], sem.at[t, 0]).start()
        return
    for e, (gi, col, dst, part) in enumerate(w.entries(tn)):
        rows = w.groups()[gi].rows
        for p in range(8):
            at = pl.multiple_of(idx[gi][p] * (rows * w.sub) + part * rows, rows)
            pltpu.make_async_copy(
                refs[8 * gi + p].at[:, pl.ds(w.groups()[gi].cols[p] + col, tn)],
                wbuf.at[pl.ds(at, rows), pl.ds(dst, tn)],
                sem.at[e, p],
            ).start()


def wait_weight(w, tn, refs, idx, wbuf, sem, t):
    cols = pl.ds(pl.multiple_of(t * tn, tn), tn)
    if w.whole is not None:
        pltpu.make_async_copy(refs[0].at[:, pl.ds(0, tn)], wbuf.at[:, cols], sem.at[t, 0]).wait()
        return
    rows = w.groups()[0].rows
    for part in range(w.sub):
        for p in range(8):
            pltpu.make_async_copy(
                refs[p].at[:, pl.ds(0, tn)], wbuf.at[pl.ds((p * w.sub + part) * rows, rows), cols],
                sem.at[t * w.sub + part, p],
            ).wait()


def weight_sems(w, tn):
    tiles = w.n // tn
    return pltpu.SemaphoreType.DMA((tiles, 1) if w.whole is not None else (tiles * w.sub, 8))


HBM = pltpu.MemorySpace.HBM


def hbm_spec():
    return pl.BlockSpec(memory_space=HBM)


def full_spec(shape):
    return pl.BlockSpec(shape, lambda *_: (0,) * len(shape))


def run_kernel(body, name, grid, scalars, ins, weights, outs, scratch, limit, flops):
    scal = list(scalars)
    for w, _ in weights:
        scal += w.indices()
    n_scal, n_user = len(scal), len(scalars)
    operands = [a for a, _ in ins]
    specs = [s for _, s in ins]
    for w, _ in weights:
        ops = w.operands()
        operands += ops
        specs += [hbm_spec()] * len(ops)
    n_in = len(ins)
    scr = list(scratch)
    for w, tn in weights:
        scr += [pltpu.VMEM((w.k, w.n), BF16), weight_sems(w, tn)]

    def kernel(*refs):
        s = refs[:n_scal]
        user_s, s = s[:n_user], s[n_user:]
        pos = n_scal
        in_refs = refs[pos : pos + n_in]
        pos += n_in
        w_refs = []
        for w, _ in weights:
            m = len(w.operands())
            w_refs.append(refs[pos : pos + m])
            pos += m
        out_refs = refs[pos : pos + len(outs)]
        pos += len(outs)
        scr_refs = refs[pos : pos + len(scratch)]
        pos += len(scratch)
        handles = []
        si = 0
        for wi, (w, tn) in enumerate(weights):
            gi = len(w.indices())
            handles.append((w, tn, w_refs[wi], s[si : si + gi], refs[pos], refs[pos + 1]))
            si += gi
            pos += 2
        first = pl.program_id(0) == 0

        @pl.when(first)
        def _():
            for h in handles:
                start_weight(*h)

        def wait(k, t):
            @pl.when(first)
            def _():
                wait_weight(*handles[k], t)

        body(user_s, in_refs, out_refs, scr_refs, [h[4] for h in handles], wait)

    bytes_acc = sum(int(a.size) * a.dtype.itemsize for a in operands) + sum(
        functools.reduce(lambda x, y: x * y, o[0], 1) * jnp.dtype(o[1]).itemsize for o in outs
    )
    return pl.pallas_call(
        kernel,
        grid_spec=pltpu.PrefetchScalarGridSpec(
            num_scalar_prefetch=n_scal,
            grid=grid,
            in_specs=specs,
            out_specs=[o[2] for o in outs],
            scratch_shapes=scr,
        ),
        out_shape=[jax.ShapeDtypeStruct(o[0], o[1]) for o in outs],
        compiler_params=pltpu.CompilerParams(vmem_limit_bytes=limit * MIB),
        cost_estimate=pl.CostEstimate(flops=flops, bytes_accessed=bytes_acc, transcendentals=0),
        name=name,
    )(*scal, *operands)


def rows_spec(length, width):
    return pl.BlockSpec((length, width), lambda i, *_: (i, 0))


def emitted(w, keep=True):
    return [((w.k, w.n), BF16, full_spec((w.k, w.n)))] if keep and w.whole is None else []


def emit_weight(w, outs, at, wbuf, keep=True, step=0):
    if keep and w.whole is None:

        @pl.when(pl.program_id(0) == step)
        def _():
            outs[at][...] = wbuf[...]


def take_weight(w, results, at):
    return w.whole if w.whole is not None else results[at]


def image_qkv(tokens, gains, w, clips, length, tn):
    d, n = w.k, w.n

    def body(_s, ins, outs, _scr, wb, wait):
        h = to_low(normed(ins[0][...].astype(F32), ins[1][0:1, :]))

        def step(t, c):
            wait(0, t)
            at = pl.ds(pl.multiple_of(t * tn, tn), tn)
            outs[0][:, at] = to_low(dot_f32(h, wb[0][:, at]))
            return c

        lax.fori_loop(0, n // tn, step, 0)

    return run_kernel(
        body, "image_qkv", (clips,), [],
        [(tokens, rows_spec(length, d)), (gains, full_spec((3, d)))], [(w, tn)],
        [((clips * length, n), BF16, rows_spec(length, n))], [], 40, 2 * clips * length * d * n,
    )[0]


def audio_in(patches, w_patch, gains, w, clips, length, tn):
    d, n, pk = w.k, w.n, w_patch.shape[0]

    def body(_s, ins, outs, _scr, wb, wait):
        x0 = dot_f32(ins[0][...], ins[1][...])
        outs[0][...] = x0
        h = to_low(normed(x0, ins[2][0:1, :]))
        outs[1][...] = h

        def step(t, c):
            wait(0, t)
            at = pl.ds(pl.multiple_of(t * tn, tn), tn)
            outs[2][:, at] = to_low(dot_f32(h, wb[0][:, at]))
            return c

        lax.fori_loop(0, n // tn, step, 0)

        emit_weight(w, outs, 3, wb[0])

    m = clips * length
    return run_kernel(
        body, "audio_in", (clips,), [],
        [(patches, rows_spec(length, pk)), (w_patch, full_spec((pk, d))), (gains, full_spec((3, d)))], [(w, tn)],
        [((m, d), F32, rows_spec(length, d)), ((m, d), BF16, rows_spec(length, d)),
         ((m, n), BF16, rows_spec(length, n))] + emitted(w),
        [], 40, 2 * m * d * (n + pk),
    )


def attn_forward(qkv, lengths, clips, length, heads, masked):
    d = qkv.shape[1] // 3
    hd = d // heads
    scale = hd ** (-0.5)
    tiles = d // 128

    def body(s_refs, ins, outs, _scr, _wb, _wait):
        qkv_ref, out = ins[0], outs[0]
        lane = lax.broadcasted_iota(jnp.int32, (1, 128), 1)
        if masked:
            keys = lax.broadcasted_iota(jnp.int32, (1, length), 1)
            ok = keys < s_refs[0][pl.program_id(0)]
        acc = {}
        for h in range(heads):
            lo, hi = h * hd, (h + 1) * hd
            t0, t1 = lo // 128, (hi - 1) // 128
            wide = (t1 - t0 + 1) * 128
            at = slice(t0 * 128, t0 * 128 + wide)
            col = lax.broadcasted_iota(jnp.int32, (1, wide), 1) + t0 * 128
            mine = (col >= lo) & (col < hi)
            q = qkv_ref[:, at]
            q = jnp.where(mine, q, jnp.zeros_like(q))
            k = qkv_ref[:, d + t0 * 128 : d + t0 * 128 + wide]
            v = qkv_ref[:, 2 * d + t0 * 128 : 2 * d + t0 * 128 + wide]
            sc = dot_nt(q, k) * scale
            if masked:
                sc = jnp.where(ok, sc, -1e30)
            e = jnp.exp(sc - jnp.max(sc, axis=-1, keepdims=True))
            p = to_low(e * (1.0 / jnp.sum(e, axis=-1, keepdims=True)))
            o = dot_f32(p, v)
            for t in range(t0, t1 + 1):
                part = o[:, (t - t0) * 128 : (t - t0 + 1) * 128]
                full = lane + t * 128
                sel = (full >= lo) & (full < hi)
                acc[t] = jnp.where(sel, part, acc[t]) if t in acc else part
                if min((t + 1) * 128, d) <= hi:
                    out[:, t * 128 : (t + 1) * 128] = to_low(acc.pop(t))

    m = clips * length
    return run_kernel(
        body, "attn_forward", (clips,), [lengths], [(qkv, rows_spec(length, 3 * d))], [],
        [((m, d), BF16, rows_spec(length, d))], [], 32, 4 * m * length * 256 * heads,
    )[0]


def out_norm(mixed, resid, gains, w, clips, length, keep):
    d = w.n

    def body(_s, ins, outs, _scr, wb, wait):
        wait(0, 0)
        x1 = ins[1][...].astype(F32) + dot_f32(ins[0][...], wb[0][...])
        outs[0][...] = x1
        outs[1][...] = to_low(normed(x1, ins[2][1:2, :]))
        emit_weight(w, outs, 2, wb[0], keep)

    m = clips * length
    outs = [((m, d), F32, rows_spec(length, d)), ((m, d), BF16, rows_spec(length, d))] + emitted(w, keep)
    return run_kernel(
        body, "out_norm", (clips,), [],
        [(mixed, rows_spec(length, d)), (resid, rows_spec(length, d)), (gains, full_spec((3, d)))], [(w, d)],
        outs, [], 32, 2 * m * d * d,
    )


def gelu_parts(z):
    zz = z * z
    t = jnp.tanh(GELU_C * z * (1.0 + GELU_A * zz))
    half = 0.5 * (1.0 + t)
    return z * half, half, t, zz


def up_gelu(h_two, w, clips, length, tn, keep):
    d, n = w.k, w.n

    def body(_s, ins, outs, _scr, wb, wait):
        h = ins[0][...]

        def step(t, c):
            wait(0, t)
            at = pl.ds(pl.multiple_of(t * tn, tn), tn)
            z = dot_f32(h, wb[0][:, at])
            u, half, tz, zz = gelu_parts(z)
            outs[0][:, at] = to_low(u)
            if keep:
                slope = half + z * (0.5 * GELU_C) * (1.0 - tz * tz) * (1.0 + (3.0 * GELU_A) * zz)
                outs[1][:, at] = to_low(slope)
            return c

        lax.fori_loop(0, n // tn, step, 0)
        emit_weight(w, outs, 2, wb[0], keep)

    m = clips * length
    outs = [((m, n), BF16, rows_spec(length, n))]
    if keep:
        outs += [((m, n), BF16, rows_spec(length, n))] + emitted(w)
    return run_kernel(
        body, "up_gelu", (clips,), [], [(h_two, rows_spec(length, d))], [(w, tn)], outs, [], 44, 2 * m * d * n,
    )


def down_left(hidden, resid, w, clips, length, kt):
    k, n = w.k, w.n

    def body(_s, ins, outs, _scr, wb, wait):
        wait(0, 0)
        outs[0][...] = ins[1][...]

        def step(t, c):
            at = pl.ds(pl.multiple_of(t * kt, kt), kt)
            outs[0][...] += dot_f32(ins[0][:, at], wb[0][at, :])
            return c

        lax.fori_loop(0, k // kt, step, 0)

    m = clips * length
    return run_kernel(
        body, "down_left", (clips,), [], [(hidden, rows_spec(length, k)), (resid, rows_spec(length, n))],
        [(w, n)], [((m, n), F32, rows_spec(length, n))], [], 44, 2 * m * n * k,
    )[0]


def down_embed(hidden, resid, left, gains, lengths, w, w_proj, clips, length, kt, keep):
    d, k, pj, n = resid.shape[1], w.k, w_proj.n, w.n
    have = d - n

    def body(s_refs, ins, outs, scr, wb, wait):
        g = pl.program_id(0)
        wait(0, 0)
        if have:
            scr[0][:, :have] = ins[3][...]
        scr[0][:, have:] = ins[1][:, have:]

        def step(t, c):
            at = pl.ds(pl.multiple_of(t * kt, kt), kt)
            scr[0][:, have:] += dot_f32(ins[0][:, at], wb[0][at, :])
            return c

        lax.fori_loop(0, k // kt, step, 0)
        x2 = scr[0][...]
        size = s_refs[0][g]
        row = lax.broadcasted_iota(jnp.int32, (length, 1), 0)
        weight = jnp.where(row < size, 1.0 / size.astype(F32), 0.0)
        pooled = jnp.sum(normed(x2, ins[2][2:3, :]) * weight, axis=0, keepdims=True)
        scr[1][pl.ds(g, 1), :] = pooled
        if keep:
            outs[3][...] = x2
            emit_weight(w, outs, 4, wb[0])
            emit_weight(w_proj, outs, 5, wb[1], True, clips - 1)
        wait(1, 0)

        @pl.when(g == clips - 1)
        def _():
            pool_all = scr[1][...]
            raw = dot_f32(to_low(pool_all), wb[1][...])
            outs[0][...] = to_low(unit_rows(raw))
            outs[1][...] = raw
            outs[2][...] = pool_all

    m = clips * length
    outs = [((clips, pj), BF16, full_spec((clips, pj))), ((clips, pj), F32, full_spec((clips, pj))),
            ((clips, d), F32, full_spec((clips, d)))]
    if keep:
        outs += [((m, d), F32, rows_spec(length, d))] + emitted(w) + emitted(w_proj)
    ins = [(hidden, rows_spec(length, k)), (resid, rows_spec(length, d)), (gains, full_spec((3, d)))]
    if have:
        ins.append((left, rows_spec(length, have)))
    return run_kernel(
        body, "down_embed", (clips,), [lengths], ins, [(w, n), (w_proj, pj)], outs,
        [pltpu.VMEM((length, d), F32), pltpu.VMEM((clips, d), F32)], 44, 2 * m * n * k,
    )


def attn_backward(qkv, d_mixed, lengths, clips, length, heads):
    d = qkv.shape[1] // 3
    hd = d // heads
    scale = hd ** (-0.5)
    per = 128 // hd

    def body(s_refs, ins, outs, _scr, _wb, _wait):
        qkv_ref, do_ref, out = ins[0], ins[1], outs[0]
        lane = lax.broadcasted_iota(jnp.int32, (1, 128), 1)
        ok = lax.broadcasted_iota(jnp.int32, (1, length), 1) < s_refs[0][pl.program_id(0)]
        for t in range(d // 128):
            at = slice(t * 128, (t + 1) * 128)
            q, do = qkv_ref[:, at], do_ref[:, at]
            k = qkv_ref[:, d + t * 128 : d + (t + 1) * 128]
            v = qkv_ref[:, 2 * d + t * 128 : 2 * d + (t + 1) * 128]
            dq = dk = dv = None
            for h in range(per):
                mine = (lane >= h * hd) & (lane < (h + 1) * hd)
                qm = jnp.where(mine, q, jnp.zeros_like(q))
                dom = jnp.where(mine, do, jnp.zeros_like(do))
                sc = jnp.where(ok, dot_nt(qm, k) * scale, -1e30)
                e = jnp.exp(sc - jnp.max(sc, axis=-1, keepdims=True))
                p = e * (1.0 / jnp.sum(e, axis=-1, keepdims=True))
                dp = dot_nt(dom, v)
                ds = to_low(p * (dp - jnp.sum(p * dp, axis=-1, keepdims=True)))
                dv_h = dot_tn(to_low(p), do)
                dq_h = dot_f32(ds, k)
                dk_h = dot_tn(ds, q)
                dq = dq_h if dq is None else jnp.where(mine, dq_h, dq)
                dk = dk_h if dk is None else jnp.where(mine, dk_h, dk)
                dv = dv_h if dv is None else jnp.where(mine, dv_h, dv)
            out[:, at] = to_low(dq * scale)
            out[:, d + t * 128 : d + (t + 1) * 128] = to_low(dk * scale)
            out[:, 2 * d + t * 128 : 2 * d + (t + 1) * 128] = to_low(dv)

    m = clips * length
    return run_kernel(
        body, "attn_backward", (clips,), [lengths],
        [(qkv, rows_spec(length, 3 * d)), (d_mixed, rows_spec(length, d))], [],
        [((m, 3 * d), BF16, rows_spec(length, 3 * d))], [], 32, 10 * m * length * 256 * heads,
    )[0]


AXES = ("dp", "rep")


def joint_perm(reps, fn):
    out = []
    for dp in range(8):
        for z in range(reps):
            dst = fn(dp, z)
            if dst is not None:
                out.append((dp * reps + z, dst[0] * reps + dst[1]))
    return out


def send(value, reps, fn):
    return lax.ppermute(value, AXES, joint_perm(reps, fn))


class Ring:
    def __init__(self, packed, col, width, reps):
        self.own, self.col, self.width, self.reps = packed, col, width, reps
        self.mine = packed[:, col : col + width]

    def first(self):
        self.near = send(self.mine, self.reps, lambda dp, z: (dp ^ (2 if z % 2 == 0 else 4), z))

    def second(self):
        self.diag = send(self.near, self.reps, lambda dp, z: (dp ^ (4 if z % 2 == 0 else 2), z))
        self.other = send(self.near, self.reps, lambda dp, z: (dp, z ^ 1))

    def twin(self, *names):
        for name in names:
            setattr(self, name + "_twin", send(getattr(self, name), self.reps, lambda dp, z: (dp ^ 1, z)))

    def group(self, own_twin):
        odd = lax.axis_index("rep") % 2 == 1
        x, y = jnp.int32(2), jnp.int32(4)
        flip = jnp.stack([jnp.int32(0), jnp.where(odd, y, x), jnp.int32(6), jnp.where(odd, x, y)])
        base = jnp.bitwise_xor(flip, lax.axis_index("dp").astype(jnp.int32))
        arrays = [self.own, self.near, self.diag, self.other, own_twin, self.near_twin, self.diag_twin, self.other_twin]
        index = jnp.concatenate([base, jnp.bitwise_xor(base, 1)])
        return Group(arrays, index, self.own.shape[0], (self.col, 0, 0, 0) * 2)


def fence(held, values):
    flat = [(r, n) for r, names in held for n in names.split()]
    out = lax.optimization_barrier(tuple(getattr(r, n) for r, n in flat) + tuple(values))
    for (r, n), v in zip(flat, out):
        setattr(r, n, v)
    return out[len(flat) :]


def take(v, i, axis):
    return lax.dynamic_index_in_dim(v, i, axis, keepdims=False)


def in_width(v, width):
    n = v.shape[-1]
    blocks = [v[..., i * width : (i + 1) * width] for i in range(n // width)]
    rest = n % width
    if rest:
        last, k, rows = v[..., n - rest :], width // rest, v.shape[-2]
        blocks.append(jnp.concatenate(
            [last[..., i * (rows // k) : (i + 1) * (rows // k), :] for i in range(k)], axis=-1))
    return jnp.concatenate(blocks, axis=-2)


def from_width(v, rows, n):
    width = v.shape[-1]
    full = n // width
    blocks = [v[i * rows : (i + 1) * rows] for i in range(full)]
    rest = n % width
    if rest:
        last, k = v[full * rows :], width // rest
        blocks.append(jnp.concatenate([last[:, i * rest : (i + 1) * rest] for i in range(k)], axis=0))
    return jnp.concatenate(blocks, axis=1)


def reduce_group(grads, kind, reps, width):
    me, rep = lax.axis_index("dp"), lax.axis_index("rep")
    y, x, c = me // 4, (me // 2) % 2, me % 2
    split = [v.reshape(2, 2, 2, v.shape[0] // 8, v.shape[1]) for v in grads]
    pick = lambda i: jnp.concatenate([in_width(take(v, i, 2), width) for v in split], axis=-2)
    s = pick(c) + send(to_low(pick(1 - c)), reps, lambda dp, z: (dp ^ 1, z)).astype(F32)
    for step in ((0, 1) if kind == 0 else (1, 0)):
        bit, at, axis = ((2, x, s.ndim - 3), (4, y, 0))[step]
        got = send(to_low(take(s, 1 - at, axis)), reps, lambda dp, z: (dp ^ bit, z))
        s = take(s, at, axis) + got.astype(F32)
    low = to_low(s)
    got = send(low, reps, lambda dp, z: {0: (dp, 1), 3: (dp, 2)}.get(z))
    low = to_low(low.astype(F32) + got.astype(F32))
    got = send(low, reps, lambda dp, z: {1: (dp, 2), 2: (dp, 1)}.get(z))
    low = to_low(low.astype(F32) + got.astype(F32))
    got = send(low, reps, lambda dp, z: {1: (dp, 0), 2: (dp, 3)}.get(z))
    total = jnp.where((rep == 1) | (rep == 2), low, got).astype(F32)
    out, at = [], 0
    for v in split:
        rows, n = v.shape[-2:]
        size = rows * n // width
        out.append(from_width(total[at : at + size], rows, n))
        at += size
    return out


def adam_step(weight, gradient, moment_one, moment_two, step_rate, decay):
    first_new = BETA_ONE * moment_one + (1.0 - BETA_ONE) * gradient
    second_new = BETA_TWO * moment_two + (1.0 - BETA_TWO) * gradient * gradient
    fixed_one = first_new / (1.0 - BETA_ONE**STEP)
    fixed_two = second_new / (1.0 - BETA_TWO**STEP)
    update = fixed_one / (jnp.sqrt(fixed_two) + ADAM_EPS) + decay * weight
    return (weight - step_rate * update, first_new, second_new)


def as_columns(v, rows):
    return jnp.concatenate([v[i * rows : (i + 1) * rows] for i in range(v.shape[0] // rows)], axis=1)


def local(dp_size, rep_size, *args):
    (audio_patches, clip_lengths, video_ids, image_tokens, i_qkv, i_out, i_up, i_down, i_proj, i_gains) = args[:10]
    masters, firsts_in, seconds_in = args[10:17], args[17:24], args[24:31]
    a_patch, a_qkv, a_out, a_up, a_down, a_proj, a_gains = (to_low(w) for w in masters)
    fast = dp_size == 8 and rep_size == 4
    clip_dev = audio_patches.shape[1]
    clips = MICRO * clip_dev
    d_i, d_a, ff_a, pj = i_out.shape[1], a_out.shape[1], a_up.shape[1], a_proj.shape[1]
    ff_i = i_up.shape[1]

    rp = a_patch.shape[0]
    small = jnp.concatenate(
        [a_patch, jnp.pad(a_gains.reshape(1, -1), ((0, 0), (0, d_a - a_gains.size))),
         jnp.pad(i_gains.reshape(1, -1), ((0, 0), (0, d_a - i_gains.size)))], axis=0)
    small = lax.all_gather(small, "dp", axis=0)
    img_sizes = jnp.full((clips,), IMG_LEN, jnp.int32)
    tokens = image_tokens.reshape(clips * IMG_LEN, d_i)
    sizes = clip_lengths.reshape(clips)
    patches = jnp.pad(audio_patches.reshape(clips, LEN, -1), ((0, 0), (0, PAD_LEN - LEN), (0, 0)))
    patches = patches.reshape(clips * PAD_LEN, -1)
    half, sub_i, sub_a = ff_i // 2, ff_i // d_i, ff_a // d_a
    dl = d_i * 3 // 5
    fr = d_a * 8 // 3
    if fast:
        down_i, down_a = as_columns(i_down, i_qkv.shape[0]), as_columns(a_down, a_qkv.shape[0])
        left = [down_i[:, j * d_i : j * d_i + dl] for j in range(sub_i)]
        right = [down_i[:, j * d_i + dl : (j + 1) * d_i] for j in range(sub_i)]
        own_a = jnp.concatenate([a_qkv, a_out, a_up, down_a, a_proj], axis=1)
        own_i = jnp.concatenate([i_qkv, i_out, i_up, i_proj] + left + right, axis=1)
        small, own_a, own_i = lax.optimization_barrier((small, own_a, own_i))
        cut_a = 4 * d_a + fr
        ca = Ring(own_a, 0, cut_a, rep_size), Ring(own_a, cut_a, own_a.shape[1] - cut_a, rep_size)
        widths, at, ci = [3 * d_i, d_i + half, half + pj, sub_i * dl, sub_i * (d_i - dl)], 0, []
        for wd in widths:
            ci.append(Ring(own_i, at, wd, rep_size))
            at += wd
        swap = lambda v: send(v, rep_size, lambda dp, z: (dp ^ 1, z))
        twin_a, twin_i = swap(own_a), swap(own_i)

        ca[0].first()
        fence([(ca[0], "near"), (ca[1], "mine")], ())
        ca[0].second()
        ca[0].twin("near")
        ca[1].first()
        patches, twin_a = fence([(ca[0], "diag other near_twin"), (ca[1], "near"), (ci[0], "mine")], (patches, twin_a))
        ca[0].twin("diag", "other")
        ca[1].second()
        ca[1].twin("near")
        ci[0].first()
        ga0 = ca[0].group(twin_a)
        wa_qkv = Weight(d_a, 3 * d_a, [(ga0, 0, 3 * d_a, 0, 0)])
        wa_out = Weight(d_a, d_a, [(ga0, 3 * d_a, d_a, 0, 0)])
    else:
        whole = lambda v: lax.all_gather(v, "dp", axis=0, tiled=True)
        make = lambda v: Weight(v.shape[0] * dp_size, v.shape[1], whole=whole(v))
        cut = lambda v: Weight(v.shape[0], v.shape[1], whole=v)
        wi_qkv, wi_out, wi_up, wi_proj = (make(v) for v in (i_qkv, i_out, i_up, i_proj))
        wi_left, wi_right = cut(whole(i_down)[:, :dl]), cut(whole(i_down)[:, dl:])
        wa_qkv, wa_out, wa_up, wa_down, wa_proj = (make(v) for v in (a_qkv, a_out, a_up, a_down, a_proj))

    w_patch = small[:, :rp].reshape(rp * dp_size, d_a)
    unpack = lambda v, g: v[:, : g.size].reshape(dp_size, 3, -1).transpose(1, 0, 2).reshape(3, -1).astype(F32)
    gains_a, gains_i = unpack(small[:, rp], a_gains), unpack(small[:, rp + 1], i_gains)

    got = audio_in(patches, w_patch, gains_a, wa_qkv, clips, PAD_LEN, d_a)
    resid_in, h_one, qkv = got[:3]
    full_qkv = take_weight(wa_qkv, got, 3)
    mixed = attn_forward(qkv, sizes, clips, PAD_LEN, HEADS_A, True)
    got = out_norm(mixed, resid_in, gains_a, wa_out, clips, PAD_LEN, True)
    resid_mid, h_two = got[:2]
    full_out = take_weight(wa_out, got, 2)

    if fast:
        (h_two,) = fence([(ca[1], "diag other near_twin"), (ci[0], "near"), (ci[1], "mine")], (h_two,))
        ca[1].twin("diag", "other")
        ci[0].second()
        ci[0].twin("near")
        ci[1].first()
        ga1 = ca[1].group(twin_a)
        wa_up = Weight(d_a, ff_a, [(ga0, 4 * d_a, fr, 0, 0), (ga1, 0, ff_a - fr, fr, 0)])
        wa_down = Weight(ff_a, d_a, [(ga1, ff_a - fr + j * d_a, d_a, 0, j) for j in range(sub_a)], sub=sub_a)
        wa_proj = Weight(d_a, pj, [(ga1, 2 * ff_a - fr, pj, 0, 0)])
    got = up_gelu(h_two, wa_up, clips, PAD_LEN, 1024, True)
    hidden, slope = got[:2]
    full_up = take_weight(wa_up, got, 2)

    if fast:
        hidden, tokens, twin_i = fence(
            [(ci[0], "diag other near_twin"), (ci[1], "near"), (ci[2], "mine")], (hidden, tokens, twin_i))
        ci[0].twin("diag", "other")
        ci[1].second()
        ci[1].twin("near")
        ci[2].first()
        gi = [ci[0].group(twin_i)]
        wi_qkv = Weight(d_i, 3 * d_i, [(gi[0], 0, 3 * d_i, 0, 0)])
    qkv_i = image_qkv(tokens, gains_i, wi_qkv, clips, IMG_LEN, d_i)
    mixed_i = attn_forward(qkv_i, img_sizes, clips, IMG_LEN, HEADS_I, False)

    if fast:
        mixed_i, hidden = fence(
            [(ci[1], "diag other near_twin"), (ci[2], "near"), (ci[3], "mine")], (mixed_i, hidden))
        ci[1].twin("diag", "other")
        ci[2].second()
        ci[2].twin("near")
        ci[3].first()
        gi.append(ci[1].group(twin_i))
        wi_out = Weight(d_i, d_i, [(gi[1], 0, d_i, 0, 0)])
    got = down_embed(hidden, resid_mid, None, gains_a, sizes, wa_down, wa_proj, clips, PAD_LEN, d_a, True)
    aud_emb, embed_raw, pooled, resid_out = got[:4]
    full_down, full_proj = take_weight(wa_down, got, 4), take_weight(wa_proj, got, 5)
    mid_i, h_two_i = out_norm(mixed_i, tokens, gains_i, wi_out, clips, IMG_LEN, False)

    if fast:
        h_two_i, aud_emb = fence(
            [(ci[2], "diag other near_twin"), (ci[3], "near"), (ci[4], "mine")], (h_two_i, aud_emb))
        ci[2].twin("diag", "other")
        ci[3].second()
        ci[3].twin("near")
        ci[4].first()
        gi.append(ci[2].group(twin_i))
        wi_up = Weight(d_i, ff_i, [(gi[1], d_i, half, 0, 0), (gi[2], 0, half, half, 0)])
        wi_proj = Weight(d_i, pj, [(gi[2], half, pj, 0, 0)])
    hidden_i = up_gelu(h_two_i, wi_up, clips, IMG_LEN, d_i, False)[0]

    if fast:
        (hidden_i,) = fence([(ci[3], "diag other near_twin"), (ci[4], "near")], (hidden_i,))
        ci[3].twin("diag", "other")
        ci[4].second()
        ci[4].twin("near")
        gi.append(ci[3].group(twin_i))
        wi_left = Weight(ff_i, dl, [(gi[3], j * dl, dl, 0, j) for j in range(sub_i)], sub=sub_i)
    left_i = down_left(hidden_i, mid_i, wi_left, clips, IMG_LEN, d_i)

    if fast:
        (left_i,) = fence([(ci[4], "diag other near_twin")], (left_i,))
        ci[4].twin("diag", "other")
        gi.append(ci[4].group(twin_i))
        dr = d_i - dl
        wi_right = Weight(ff_i, dr, [(gi[4], j * dr, dr, 0, j) for j in range(sub_i)], sub=sub_i)
    img_emb = down_embed(hidden_i, mid_i, left_i, gains_i, img_sizes, wi_right, wi_proj, clips, IMG_LEN, d_i, False)[0]

    ids_low = jnp.broadcast_to(to_low(video_ids.reshape(clips, 1)), (clips, 128))
    joined = jnp.concatenate([aud_emb, img_emb, ids_low], axis=1).reshape(MICRO, clip_dev, 2 * pj + 128)
    joined = lax.all_gather(lax.all_gather(joined, "rep", axis=1, tiled=True), "dp", axis=1, tiled=True)
    aud_all, img_all, all_ids = joined[:, :, :pj], joined[:, :, pj : 2 * pj], joined[:, :, 2 * pj]
    rows = all_ids.shape[1]
    same = jnp.arange(rows)[:, None] == jnp.arange(rows)[None, :]
    allowed = jnp.logical_or(all_ids[:, :, None] != all_ids[:, None, :], same[None])
    loss_scale = rows / jnp.sum(allowed.astype(F32))
    logits = jnp.einsum("mid,mjd->mij", aud_all, img_all, preferred_element_type=F32) * LOGIT_SCALE
    masked = jnp.where(allowed, logits, -1e30)
    matched = jnp.sum(jnp.where(same, logits, 0.0), axis=2)
    row_lse = jax.nn.logsumexp(masked, axis=2)
    col_lse = jax.nn.logsumexp(masked, axis=1)
    loss = (jnp.sum(row_lse - matched) + jnp.sum(col_lse - matched)) * loss_scale
    start_row = lax.axis_index(AXES) * clip_dev
    own = lambda v: lax.dynamic_slice_in_dim(v, start_row, clip_dev, 1)
    own_masked = own(masked)
    d_logits = (
        jnp.exp(own_masked - own(row_lse)[:, :, None])
        + jnp.exp(own_masked - col_lse[:, None, :])
        - 2.0 * lax.dynamic_slice_in_dim(same.astype(F32), start_row, clip_dev, 0)[None]
    ) * (loss_scale * LOGIT_SCALE)
    d_embed = jnp.einsum("mij,mjd->mid", d_logits, img_all.astype(F32), precision=HIGHEST).reshape(clips, pj)

    d_raw = to_low(jax.vjp(unit_rows, embed_raw)[1](d_embed)[0])
    g_proj = dot_tn(to_low(pooled), d_raw)
    d_pooled = dot_nt(d_raw, full_proj)
    valid = jnp.arange(PAD_LEN)[None, :] < sizes[:, None]
    pool_weight = valid.astype(F32) / sizes[:, None].astype(F32)
    d_normed = (d_pooled[:, None, :] * pool_weight[:, :, None]).reshape(clips * PAD_LEN, d_a)
    d_out, g_three = jax.vjp(normed, resid_out, gains_a[2])[1](d_normed)
    d_low = to_low(d_out)
    g_down = dot_tn(hidden, d_low)
    d_pre = to_low(dot_nt(d_low, full_down) * slope.astype(F32))
    g_up = dot_tn(h_two, d_pre)
    d_ln_two, g_two = jax.vjp(normed, resid_mid, gains_a[1])[1](dot_nt(d_pre, full_up))
    d_mid = d_out + d_ln_two
    d_mid_low = to_low(d_mid)
    g_out = dot_tn(mixed, d_mid_low)
    d_mixed = to_low(dot_nt(d_mid_low, full_out))
    d_qkv = attn_backward(qkv, d_mixed, sizes, clips, PAD_LEN, HEADS_A)
    g_qkv = dot_tn(h_one, d_qkv)
    d_ln_one, g_one = jax.vjp(normed, resid_in, gains_a[0])[1](dot_nt(d_qkv, full_qkv))
    d_in = to_low(d_mid + d_ln_one)
    g_patch = dot_tn(patches, d_in)
    g_gains = jnp.stack([g_one, g_two, g_three])

    if fast:
        share = d_a // dp_size
        gain_rows = jnp.pad(g_gains.reshape(3, dp_size, share).transpose(1, 0, 2).reshape(dp_size, 1, 3 * share),
                            ((0, 0), (0, 7), (0, d_a - 3 * share))).reshape(dp_size * 8, d_a)
        r_down, r_proj = reduce_group([g_down, g_proj], 0, rep_size, d_a)
        (r_up,) = reduce_group([g_up], 1, rep_size, d_a)
        r_qkv, r_out, r_patch, r_gain = reduce_group([g_qkv, g_out, g_patch, gain_rows], 0, rep_size, d_a)
        summed = [r_patch, r_qkv, r_out, r_up, r_down, r_proj, r_gain[0, : 3 * share].reshape(3, share)]
    else:
        summed = [lax.psum(lax.psum_scatter(v, "dp", scatter_dimension=0, tiled=True), "rep")
                  for v in (g_patch, g_qkv, g_out, g_up, g_down, g_proj)]
        summed.append(lax.psum(lax.psum_scatter(g_gains, "dp", scatter_dimension=1, tiled=True), "rep"))
    local_squares = sum(jnp.sum(v * v) for v in summed)
    grad_norm = jnp.sqrt(lax.psum(local_squares, "dp"))
    factor = jnp.minimum(1.0, CLIP_NORM / grad_norm)
    results = []
    for index in range(7):
        step_rate = RATE_GAIN if index == 6 else RATE_MATRIX
        decay = 0.0 if index == 6 else WEIGHT_DECAY
        results.append(
            adam_step(masters[index], summed[index] * factor, firsts_in[index], seconds_in[index], step_rate, decay)
        )
    return (loss, grad_norm, *(r[0] for r in results), *(r[1] for r in results), *(r[2] for r in results))


def solution(mesh):
    batch4 = P(None, AXES, None, None)
    batch2 = P(None, AXES)
    split = P("dp", None)
    gain = P(None, "dp")
    weights = (split,) * 6 + (gain,)
    placed = (batch4, batch2, batch2, batch4) + (split,) * 5 + (gain,) + weights * 3
    return jax.shard_map(
        functools.partial(local, mesh.shape["dp"], mesh.shape["rep"]),
        mesh=mesh,
        in_specs=placed,
        out_specs=(P(), P()) + weights * 3,
        check_vma=False,
    )
```

```python
import functools

import jax
import jax.numpy as jnp
from jax import lax
from jax.experimental import pallas as pl
from jax.experimental.pallas import tpu as pltpu
from jax.sharding import PartitionSpec as P

HEADS_A = 12
HEADS_I = 16
LEN = 228
IMG_LEN = 256
MICRO = 2
STEP = 7

HIGHEST = lax.Precision.HIGHEST
F32 = jnp.float32
BF16 = jnp.bfloat16
NORM_EPS = 1e-06
LOGIT_SCALE = 50.0
CLIP_NORM = 0.01
BETA_ONE = 0.9
BETA_TWO = 0.999
ADAM_EPS = 1e-08
WEIGHT_DECAY = 0.1
RATE_MATRIX = 0.05
RATE_GAIN = 0.3
PAD_LEN = 240
GELU_C = 0.7978845608028654
GELU_A = 0.044715
VMEM_GRANT = 60 << 20


def to_low(v):
    return v.astype(BF16)


def normed(resid, gain):
    center = resid - jnp.mean(resid, axis=-1, keepdims=True)
    spread = jnp.mean(center * center, axis=-1, keepdims=True)
    return center * lax.rsqrt(spread + NORM_EPS) * gain


def unit_rows(embed_raw):
    return embed_raw * lax.rsqrt(jnp.sum(embed_raw * embed_raw, axis=-1, keepdims=True) + NORM_EPS)


def dot_f32(a, b):
    return lax.dot_general(a, b, (((1,), (0,)), ((), ())), preferred_element_type=F32)


def dot_nt(a, b):
    return lax.dot_general(a, b, (((1,), (1,)), ((), ())), preferred_element_type=F32)


def dot_tn(a, b):
    return lax.dot_general(a, b, (((0,), (0,)), ((), ())), preferred_element_type=F32)


class Group:
    def __init__(self, arrays, index, rows, cols):
        self.arrays, self.index, self.rows, self.cols = arrays, index, rows, cols


class Weight:
    def __init__(self, k, n, segs=None, sub=1, whole=None):
        self.k, self.n, self.segs, self.sub, self.whole = k, n, segs, sub, whole

    def groups(self):
        seen = []
        for seg in self.segs:
            if seg[0] not in seen:
                seen.append(seg[0])
        return seen

    def operands(self):
        if self.whole is not None:
            return [self.whole]
        return [v for g in self.groups() for v in g.arrays]

    def indices(self):
        return [] if self.whole is not None else [g.index for g in self.groups()]

    def entries(self, tn):
        groups, out = self.groups(), []
        for g, col, width, dst, part in self.segs:
            assert width % tn == 0
            out += [(groups.index(g), col + t * tn, dst + t * tn, part) for t in range(width // tn)]
        return sorted(out, key=lambda e: (e[2], e[3]))


def start_weight(w, tn, refs, idx, wbuf, sem):
    if w.whole is not None:
        for t in range(w.n // tn):
            cols = pl.ds(t * tn, tn)
            pltpu.make_async_copy(refs[0].at[:, cols], wbuf.at[:, cols], sem.at[t, 0]).start()
        return
    for e, (gi, col, dst, part) in enumerate(w.entries(tn)):
        rows = w.groups()[gi].rows
        for p in range(8):
            at = pl.multiple_of(idx[gi][p] * (rows * w.sub) + part * rows, rows)
            pltpu.make_async_copy(
                refs[8 * gi + p].at[:, pl.ds(w.groups()[gi].cols[p] + col, tn)],
                wbuf.at[pl.ds(at, rows), pl.ds(dst, tn)],
                sem.at[e, p],
            ).start()


def wait_weight(w, tn, refs, idx, wbuf, sem, t):
    cols = pl.ds(pl.multiple_of(t * tn, tn), tn)
    if w.whole is not None:
        pltpu.make_async_copy(refs[0].at[:, pl.ds(0, tn)], wbuf.at[:, cols], sem.at[t, 0]).wait()
        return
    rows = w.groups()[0].rows
    for part in range(w.sub):
        for p in range(8):
            pltpu.make_async_copy(
                refs[p].at[:, pl.ds(0, tn)], wbuf.at[pl.ds((p * w.sub + part) * rows, rows), cols],
                sem.at[t * w.sub + part, p],
            ).wait()


def weight_sems(w, tn):
    tiles = w.n // tn
    return pltpu.SemaphoreType.DMA((tiles, 1) if w.whole is not None else (tiles * w.sub, 8))


HBM = pltpu.MemorySpace.HBM


def hbm_spec():
    return pl.BlockSpec(memory_space=HBM)


def full_spec(shape):
    return pl.BlockSpec(shape, lambda *_: (0,) * len(shape))


def run_kernel(body, name, grid, scalars, ins, weights, outs, scratch, flops, alias=None):
    scal = list(scalars)
    for w, _ in weights:
        scal += w.indices()
    n_scal, n_user = len(scal), len(scalars)
    operands = [a for a, _ in ins]
    specs = [s for _, s in ins]
    for w, _ in weights:
        ops = w.operands()
        operands += ops
        specs += [hbm_spec()] * len(ops)
    n_in = len(ins)
    scr = list(scratch)
    for w, tn in weights:
        scr += [pltpu.VMEM((w.k, w.n), BF16), weight_sems(w, tn)]

    def kernel(*refs):
        s = refs[:n_scal]
        user_s, s = s[:n_user], s[n_user:]
        pos = n_scal
        in_refs = refs[pos : pos + n_in]
        pos += n_in
        w_refs = []
        for w, _ in weights:
            m = len(w.operands())
            w_refs.append(refs[pos : pos + m])
            pos += m
        out_refs = refs[pos : pos + len(outs)]
        pos += len(outs)
        scr_refs = refs[pos : pos + len(scratch)]
        pos += len(scratch)
        handles = []
        si = 0
        for wi, (w, tn) in enumerate(weights):
            gi = len(w.indices())
            handles.append((w, tn, w_refs[wi], s[si : si + gi], refs[pos], refs[pos + 1]))
            si += gi
            pos += 2
        first = pl.program_id(0) == 0

        @pl.when(first)
        def _():
            for h in handles:
                start_weight(*h)

        def wait(k, t):
            @pl.when(first)
            def _():
                wait_weight(*handles[k], t)

        body(user_s, in_refs, out_refs, scr_refs, [h[4] for h in handles], wait)

    bytes_acc = sum(int(a.size) * a.dtype.itemsize for a in operands) + sum(
        functools.reduce(lambda x, y: x * y, o[0], 1) * jnp.dtype(o[1]).itemsize for o in outs
    )
    return pl.pallas_call(
        kernel,
        grid_spec=pltpu.PrefetchScalarGridSpec(
            num_scalar_prefetch=n_scal,
            grid=grid,
            in_specs=specs,
            out_specs=[o[2] for o in outs],
            scratch_shapes=scr,
        ),
        out_shape=[jax.ShapeDtypeStruct(o[0], o[1]) for o in outs],
        input_output_aliases={} if alias is None else {n_scal + alias: 0},
        compiler_params=pltpu.CompilerParams(vmem_limit_bytes=VMEM_GRANT),
        cost_estimate=pl.CostEstimate(flops=flops, bytes_accessed=bytes_acc, transcendentals=0),
        name=name,
    )(*scal, *operands)


def rows_spec(length, width):
    return pl.BlockSpec((length, width), lambda i, *_: (i, 0))


def image_qkv(tokens, gains, w, clips, length, tn):
    d, n = w.k, w.n

    def body(_s, ins, outs, _scr, wb, wait):
        h = to_low(normed(ins[0][...].astype(F32), ins[1][0:1, :]))

        def step(t, c):
            wait(0, t)
            at = pl.ds(pl.multiple_of(t * tn, tn), tn)
            outs[0][:, at] = to_low(dot_f32(h, wb[0][:, at]))
            return c

        lax.fori_loop(0, n // tn, step, 0)

    return run_kernel(
        body, "image_qkv", (clips,), [],
        [(tokens, rows_spec(length, d)), (gains, full_spec((3, d)))], [(w, tn)],
        [((clips * length, n), BF16, rows_spec(length, n))], [], 2 * clips * length * d * n,
    )[0]


def audio_in(patches, w_patch, gains, w, clips, length, tn):
    d, n, pk = w.k, w.n, w_patch.shape[0]

    def body(_s, ins, outs, _scr, wb, wait):
        x0 = dot_f32(ins[0][...], ins[1][...])
        outs[0][...] = x0
        h = to_low(normed(x0, ins[2][0:1, :]))
        outs[1][...] = h

        def step(t, c):
            wait(0, t)
            at = pl.ds(pl.multiple_of(t * tn, tn), tn)
            outs[2][:, at] = to_low(dot_f32(h, wb[0][:, at]))
            return c

        lax.fori_loop(0, n // tn, step, 0)

    m = clips * length
    return run_kernel(
        body, "audio_in", (clips,), [],
        [(patches, rows_spec(length, pk)), (w_patch, full_spec((pk, d))), (gains, full_spec((3, d)))], [(w, tn)],
        [((m, d), F32, rows_spec(length, d)), ((m, d), BF16, rows_spec(length, d)),
         ((m, n), BF16, rows_spec(length, n))],
        [], 2 * m * d * (n + pk),
    )


def attn_forward(qkv, lengths, clips, length, heads, masked):
    d = qkv.shape[1] // 3
    hd = d // heads
    scale = hd ** (-0.5)
    tiles = d // 128

    def body(s_refs, ins, outs, _scr, _wb, _wait):
        qkv_ref, out = ins[0], outs[0]
        lane = lax.broadcasted_iota(jnp.int32, (1, 128), 1)
        if masked:
            keys = lax.broadcasted_iota(jnp.int32, (1, length), 1)
            ok = keys < s_refs[0][pl.program_id(0)]
        acc = {}
        for h in range(heads):
            lo, hi = h * hd, (h + 1) * hd
            t0, t1 = lo // 128, (hi - 1) // 128
            wide = (t1 - t0 + 1) * 128
            at = slice(t0 * 128, t0 * 128 + wide)
            col = lax.broadcasted_iota(jnp.int32, (1, wide), 1) + t0 * 128
            mine = (col >= lo) & (col < hi)
            q = qkv_ref[:, at]
            q = jnp.where(mine, q, jnp.zeros_like(q))
            k = qkv_ref[:, d + t0 * 128 : d + t0 * 128 + wide]
            v = qkv_ref[:, 2 * d + t0 * 128 : 2 * d + t0 * 128 + wide]
            sc = dot_nt(q, k) * scale
            if masked:
                sc = jnp.where(ok, sc, -1e30)
            e = jnp.exp(sc - jnp.max(sc, axis=-1, keepdims=True))
            p = to_low(e * (1.0 / jnp.sum(e, axis=-1, keepdims=True)))
            o = dot_f32(p, v)
            for t in range(t0, t1 + 1):
                part = o[:, (t - t0) * 128 : (t - t0 + 1) * 128]
                full = lane + t * 128
                sel = (full >= lo) & (full < hi)
                acc[t] = jnp.where(sel, part, acc[t]) if t in acc else part
                if min((t + 1) * 128, d) <= hi:
                    out[:, t * 128 : (t + 1) * 128] = to_low(acc.pop(t))

    m = clips * length
    return run_kernel(
        body, "attn_forward", (clips,), [lengths], [(qkv, rows_spec(length, 3 * d))], [],
        [((m, d), BF16, rows_spec(length, d))], [], 4 * m * length * 256 * heads,
    )[0]


def out_norm(mixed, resid, gains, w, clips, length):
    d = w.n

    def body(_s, ins, outs, _scr, wb, wait):
        wait(0, 0)
        x1 = ins[1][...].astype(F32) + dot_f32(ins[0][...], wb[0][...])
        outs[0][...] = x1
        outs[1][...] = to_low(normed(x1, ins[2][1:2, :]))

    m = clips * length
    outs = [((m, d), F32, rows_spec(length, d)), ((m, d), BF16, rows_spec(length, d))]
    return run_kernel(
        body, "out_norm", (clips,), [],
        [(mixed, rows_spec(length, d)), (resid, rows_spec(length, d)), (gains, full_spec((3, d)))], [(w, d)],
        outs, [], 2 * m * d * d,
    )


def gelu_parts(z):
    zz = z * z
    t = jnp.tanh(GELU_C * z * (1.0 + GELU_A * zz))
    half = 0.5 * (1.0 + t)
    return z * half, half, t, zz


def up_gelu(h_two, w, clips, length, tn, keep):
    d, n = w.k, w.n

    def body(_s, ins, outs, _scr, wb, wait):
        h = ins[0][...]

        def step(t, c):
            wait(0, t)
            at = pl.ds(pl.multiple_of(t * tn, tn), tn)
            z = dot_f32(h, wb[0][:, at])
            u, half, tz, zz = gelu_parts(z)
            outs[0][:, at] = to_low(u)
            if keep:
                slope = half + z * (0.5 * GELU_C) * (1.0 - tz * tz) * (1.0 + (3.0 * GELU_A) * zz)
                outs[1][:, at] = to_low(slope)
            return c

        lax.fori_loop(0, n // tn, step, 0)

    m = clips * length
    outs = [((m, n), BF16, rows_spec(length, n))]
    if keep:
        outs += [((m, n), BF16, rows_spec(length, n))]
    return run_kernel(
        body, "up_gelu", (clips,), [], [(h_two, rows_spec(length, d))], [(w, tn)], outs, [], 2 * m * d * n,
    )


def down_left(hidden, resid, w, clips, length, kt):
    k, n = w.k, w.n

    def body(_s, ins, outs, _scr, wb, wait):
        wait(0, 0)
        outs[0][...] = ins[1][...]

        def step(t, c):
            at = pl.ds(pl.multiple_of(t * kt, kt), kt)
            outs[0][...] += dot_f32(ins[0][:, at], wb[0][at, :])
            return c

        lax.fori_loop(0, k // kt, step, 0)

    m = clips * length
    return run_kernel(
        body, "down_left", (clips,), [], [(hidden, rows_spec(length, k)), (resid, rows_spec(length, n))],
        [(w, n)], [((m, n), F32, rows_spec(length, n))], [], 2 * m * n * k,
    )[0]


def down_embed(hidden, resid, left, gains, lengths, w, w_proj, clips, length, kt, keep):
    d, k, pj, n = resid.shape[1], w.k, w_proj.n, w.n
    have = d - n

    def body(s_refs, ins, outs, scr, wb, wait):
        g = pl.program_id(0)
        wait(0, 0)
        if have:
            scr[0][:, :have] = ins[3][...]
        scr[0][:, have:] = ins[1][:, have:]

        def step(t, c):
            at = pl.ds(pl.multiple_of(t * kt, kt), kt)
            scr[0][:, have:] += dot_f32(ins[0][:, at], wb[0][at, :])
            return c

        lax.fori_loop(0, k // kt, step, 0)
        x2 = scr[0][...]
        size = s_refs[0][g]
        row = lax.broadcasted_iota(jnp.int32, (length, 1), 0)
        weight = jnp.where(row < size, 1.0 / size.astype(F32), 0.0)
        pooled = jnp.sum(normed(x2, ins[2][2:3, :]) * weight, axis=0, keepdims=True)
        scr[1][pl.ds(g, 1), :] = pooled
        if keep:
            outs[3][...] = x2
        wait(1, 0)

        @pl.when(g == clips - 1)
        def _():
            pool_all = scr[1][...]
            raw = dot_f32(to_low(pool_all), wb[1][...])
            outs[0][...] = to_low(unit_rows(raw))
            outs[1][...] = raw
            outs[2][...] = pool_all

    m = clips * length
    outs = [((clips, pj), BF16, full_spec((clips, pj))), ((clips, pj), F32, full_spec((clips, pj))),
            ((clips, d), F32, full_spec((clips, d)))]
    if keep:
        outs += [((m, d), F32, rows_spec(length, d))]
    ins = [(hidden, rows_spec(length, k)), (resid, rows_spec(length, d)), (gains, full_spec((3, d)))]
    if have:
        ins.append((left, rows_spec(length, have)))
    return run_kernel(
        body, "down_embed", (clips,), [lengths], ins, [(w, n), (w_proj, pj)], outs,
        [pltpu.VMEM((length, d), F32), pltpu.VMEM((clips, d), F32)], 2 * m * n * k,
    )


def attn_backward(qkv, d_mixed, lengths, clips, length, heads, first=0, so_far=None):
    d = qkv.shape[1] // 3
    hd = d // heads
    scale = hd ** (-0.5)
    per = 128 // hd

    def body(s_refs, ins, outs, _scr, _wb, _wait):
        qkv_ref, do_ref, out = ins[0], ins[1], outs[0]
        lane = lax.broadcasted_iota(jnp.int32, (1, 128), 1)
        ok = lax.broadcasted_iota(jnp.int32, (1, length), 1) < s_refs[0][pl.program_id(0) + first]
        for t in range(d // 128):
            at = slice(t * 128, (t + 1) * 128)
            q, do = qkv_ref[:, at], do_ref[:, at]
            k = qkv_ref[:, d + t * 128 : d + (t + 1) * 128]
            v = qkv_ref[:, 2 * d + t * 128 : 2 * d + (t + 1) * 128]
            dq = dk = dv = None
            for h in range(per):
                mine = (lane >= h * hd) & (lane < (h + 1) * hd)
                qm = jnp.where(mine, q, jnp.zeros_like(q))
                dom = jnp.where(mine, do, jnp.zeros_like(do))
                sc = jnp.where(ok, dot_nt(qm, k) * scale, -1e30)
                e = jnp.exp(sc - jnp.max(sc, axis=-1, keepdims=True))
                p = e * (1.0 / jnp.sum(e, axis=-1, keepdims=True))
                dp = dot_nt(dom, v)
                ds = to_low(p * (dp - jnp.sum(p * dp, axis=-1, keepdims=True)))
                dv_h = dot_tn(to_low(p), do)
                dq_h = dot_f32(ds, k)
                dk_h = dot_tn(ds, q)
                dq = dq_h if dq is None else jnp.where(mine, dq_h, dq)
                dk = dk_h if dk is None else jnp.where(mine, dk_h, dk)
                dv = dv_h if dv is None else jnp.where(mine, dv_h, dv)
            out[:, at] = to_low(dq * scale)
            out[:, d + t * 128 : d + (t + 1) * 128] = to_low(dk * scale)
            out[:, 2 * d + t * 128 : 2 * d + (t + 1) * 128] = to_low(dv)

    m = qkv.shape[0]
    rows = lambda n: pl.BlockSpec((length, n), lambda i, *_: (i + first, 0))
    ins = [(qkv, rows(3 * d)), (d_mixed, rows(d))] + ([] if so_far is None else [(so_far, hbm_spec())])
    return run_kernel(
        body, "attn_backward", (clips,), [lengths], ins, [], [((m, 3 * d), BF16, rows(3 * d))], [],
        10 * clips * length * length * 256 * heads, None if so_far is None else 2,
    )[0]


def norm_back(resid, gain, d_out):
    center = resid - jnp.mean(resid, axis=-1, keepdims=True)
    rate = lax.rsqrt(jnp.mean(center * center, axis=-1, keepdims=True) + NORM_EPS)
    unit = center * rate
    d_unit = d_out * gain
    tail = unit * jnp.mean(d_unit * unit, axis=-1, keepdims=True)
    return rate * (d_unit - jnp.mean(d_unit, axis=-1, keepdims=True) - tail), jnp.sum(d_out * unit, axis=0, keepdims=True)


def packed_rows(parts):
    return sum(k // 8 * n // w for k, n, w in parts)


def gradient_outs(parts, fast):
    if not fast:
        return [((k, n), F32, full_spec((k, n))) for k, n, _ in parts]
    shape = (4, packed_rows(parts), parts[0][2])
    return [(shape, BF16, full_spec(shape)), (shape, F32, full_spec(shape))]


def emit_gradients(parts, accs, outs, core, fast):
    if not fast:
        for acc, out in zip(accs, outs):
            out[...] = acc[...]
        return
    for yx in range(4):
        for out, c in ((outs[0], 1 - core), (outs[1], core)):
            at = 0
            for (k, n, width), acc in zip(parts, accs):
                rows = k // 8
                first = pl.multiple_of((2 * yx + c) * rows, rows)
                for j in range(n // width):
                    out[yx, at : at + rows, :] = acc[pl.ds(first, rows), j * width : (j + 1) * width].astype(out.dtype)
                    at += rows
                rest = n % width
                if rest:
                    k2 = width // rest
                    for i in range(k2):
                        sub = rows // k2
                        part = acc[pl.ds(pl.multiple_of(first + i * sub, sub), sub), n - rest : n]
                        out[yx, at : at + sub, i * rest : (i + 1) * rest] = part.astype(out.dtype)
                    at += rows // k2


def contrast_back(joined, embed_raw, first_row, pj, micro, per):
    rows = joined.shape[1]
    row = lax.broadcasted_iota(jnp.int32, (rows, rows), 0)
    col = lax.broadcasted_iota(jnp.int32, (rows, rows), 1)
    same = row == col
    lane = lax.broadcasted_iota(jnp.int32, (rows, 128), 1)
    allowed, count = [], 0.0
    for m in range(micro):
        ids = joined[m, :, 2 * pj :].astype(F32)
        left = jnp.where(lane == 0, ids, jnp.where(lane == 1, 1.0, 0.0))
        right = jnp.where(lane == 0, 1.0, jnp.where(lane == 1, -ids, 0.0))
        allowed.append((dot_nt(to_low(left), to_low(right)) != 0.0) | same)
        count = count + jnp.sum(allowed[m].astype(F32))
    scale = rows / count
    total, d_embed = 0.0, None
    pick_row = lax.broadcasted_iota(jnp.int32, (micro * per, rows), 0)
    pick_col = lax.broadcasted_iota(jnp.int32, (micro * per, rows), 1)
    for m in range(micro):
        image = joined[m, :, pj : 2 * pj]
        logits = dot_nt(joined[m, :, :pj], image) * LOGIT_SCALE
        masked = jnp.where(allowed[m], logits, -1e30)
        row_top, col_top = jnp.max(masked, axis=1, keepdims=True), jnp.max(masked, axis=0, keepdims=True)
        row_lse = row_top + jnp.log(jnp.sum(jnp.exp(masked - row_top), axis=1, keepdims=True))
        col_lse = col_top + jnp.log(jnp.sum(jnp.exp(masked - col_top), axis=0, keepdims=True))
        matched = jnp.sum(jnp.where(same, logits, 0.0))
        total = total + (jnp.sum(row_lse) - matched) + (jnp.sum(col_lse) - matched)
        d_logits = jnp.exp(masked - row_lse) + jnp.exp(masked - col_lse) - jnp.where(same, 2.0, 0.0)
        here = (pick_row >= m * per) & (pick_row < (m + 1) * per) & (pick_col == first_row + pick_row - m * per)
        own = jnp.dot(here.astype(F32), d_logits * (scale * LOGIT_SCALE), precision=HIGHEST, preferred_element_type=F32)
        part = jnp.dot(own, image.astype(F32), precision=HIGHEST, preferred_element_type=F32)
        d_embed = part if d_embed is None else d_embed + part
    rate = lax.rsqrt(jnp.sum(embed_raw * embed_raw, axis=-1, keepdims=True) + NORM_EPS)
    inner = jnp.sum(embed_raw * d_embed, axis=-1, keepdims=True)
    return total * scale, rate * d_embed - embed_raw * (rate * rate * rate * inner)


def down_backward(joined, embed_raw, pooled, resid_out, hidden, slope, gains, lengths, place, w, w_proj, clips, length,
                  fast):
    k, d, pj = w.k, w.n, w_proj.n
    kt = d
    parts = [(k, d, d), (d, pj, d)]

    def body(s_refs, ins, outs, scr, wb, wait):
        g = pl.program_id(0)
        sizes, at = s_refs
        joined_ref, raw_ref, pooled_ref, x2_ref, u_ref, slope_ref, gain_ref = ins
        loss_ref, dpre_ref, dout_ref, g3_ref = outs[:4]
        d_pooled, d_raw_ref, acc = scr
        wait(1, 0)

        @pl.when(g == 0)
        def _():
            loss, d_raw = contrast_back(joined_ref[...], raw_ref[...], at[1], pj, MICRO, clips // MICRO)
            loss_ref[...] = jnp.full((1, 128), loss, F32)
            d_raw_ref[...] = to_low(d_raw)
            d_pooled[...] = dot_nt(to_low(d_raw), wb[1][...])
            acc[...] = jnp.zeros_like(acc)
            g3_ref[...] = jnp.zeros_like(g3_ref)

        size = sizes[g]
        row = lax.broadcasted_iota(jnp.int32, (length, 1), 0)
        weight = jnp.where(row < size, 1.0 / size.astype(F32), 0.0)
        d_out, g_three = norm_back(x2_ref[...], gain_ref[2:3, :], d_pooled[pl.ds(g, 1), :] * weight)
        g3_ref[...] += g_three
        dout_ref[...] = d_out
        d_low = to_low(d_out)
        wait(0, 0)

        def step(t, c):
            cols = pl.ds(pl.multiple_of(t * kt, kt), kt)
            d_hidden = dot_nt(d_low, wb[0][cols, :])
            dpre_ref[:, cols] = to_low(d_hidden * slope_ref[:, cols].astype(F32))
            acc[cols, :] += dot_tn(u_ref[:, cols], d_low)
            return c

        lax.fori_loop(0, k // kt, step, 0)

        @pl.when(g == clips - 1)
        def _():
            g_proj = dot_tn(to_low(pooled_ref[...]), d_raw_ref[...])
            outs[6][...] = g_proj
            emit_gradients(parts, [acc, outs[6]], outs[4:6], at[0], fast)

    m = clips * length
    outs = [((1, 128), F32, full_spec((1, 128))), ((m, k), BF16, rows_spec(length, k)),
            ((m, d), F32, rows_spec(length, d)), ((1, d), F32, full_spec((1, d)))]
    outs += gradient_outs(parts, fast) + [((d, pj), F32, full_spec((d, pj)))]
    ins = [(joined, full_spec(joined.shape)), (embed_raw, full_spec((clips, pj))), (pooled, full_spec((clips, d))),
           (resid_out, rows_spec(length, d)), (hidden, rows_spec(length, k)), (slope, rows_spec(length, k)),
           (gains, full_spec((3, d)))]
    return run_kernel(
        body, "down_backward", (clips,), [lengths, place], ins, [(w, d), (w_proj, pj)], outs,
        [pltpu.VMEM((clips, d), F32), pltpu.VMEM((clips, pj), BF16), pltpu.VMEM((k, d), F32)], 4 * m * d * k,
    )


def up_backward(d_pre, h_two, resid_mid, d_out, mixed, gains, place, w, w_out, clips, length, kt, fast):
    d, n = w.k, w.n
    parts = [(d, n, d), (d, d, d)]

    def body(s_refs, ins, outs, scr, wb, wait):
        g = pl.program_id(0)
        (at,) = s_refs
        dpre_ref, h_ref, x1_ref, dout_ref, o_ref, gain_ref = ins
        dmid_ref, dmix_ref, g2_ref = outs[:3]
        acc, acc_out, back = scr

        @pl.when(g == 0)
        def _():
            acc[...] = jnp.zeros_like(acc)
            acc_out[...] = jnp.zeros_like(acc_out)
            g2_ref[...] = jnp.zeros_like(g2_ref)

        h = h_ref[...]
        back[...] = jnp.zeros_like(back)

        def step(t, c):
            cols = pl.ds(pl.multiple_of(t * kt, kt), kt)
            wait(0, t)
            dp = dpre_ref[:, cols]
            acc[:, cols] += dot_tn(h, dp)
            back[...] += dot_nt(dp, wb[0][:, cols])
            return c

        lax.fori_loop(0, n // kt, step, 0)
        d_ln, g_two = norm_back(x1_ref[...], gain_ref[1:2, :], back[...])
        g2_ref[...] += g_two
        d_mid = dout_ref[...] + d_ln
        dmid_ref[...] = d_mid
        d_low = to_low(d_mid)
        wait(1, 0)
        acc_out[...] += dot_tn(o_ref[...], d_low)
        dmix_ref[...] = to_low(dot_nt(d_low, wb[1][...]))

        @pl.when(g == clips - 1)
        def _():
            emit_gradients(parts, [acc, acc_out], outs[3:5], at[0], fast)

    m = clips * length
    rows = rows_spec(length, d)
    outs = [((m, d), F32, rows), ((m, d), BF16, rows), ((1, d), F32, full_spec((1, d)))] + gradient_outs(parts, fast)
    ins = [(d_pre, rows_spec(length, n)), (h_two, rows), (resid_mid, rows), (d_out, rows), (mixed, rows),
           (gains, full_spec((3, d)))]
    return run_kernel(
        body, "up_backward", (clips,), [place], ins, [(w, kt), (w_out, d)], outs,
        [pltpu.VMEM((d, n), F32), pltpu.VMEM((d, d), F32), pltpu.VMEM((length, d), F32)], 4 * m * d * (n + d),
    )


def qkv_backward(d_qkv, h_one, resid_in, d_mid, patches, gains, g_two, g_three, place, w, clips, length, fast):
    d, n, pk = w.k, w.n, patches.shape[1]
    parts = [(d, n, d), (pk, d, d)]
    extra = 16

    def body(s_refs, ins, outs, scr, wb, wait):
        g = pl.program_id(0)
        (at,) = s_refs
        dqkv_ref, h_ref, x0_ref, dmid_ref, patch_ref, gain_ref, g2_ref, g3_ref = ins
        acc, acc_patch, back, acc_gain = scr

        @pl.when(g == 0)
        def _():
            acc[...] = jnp.zeros_like(acc)
            acc_patch[...] = jnp.zeros_like(acc_patch)
            acc_gain[...] = jnp.zeros_like(acc_gain)
            acc_gain[1:2, :] = g2_ref[...]
            acc_gain[2:3, :] = g3_ref[...]

        h = h_ref[...]
        back[...] = jnp.zeros_like(back)

        def step(t, c):
            cols = pl.ds(pl.multiple_of(t * d, d), d)
            wait(0, t)
            dq = dqkv_ref[:, cols]
            acc[:, cols] += dot_tn(h, dq)
            back[...] += dot_nt(dq, wb[0][:, cols])
            return c

        lax.fori_loop(0, n // d, step, 0)
        d_ln, g_one = norm_back(x0_ref[...], gain_ref[0:1, :], back[...])
        acc_gain[0:1, :] += g_one
        acc_patch[...] += dot_tn(patch_ref[...], to_low(dmid_ref[...] + d_ln))

        @pl.when(g == clips - 1)
        def _():
            emit_gradients(parts, [acc, acc_patch], outs[:2], at[0], fast)
            if fast:
                rows = packed_rows(parts)
                for yx in range(4):
                    for out in outs[:2]:
                        out[yx, rows : rows + extra, :] = acc_gain[...].astype(out.dtype)
            else:
                outs[2][...] = acc_gain[...]

    m = clips * length
    rows = rows_spec(length, d)
    if fast:
        shape = (4, packed_rows(parts) + extra, d)
        outs = [(shape, BF16, full_spec(shape)), (shape, F32, full_spec(shape))]
    else:
        outs = gradient_outs(parts, fast) + [((extra, d), F32, full_spec((extra, d)))]
    ins = [(d_qkv, rows_spec(length, n)), (h_one, rows), (resid_in, rows), (d_mid, rows),
           (patches, rows_spec(length, pk)), (gains, full_spec((3, d))), (g_two, full_spec((1, d))),
           (g_three, full_spec((1, d)))]
    return run_kernel(
        body, "qkv_backward", (clips,), [place], ins, [(w, d)], outs,
        [pltpu.VMEM((d, n), F32), pltpu.VMEM((pk, d), F32), pltpu.VMEM((length, d), F32), pltpu.VMEM((extra, d), F32)],
        4 * m * d * n,
    )


AXES = ("dp", "rep")


def joint_perm(reps, fn):
    out = []
    for dp in range(8):
        for z in range(reps):
            dst = fn(dp, z)
            if dst is not None:
                out.append((dp * reps + z, dst[0] * reps + dst[1]))
    return out


def send(value, reps, fn):
    return lax.ppermute(value, AXES, joint_perm(reps, fn))


class Ring:
    def __init__(self, packed, col, width, reps):
        self.own, self.col, self.width, self.reps = packed, col, width, reps
        self.mine = packed[:, col : col + width]

    def first(self):
        self.near = send(self.mine, self.reps, lambda dp, z: (dp ^ (2 if z % 2 == 0 else 4), z))

    def second(self):
        self.diag = send(self.near, self.reps, lambda dp, z: (dp ^ (4 if z % 2 == 0 else 2), z))
        self.other = send(self.near, self.reps, lambda dp, z: (dp, z ^ 1))

    def twin(self, *names):
        for name in names:
            setattr(self, name + "_twin", send(getattr(self, name), self.reps, lambda dp, z: (dp ^ 1, z)))

    def group(self, own_twin):
        odd = lax.axis_index("rep") % 2 == 1
        x, y = jnp.int32(2), jnp.int32(4)
        flip = jnp.stack([jnp.int32(0), jnp.where(odd, y, x), jnp.int32(6), jnp.where(odd, x, y)])
        base = jnp.bitwise_xor(flip, lax.axis_index("dp").astype(jnp.int32))
        arrays = [self.own, self.near, self.diag, self.other, own_twin, self.near_twin, self.diag_twin, self.other_twin]
        index = jnp.concatenate([base, jnp.bitwise_xor(base, 1)])
        return Group(arrays, index, self.own.shape[0], (self.col, 0, 0, 0) * 2)


def fence(held, values):
    flat = [(r, n) for r, names in held for n in names.split()]
    out = lax.optimization_barrier(tuple(getattr(r, n) for r, n in flat) + tuple(values))
    for (r, n), v in zip(flat, out):
        setattr(r, n, v)
    return out[len(flat) :]


def take(v, i, axis):
    return lax.dynamic_index_in_dim(v, i, axis, keepdims=False)


def from_width(v, rows, n):
    width = v.shape[-1]
    full = n // width
    blocks = [v[i * rows : (i + 1) * rows] for i in range(full)]
    rest = n % width
    if rest:
        last, k = v[full * rows :], width // rest
        blocks.append(jnp.concatenate([last[:, i * rest : (i + 1) * rest] for i in range(k)], axis=0))
    return jnp.concatenate(blocks, axis=1)


class Sum:
    def __init__(self, leave, stay, parts, reps):
        self.reps, self.leave, self.stay, self.parts = reps, leave, stay, parts
        me = lax.axis_index("dp")
        self.y, self.x = me // 4, (me // 2) % 2
        self.odd = lax.axis_index("rep") % 2 == 1

    def hops(self, *pairs):
        self.due = [(to_low(v), fn) for v, fn in pairs]

    def core(self):
        self.hops((self.leave, lambda dp, z: (dp ^ 1, z)))

    def plane(self):
        s = (self.stay + self.got[0].astype(F32)).reshape((2, 2) + self.stay.shape[1:])
        half = s.shape[-2] // 2
        self.a, self.b = s[:, :, :half], s[:, :, half:]
        self.hops((take(self.a, 1 - self.x, 1), lambda dp, z: (dp ^ 2, z)),
                  (take(self.b, 1 - self.y, 0), lambda dp, z: (dp ^ 4, z)))

    def plane_again(self):
        self.a = take(self.a, self.x, 1) + self.got[0].astype(F32)
        self.b = take(self.b, self.y, 0) + self.got[1].astype(F32)
        self.hops((take(self.a, 1 - self.y, 0), lambda dp, z: (dp ^ 4, z)),
                  (take(self.b, 1 - self.x, 0), lambda dp, z: (dp ^ 2, z)))

    def pair(self):
        a = take(self.a, self.y, 0) + self.got[0].astype(F32)
        b = take(self.b, self.x, 0) + self.got[1].astype(F32)
        self.a = jnp.where(self.odd, b, a)
        self.hops((jnp.where(self.odd, a, b), lambda dp, z: (dp, z ^ 1)))

    def across(self):
        self.a = to_low(self.a + self.got[0].astype(F32))
        self.hops((self.a, lambda dp, z: (dp, z ^ 2)))

    def share(self):
        self.a = to_low(self.a.astype(F32) + self.got[0].astype(F32))
        self.hops((self.a, lambda dp, z: (dp, z ^ 1)))

    def result(self):
        other = self.got[0]
        total = jnp.concatenate([jnp.where(self.odd, other, self.a), jnp.where(self.odd, self.a, other)], axis=0)
        total, out, at = total.astype(F32), [], 0
        for k, n, width in self.parts:
            rows = k // 8
            size = rows * n // width
            out.append(from_width(total[at : at + size], rows, n))
            at += size
        return out


def go(sums, *values):
    flat = [v for s in sums for v, _ in s.due]
    out = lax.optimization_barrier(tuple(flat) + values)
    at = 0
    for s in sums:
        s.got = tuple(send(out[at + i], s.reps, fn) for i, (_, fn) in enumerate(s.due))
        at += len(s.due)
    return out[at:]


def order(sums, *values):
    flat = [g for s in sums for g in s.got]
    out = lax.optimization_barrier(tuple(flat) + values)
    at = 0
    for s in sums:
        s.got = out[at : at + len(s.got)]
        at += len(s.got)
    return out[at:]


def adam_step(weight, gradient, moment_one, moment_two, step_rate, decay):
    first_new = BETA_ONE * moment_one + (1.0 - BETA_ONE) * gradient
    second_new = BETA_TWO * moment_two + (1.0 - BETA_TWO) * gradient * gradient
    fixed_one = first_new / (1.0 - BETA_ONE**STEP)
    fixed_two = second_new / (1.0 - BETA_TWO**STEP)
    update = fixed_one / (jnp.sqrt(fixed_two) + ADAM_EPS) + decay * weight
    return (weight - step_rate * update, first_new, second_new)


def as_columns(v, rows):
    return jnp.concatenate([v[i * rows : (i + 1) * rows] for i in range(v.shape[0] // rows)], axis=1)


def local(dp_size, rep_size, *args):
    (audio_patches, clip_lengths, video_ids, image_tokens, i_qkv, i_out, i_up, i_down, i_proj, i_gains) = args[:10]
    masters, firsts_in, seconds_in = args[10:17], args[17:24], args[24:31]
    a_patch, a_qkv, a_out, a_up, a_down, a_proj, a_gains = (to_low(w) for w in masters)
    fast = dp_size == 8 and rep_size == 4
    clip_dev = audio_patches.shape[1]
    clips = MICRO * clip_dev
    d_i, d_a, ff_a, pj = i_out.shape[1], a_out.shape[1], a_up.shape[1], a_proj.shape[1]
    ff_i = i_up.shape[1]

    rp = a_patch.shape[0]
    small = jnp.concatenate(
        [a_patch, jnp.pad(a_gains.reshape(1, -1), ((0, 0), (0, d_a - a_gains.size))),
         jnp.pad(i_gains.reshape(1, -1), ((0, 0), (0, d_a - i_gains.size)))], axis=0)
    small = lax.all_gather(small, "dp", axis=0)
    img_sizes = jnp.full((clips,), IMG_LEN, jnp.int32)
    tokens = image_tokens.reshape(clips * IMG_LEN, d_i)
    sizes = clip_lengths.reshape(clips)
    patches = jnp.pad(audio_patches.reshape(clips, LEN, -1), ((0, 0), (0, PAD_LEN - LEN), (0, 0)))
    patches = patches.reshape(clips * PAD_LEN, -1)
    half, sub_i, sub_a = ff_i // 2, ff_i // d_i, ff_a // d_a
    dl = d_i * 3 // 5
    fr = d_a * 8 // 3
    if fast:
        down_i, down_a = as_columns(i_down, i_qkv.shape[0]), as_columns(a_down, a_qkv.shape[0])
        left = [down_i[:, j * d_i : j * d_i + dl] for j in range(sub_i)]
        right = [down_i[:, j * d_i + dl : (j + 1) * d_i] for j in range(sub_i)]
        own_a = jnp.concatenate([a_qkv, a_out, a_up, down_a, a_proj], axis=1)
        own_i = jnp.concatenate([i_qkv, i_out, i_up, i_proj] + left + right, axis=1)
        small, own_a = lax.optimization_barrier((small, own_a))
        cut_a = 4 * d_a + fr
        ca = Ring(own_a, 0, cut_a, rep_size), Ring(own_a, cut_a, own_a.shape[1] - cut_a, rep_size)
        widths, at, ci = [3 * d_i, d_i + half, half + pj, sub_i * dl, sub_i * (d_i - dl)], 0, []
        for wd in widths:
            ci.append(Ring(own_i, at, wd, rep_size))
            at += wd
        swap = lambda v: send(v, rep_size, lambda dp, z: (dp ^ 1, z))
        twin_a = swap(own_a)

        ca[0].first()
        fence([(ca[0], "near"), (ca[1], "mine")], ())
        ca[0].second()
        ca[0].twin("near")
        ca[1].first()
        patches, twin_a = fence([(ca[0], "diag other near_twin"), (ca[1], "near"), (ci[0], "mine")], (patches, twin_a))
        ca[0].twin("diag", "other")
        ca[1].second()
        ca[1].twin("near")
        ci[0].first()
        ga0 = ca[0].group(twin_a)
        wa_qkv = Weight(d_a, 3 * d_a, [(ga0, 0, 3 * d_a, 0, 0)])
        wa_out = Weight(d_a, d_a, [(ga0, 3 * d_a, d_a, 0, 0)])
    else:
        whole = lambda v: lax.all_gather(v, "dp", axis=0, tiled=True)
        make = lambda v: Weight(v.shape[0] * dp_size, v.shape[1], whole=whole(v))
        cut = lambda v: Weight(v.shape[0], v.shape[1], whole=v)
        wi_qkv, wi_out, wi_up, wi_proj = (make(v) for v in (i_qkv, i_out, i_up, i_proj))
        wi_left, wi_right = cut(whole(i_down)[:, :dl]), cut(whole(i_down)[:, dl:])
        wa_qkv, wa_out, wa_up, wa_down, wa_proj = (make(v) for v in (a_qkv, a_out, a_up, a_down, a_proj))

    w_patch = small[:, :rp].reshape(rp * dp_size, d_a)
    unpack = lambda v, g: v[:, : g.size].reshape(dp_size, 3, -1).transpose(1, 0, 2).reshape(3, -1).astype(F32)
    gains_a, gains_i = unpack(small[:, rp], a_gains), unpack(small[:, rp + 1], i_gains)

    got = audio_in(patches, w_patch, gains_a, wa_qkv, clips, PAD_LEN, d_a)
    resid_in, h_one, qkv = got[:3]
    mixed = attn_forward(qkv, sizes, clips, PAD_LEN, HEADS_A, True)
    got = out_norm(mixed, resid_in, gains_a, wa_out, clips, PAD_LEN)
    resid_mid, h_two = got[:2]

    if fast:
        (h_two,) = fence([(ca[1], "diag other near_twin"), (ci[0], "near"), (ci[1], "mine")], (h_two,))
        ca[1].twin("diag", "other")
        ci[0].second()
        ci[0].twin("near")
        ci[1].first()
        twin_i = swap(own_i)
        ga1 = ca[1].group(twin_a)
        wa_up = Weight(d_a, ff_a, [(ga0, 4 * d_a, fr, 0, 0), (ga1, 0, ff_a - fr, fr, 0)])
        wa_down = Weight(ff_a, d_a, [(ga1, ff_a - fr + j * d_a, d_a, 0, j) for j in range(sub_a)], sub=sub_a)
        wa_proj = Weight(d_a, pj, [(ga1, 2 * ff_a - fr, pj, 0, 0)])
    got = up_gelu(h_two, wa_up, clips, PAD_LEN, 1024, True)
    hidden, slope = got[:2]

    if fast:
        hidden, tokens, twin_i = fence(
            [(ci[0], "diag other near_twin"), (ci[1], "near"), (ci[2], "mine")], (hidden, tokens, twin_i))
        ci[0].twin("diag", "other")
        ci[1].second()
        ci[1].twin("near")
        ci[2].first()
        gi = [ci[0].group(twin_i)]
        wi_qkv = Weight(d_i, 3 * d_i, [(gi[0], 0, 3 * d_i, 0, 0)])
    qkv_i = image_qkv(tokens, gains_i, wi_qkv, clips, IMG_LEN, d_i)
    mixed_i = attn_forward(qkv_i, img_sizes, clips, IMG_LEN, HEADS_I, False)

    if fast:
        mixed_i, hidden = fence(
            [(ci[1], "diag other near_twin"), (ci[2], "near"), (ci[3], "mine")], (mixed_i, hidden))
        ci[1].twin("diag", "other")
        ci[2].second()
        ci[2].twin("near")
        ci[3].first()
        gi.append(ci[1].group(twin_i))
        wi_out = Weight(d_i, d_i, [(gi[1], 0, d_i, 0, 0)])
    got = down_embed(hidden, resid_mid, None, gains_a, sizes, wa_down, wa_proj, clips, PAD_LEN, d_a, True)
    aud_emb, embed_raw, pooled, resid_out = got[:4]
    mid_i, h_two_i = out_norm(mixed_i, tokens, gains_i, wi_out, clips, IMG_LEN)

    if fast:
        h_two_i, aud_emb = fence(
            [(ci[2], "diag other near_twin"), (ci[3], "near"), (ci[4], "mine")], (h_two_i, aud_emb))
        ci[2].twin("diag", "other")
        ci[3].second()
        ci[3].twin("near")
        ci[4].first()
        gi.append(ci[2].group(twin_i))
        wi_up = Weight(d_i, ff_i, [(gi[1], d_i, half, 0, 0), (gi[2], 0, half, half, 0)])
        wi_proj = Weight(d_i, pj, [(gi[2], half, pj, 0, 0)])
    hidden_i = up_gelu(h_two_i, wi_up, clips, IMG_LEN, d_i, False)[0]

    if fast:
        (hidden_i,) = fence([(ci[3], "diag other near_twin"), (ci[4], "near")], (hidden_i,))
        ci[3].twin("diag", "other")
        ci[4].second()
        ci[4].twin("near")
        gi.append(ci[3].group(twin_i))
        wi_left = Weight(ff_i, dl, [(gi[3], j * dl, dl, 0, j) for j in range(sub_i)], sub=sub_i)
    left_i = down_left(hidden_i, mid_i, wi_left, clips, IMG_LEN, d_i)

    if fast:
        (left_i,) = fence([(ci[4], "diag other near_twin")], (left_i,))
        ci[4].twin("diag", "other")
        gi.append(ci[4].group(twin_i))
        dr = d_i - dl
        wi_right = Weight(ff_i, dr, [(gi[4], j * dr, dr, 0, j) for j in range(sub_i)], sub=sub_i)
    img_emb = down_embed(hidden_i, mid_i, left_i, gains_i, img_sizes, wi_right, wi_proj, clips, IMG_LEN, d_i, False)[0]

    ids_low = jnp.broadcast_to(to_low(video_ids.reshape(clips, 1)), (clips, 128))
    joined = jnp.concatenate([aud_emb, img_emb, ids_low], axis=1).reshape(MICRO, clip_dev, 2 * pj + 128)
    joined = lax.all_gather(lax.all_gather(joined, "rep", axis=1, tiled=True), "dp", axis=1, tiled=True)
    me = lax.axis_index("dp").astype(jnp.int32)
    first_row = lax.axis_index(AXES).astype(jnp.int32) * clip_dev
    place = jnp.stack([me % 2, first_row])
    got = down_backward(joined, embed_raw, pooled, resid_out, hidden, slope, gains_a, sizes, place, wa_down, wa_proj,
                        clips, PAD_LEN, fast)
    loss, d_pre, d_out, g_three = got[0][0, 0], *got[1:4]
    if fast:
        s_down = Sum(got[4], got[5], [(ff_a, d_a, d_a), (d_a, pj, d_a)], rep_size)
        s_down.core()
        (d_pre,) = go([s_down], d_pre)
    up = up_backward(d_pre, h_two, resid_mid, d_out, mixed, gains_a, place, wa_up, wa_out, clips, PAD_LEN, 1024, fast)
    d_mid, d_mixed, g_two = up[:3]
    if fast:
        (d_mixed,) = order([s_down], d_mixed)
        s_down.plane()
        s_up = Sum(up[3], up[4], [(d_a, ff_a, d_a), (d_a, d_a, d_a)], rep_size)
        s_up.core()
        (d_mixed,) = go([s_down, s_up], d_mixed)
    d_qkv = attn_backward(qkv, d_mixed, sizes, clip_dev, PAD_LEN, HEADS_A)
    if fast:
        d_qkv, d_mixed = order([s_down, s_up], d_qkv, d_mixed)
        s_down.plane_again()
        s_up.plane()
        d_qkv, d_mixed = go([s_down, s_up], d_qkv, d_mixed)
    d_qkv = attn_backward(qkv, d_mixed, sizes, clips - clip_dev, PAD_LEN, HEADS_A, clip_dev, d_qkv)
    if fast:
        (d_qkv,) = order([s_down, s_up], d_qkv)
        s_down.pair()
        s_up.plane_again()
        (d_qkv,) = go([s_down, s_up], d_qkv)
    last = qkv_backward(d_qkv, h_one, resid_in, d_mid, patches, gains_a, g_two, g_three, place, wa_qkv, clips, PAD_LEN,
                        fast)
    share = d_a // dp_size
    mine = lambda v: lax.dynamic_slice_in_dim(v[:3], me * share, share, 1)
    if fast:
        leave, stay = order([s_down, s_up], last[0], last[1])
        s_qkv = Sum(leave, stay, [(d_a, 3 * d_a, d_a), (w_patch.shape[0], d_a, d_a), (128, d_a, d_a)], rep_size)
        s_qkv.core()
        s_down.across()
        s_up.pair()
        go([s_qkv, s_down, s_up])
        order([s_qkv])
        s_qkv.plane()
        go([s_qkv])
        order([s_down, s_up])
        s_up.across()
        s_down.share()
        go([s_up, s_down])
        order([s_qkv])
        s_qkv.plane_again()
        go([s_qkv])
        order([s_qkv, s_up])
        s_qkv.pair()
        s_up.share()
        go([s_qkv, s_up])
        order([s_qkv])
        s_qkv.across()
        go([s_qkv])
        s_qkv.share()
        go([s_qkv])
        r_down, r_proj = s_down.result()
        r_up, r_out = s_up.result()
        r_qkv, r_patch, r_gain = s_qkv.result()
        summed = [r_patch, r_qkv, r_out, r_up, r_down, r_proj, mine(r_gain)]
    else:
        grads = (last[1], last[0], up[4], up[3], got[4], got[5])
        summed = [lax.psum(lax.psum_scatter(v, "dp", scatter_dimension=0, tiled=True), "rep") for v in grads]
        summed.append(mine(lax.psum(last[2], AXES)))
    local_squares = sum(jnp.sum(v * v) for v in summed)
    grad_norm = jnp.sqrt(lax.psum(local_squares, "dp"))
    factor = jnp.minimum(1.0, CLIP_NORM / grad_norm)
    results = []
    for index in range(7):
        step_rate = RATE_GAIN if index == 6 else RATE_MATRIX
        decay = 0.0 if index == 6 else WEIGHT_DECAY
        results.append(
            adam_step(masters[index], summed[index] * factor, firsts_in[index], seconds_in[index], step_rate, decay)
        )
    return (loss, grad_norm, *(r[0] for r in results), *(r[1] for r in results), *(r[2] for r in results))


def solution(mesh):
    batch4 = P(None, AXES, None, None)
    batch2 = P(None, AXES)
    split = P("dp", None)
    gain = P(None, "dp")
    weights = (split,) * 6 + (gain,)
    placed = (batch4, batch2, batch2, batch4) + (split,) * 5 + (gain,) + weights * 3
    return jax.shard_map(
        functools.partial(local, mesh.shape["dp"], mesh.shape["rep"]),
        mesh=mesh,
        in_specs=placed,
        out_specs=(P(), P()) + weights * 3,
        check_vma=False,
    )
```

```python
import functools

import jax
import jax.numpy as jnp
from jax import lax
from jax.experimental import pallas as pl
from jax.experimental.pallas import tpu as pltpu
from jax.sharding import PartitionSpec as P

HEADS_A = 12
HEADS_I = 16
LEN = 228
IMG_LEN = 256
MICRO = 2
STEP = 7

HIGHEST = lax.Precision.HIGHEST
F32 = jnp.float32
BF16 = jnp.bfloat16
NORM_EPS = 1e-06
LOGIT_SCALE = 50.0
CLIP_NORM = 0.01
BETA_ONE = 0.9
BETA_TWO = 0.999
ADAM_EPS = 1e-08
WEIGHT_DECAY = 0.1
RATE_MATRIX = 0.05
RATE_GAIN = 0.3
PAD_LEN = 240
GELU_C = 0.7978845608028654
GELU_A = 0.044715
VMEM_GRANT = 60 << 20


def to_low(v):
    return v.astype(BF16)


def normed(resid, gain):
    center = resid - jnp.mean(resid, axis=-1, keepdims=True)
    spread = jnp.mean(center * center, axis=-1, keepdims=True)
    return center * lax.rsqrt(spread + NORM_EPS) * gain


def unit_rows(embed_raw):
    return embed_raw * lax.rsqrt(jnp.sum(embed_raw * embed_raw, axis=-1, keepdims=True) + NORM_EPS)


def dot_f32(a, b):
    return lax.dot_general(a, b, (((1,), (0,)), ((), ())), preferred_element_type=F32)


def dot_nt(a, b):
    return lax.dot_general(a, b, (((1,), (1,)), ((), ())), preferred_element_type=F32)


def dot_tn(a, b):
    return lax.dot_general(a, b, (((0,), (0,)), ((), ())), preferred_element_type=F32)


class Group:
    def __init__(self, arrays, index, rows, cols):
        self.arrays, self.index, self.rows, self.cols = arrays, index, rows, cols


class Weight:
    def __init__(self, k, n, segs=None, sub=1, whole=None):
        self.k, self.n, self.segs, self.sub, self.whole = k, n, segs, sub, whole

    def groups(self):
        seen = []
        for seg in self.segs:
            if seg[0] not in seen:
                seen.append(seg[0])
        return seen

    def operands(self):
        if self.whole is not None:
            return [self.whole]
        return [v for g in self.groups() for v in g.arrays]

    def indices(self):
        return [] if self.whole is not None else [g.index for g in self.groups()]

    def entries(self, tn):
        groups, out = self.groups(), []
        for g, col, width, dst, part in self.segs:
            assert width % tn == 0
            out += [(groups.index(g), col + t * tn, dst + t * tn, part) for t in range(width // tn)]
        return sorted(out, key=lambda e: (e[2], e[3]))


def start_weight(w, tn, refs, idx, wbuf, sem):
    if w.whole is not None:
        for t in range(w.n // tn):
            cols = pl.ds(t * tn, tn)
            pltpu.make_async_copy(refs[0].at[:, cols], wbuf.at[:, cols], sem.at[t, 0]).start()
        return
    for e, (gi, col, dst, part) in enumerate(w.entries(tn)):
        rows = w.groups()[gi].rows
        for p in range(8):
            at = pl.multiple_of(idx[gi][p] * (rows * w.sub) + part * rows, rows)
            pltpu.make_async_copy(
                refs[8 * gi + p].at[:, pl.ds(w.groups()[gi].cols[p] + col, tn)],
                wbuf.at[pl.ds(at, rows), pl.ds(dst, tn)],
                sem.at[e, p],
            ).start()


def wait_weight(w, tn, refs, idx, wbuf, sem, t):
    cols = pl.ds(pl.multiple_of(t * tn, tn), tn)
    if w.whole is not None:
        pltpu.make_async_copy(refs[0].at[:, pl.ds(0, tn)], wbuf.at[:, cols], sem.at[t, 0]).wait()
        return
    rows = w.groups()[0].rows
    for part in range(w.sub):
        for p in range(8):
            pltpu.make_async_copy(
                refs[p].at[:, pl.ds(0, tn)], wbuf.at[pl.ds((p * w.sub + part) * rows, rows), cols],
                sem.at[t * w.sub + part, p],
            ).wait()


def weight_sems(w, tn):
    tiles = w.n // tn
    return pltpu.SemaphoreType.DMA((tiles, 1) if w.whole is not None else (tiles * w.sub, 8))


HBM = pltpu.MemorySpace.HBM


def hbm_spec():
    return pl.BlockSpec(memory_space=HBM)


def full_spec(shape):
    return pl.BlockSpec(shape, lambda *_: (0,) * len(shape))


def run_kernel(body, name, grid, scalars, ins, weights, outs, scratch, flops, alias=None):
    scal = list(scalars)
    for w, _ in weights:
        scal += w.indices()
    n_scal, n_user = len(scal), len(scalars)
    operands = [a for a, _ in ins]
    specs = [s for _, s in ins]
    for w, _ in weights:
        ops = w.operands()
        operands += ops
        specs += [hbm_spec()] * len(ops)
    n_in = len(ins)
    scr = list(scratch)
    for w, tn in weights:
        scr += [pltpu.VMEM((w.k, w.n), BF16), weight_sems(w, tn)]

    def kernel(*refs):
        s = refs[:n_scal]
        user_s, s = s[:n_user], s[n_user:]
        pos = n_scal
        in_refs = refs[pos : pos + n_in]
        pos += n_in
        w_refs = []
        for w, _ in weights:
            m = len(w.operands())
            w_refs.append(refs[pos : pos + m])
            pos += m
        out_refs = refs[pos : pos + len(outs)]
        pos += len(outs)
        scr_refs = refs[pos : pos + len(scratch)]
        pos += len(scratch)
        handles = []
        si = 0
        for wi, (w, tn) in enumerate(weights):
            gi = len(w.indices())
            handles.append((w, tn, w_refs[wi], s[si : si + gi], refs[pos], refs[pos + 1]))
            si += gi
            pos += 2
        first = pl.program_id(0) == 0

        @pl.when(first)
        def _():
            for h in handles:
                start_weight(*h)

        def wait(k, t):
            @pl.when(first)
            def _():
                wait_weight(*handles[k], t)

        body(user_s, in_refs, out_refs, scr_refs, [h[4] for h in handles], wait)

    bytes_acc = sum(int(a.size) * a.dtype.itemsize for a in operands) + sum(
        functools.reduce(lambda x, y: x * y, o[0], 1) * jnp.dtype(o[1]).itemsize for o in outs
    )
    return pl.pallas_call(
        kernel,
        grid_spec=pltpu.PrefetchScalarGridSpec(
            num_scalar_prefetch=n_scal,
            grid=grid,
            in_specs=specs,
            out_specs=[o[2] for o in outs],
            scratch_shapes=scr,
        ),
        out_shape=[jax.ShapeDtypeStruct(o[0], o[1]) for o in outs],
        input_output_aliases={} if alias is None else {n_scal + alias: 0},
        compiler_params=pltpu.CompilerParams(vmem_limit_bytes=VMEM_GRANT),
        cost_estimate=pl.CostEstimate(flops=flops, bytes_accessed=bytes_acc, transcendentals=0),
        name=name,
    )(*scal, *operands)


def rows_spec(length, width):
    return pl.BlockSpec((length, width), lambda i, *_: (i, 0))


def attend(qkv_ref, out, d, heads, size):
    length = qkv_ref.shape[0]
    hd = d // heads
    scale = hd ** (-0.5)
    lane = lax.broadcasted_iota(jnp.int32, (1, 128), 1)
    if size is not None:
        ok = lax.broadcasted_iota(jnp.int32, (1, length), 1) < size
    acc = {}
    for h in range(heads):
        lo, hi = h * hd, (h + 1) * hd
        t0, t1 = lo // 128, (hi - 1) // 128
        wide = (t1 - t0 + 1) * 128
        col = lax.broadcasted_iota(jnp.int32, (1, wide), 1) + t0 * 128
        q = qkv_ref[:, t0 * 128 : t0 * 128 + wide]
        q = jnp.where((col >= lo) & (col < hi), q, jnp.zeros_like(q))
        k = qkv_ref[:, d + t0 * 128 : d + t0 * 128 + wide]
        v = qkv_ref[:, 2 * d + t0 * 128 : 2 * d + t0 * 128 + wide]
        sc = dot_nt(q, k) * scale
        if size is not None:
            sc = jnp.where(ok, sc, -1e30)
        e = jnp.exp(sc - jnp.max(sc, axis=-1, keepdims=True))
        p = to_low(e * (1.0 / jnp.sum(e, axis=-1, keepdims=True)))
        o = dot_f32(p, v)
        for t in range(t0, t1 + 1):
            part = o[:, (t - t0) * 128 : (t - t0 + 1) * 128]
            full = lane + t * 128
            acc[t] = jnp.where((full >= lo) & (full < hi), part, acc[t]) if t in acc else part
            if min((t + 1) * 128, d) <= hi:
                out[:, t * 128 : (t + 1) * 128] = to_low(acc.pop(t))


def image_attention(tokens, gains, w, clips, length, heads, tn):
    d, n = w.k, w.n

    def body(_s, ins, outs, scr, wb, wait):
        h = to_low(normed(ins[0][...].astype(F32), ins[1][0:1, :]))

        def step(t, c):
            wait(0, t)
            at = pl.ds(pl.multiple_of(t * tn, tn), tn)
            scr[0][:, at] = to_low(dot_f32(h, wb[0][:, at]))
            return c

        lax.fori_loop(0, n // tn, step, 0)
        attend(scr[0], outs[0], d, heads, None)

    m = clips * length
    return run_kernel(
        body, "image_attention", (clips,), [],
        [(tokens, rows_spec(length, d)), (gains, full_spec((3, d)))], [(w, tn)],
        [((m, d), BF16, rows_spec(length, d))], [pltpu.VMEM((length, n), BF16)], 2 * m * d * n,
    )[0]


def audio_attention(patches, w_patch, gains, lengths, w, w_out, clips, length, heads):
    d, n, pk = w.k, w.n, w_patch.shape[0]

    def body(s_refs, ins, outs, _scr, wb, wait):
        x0_ref, h_ref, qkv_ref, mixed_ref, x1_ref, h2_ref = outs
        x0 = dot_f32(ins[0][...], ins[1][...])
        x0_ref[...] = x0
        h = to_low(normed(x0, ins[2][0:1, :]))
        h_ref[...] = h

        def step(t, c):
            wait(0, t)
            at = pl.ds(pl.multiple_of(t * d, d), d)
            qkv_ref[:, at] = to_low(dot_f32(h, wb[0][:, at]))
            return c

        lax.fori_loop(0, n // d, step, 0)
        attend(qkv_ref, mixed_ref, d, heads, s_refs[0][pl.program_id(0)])
        wait(1, 0)
        x1 = x0_ref[...] + dot_f32(mixed_ref[...], wb[1][...])
        x1_ref[...] = x1
        h2_ref[...] = to_low(normed(x1, ins[2][1:2, :]))

    m = clips * length
    rows = rows_spec(length, d)
    return run_kernel(
        body, "audio_attention", (clips,), [lengths],
        [(patches, rows_spec(length, pk)), (w_patch, full_spec((pk, d))), (gains, full_spec((3, d)))],
        [(w, d), (w_out, d)],
        [((m, d), F32, rows), ((m, d), BF16, rows), ((m, n), BF16, rows_spec(length, n)), ((m, d), BF16, rows),
         ((m, d), F32, rows), ((m, d), BF16, rows)],
        [], 2 * m * d * (n + pk + d),
    )


def out_norm(mixed, resid, gains, w, clips, length):
    d = w.n

    def body(_s, ins, outs, _scr, wb, wait):
        wait(0, 0)
        x1 = ins[1][...].astype(F32) + dot_f32(ins[0][...], wb[0][...])
        outs[0][...] = x1
        outs[1][...] = to_low(normed(x1, ins[2][1:2, :]))

    m = clips * length
    outs = [((m, d), F32, rows_spec(length, d)), ((m, d), BF16, rows_spec(length, d))]
    return run_kernel(
        body, "out_norm", (clips,), [],
        [(mixed, rows_spec(length, d)), (resid, rows_spec(length, d)), (gains, full_spec((3, d)))], [(w, d)],
        outs, [], 2 * m * d * d,
    )


def gelu_parts(z):
    zz = z * z
    t = jnp.tanh(GELU_C * z * (1.0 + GELU_A * zz))
    half = 0.5 * (1.0 + t)
    return z * half, half, t, zz


def up_gelu(h_two, w, clips, length, tn, keep):
    d, n = w.k, w.n

    def body(_s, ins, outs, _scr, wb, wait):
        h = ins[0][...]

        def step(t, c):
            wait(0, t)
            at = pl.ds(pl.multiple_of(t * tn, tn), tn)
            z = dot_f32(h, wb[0][:, at])
            u, half, tz, zz = gelu_parts(z)
            outs[0][:, at] = to_low(u)
            if keep:
                slope = half + z * (0.5 * GELU_C) * (1.0 - tz * tz) * (1.0 + (3.0 * GELU_A) * zz)
                outs[1][:, at] = to_low(slope)
            return c

        lax.fori_loop(0, n // tn, step, 0)

    m = clips * length
    outs = [((m, n), BF16, rows_spec(length, n))]
    if keep:
        outs += [((m, n), BF16, rows_spec(length, n))]
    return run_kernel(
        body, "up_gelu", (clips,), [], [(h_two, rows_spec(length, d))], [(w, tn)], outs, [], 2 * m * d * n,
    )


def down_left(hidden, resid, w, clips, length, kt):
    k, n = w.k, w.n

    def body(_s, ins, outs, _scr, wb, wait):
        wait(0, 0)
        outs[0][...] = ins[1][...]

        def step(t, c):
            at = pl.ds(pl.multiple_of(t * kt, kt), kt)
            outs[0][...] += dot_f32(ins[0][:, at], wb[0][at, :])
            return c

        lax.fori_loop(0, k // kt, step, 0)

    m = clips * length
    return run_kernel(
        body, "down_left", (clips,), [], [(hidden, rows_spec(length, k)), (resid, rows_spec(length, n))],
        [(w, n)], [((m, n), F32, rows_spec(length, n))], [], 2 * m * n * k,
    )[0]


def down_embed(hidden, resid, left, gains, lengths, w, w_proj, clips, length, kt, keep):
    d, k, pj, n = resid.shape[1], w.k, w_proj.n, w.n
    have = d - n

    def body(s_refs, ins, outs, scr, wb, wait):
        g = pl.program_id(0)
        wait(0, 0)
        if have:
            scr[0][:, :have] = ins[3][...]
        scr[0][:, have:] = ins[1][:, have:]

        def step(t, c):
            at = pl.ds(pl.multiple_of(t * kt, kt), kt)
            scr[0][:, have:] += dot_f32(ins[0][:, at], wb[0][at, :])
            return c

        lax.fori_loop(0, k // kt, step, 0)
        x2 = scr[0][...]
        size = s_refs[0][g]
        row = lax.broadcasted_iota(jnp.int32, (length, 1), 0)
        weight = jnp.where(row < size, 1.0 / size.astype(F32), 0.0)
        pooled = jnp.sum(normed(x2, ins[2][2:3, :]) * weight, axis=0, keepdims=True)
        scr[1][pl.ds(g, 1), :] = pooled
        if keep:
            outs[3][...] = x2
        wait(1, 0)

        @pl.when(g == clips - 1)
        def _():
            pool_all = scr[1][...]
            raw = dot_f32(to_low(pool_all), wb[1][...])
            outs[0][...] = to_low(unit_rows(raw))
            outs[1][...] = raw
            outs[2][...] = pool_all

    m = clips * length
    outs = [((clips, pj), BF16, full_spec((clips, pj))), ((clips, pj), F32, full_spec((clips, pj))),
            ((clips, d), F32, full_spec((clips, d)))]
    if keep:
        outs += [((m, d), F32, rows_spec(length, d))]
    ins = [(hidden, rows_spec(length, k)), (resid, rows_spec(length, d)), (gains, full_spec((3, d)))]
    if have:
        ins.append((left, rows_spec(length, have)))
    return run_kernel(
        body, "down_embed", (clips,), [lengths], ins, [(w, n), (w_proj, pj)], outs,
        [pltpu.VMEM((length, d), F32), pltpu.VMEM((clips, d), F32)], 2 * m * n * k,
    )


def attn_backward(qkv, d_mixed, lengths, clips, length, heads, first=0, so_far=None):
    d = qkv.shape[1] // 3
    hd = d // heads
    scale = hd ** (-0.5)
    per = 128 // hd

    def body(s_refs, ins, outs, _scr, _wb, _wait):
        qkv_ref, do_ref, out = ins[0], ins[1], outs[0]
        lane = lax.broadcasted_iota(jnp.int32, (1, 128), 1)
        ok = lax.broadcasted_iota(jnp.int32, (length, 1), 0) < s_refs[0][pl.program_id(0) + first]
        for t in range(d // 128):
            at = slice(t * 128, (t + 1) * 128)
            q, do = qkv_ref[:, at], do_ref[:, at]
            k = qkv_ref[:, d + t * 128 : d + (t + 1) * 128]
            v = qkv_ref[:, 2 * d + t * 128 : 2 * d + (t + 1) * 128]
            dq = dk = dv = None
            for h in range(per):
                mine = (lane >= h * hd) & (lane < (h + 1) * hd)
                qm = jnp.where(mine, q, jnp.zeros_like(q))
                dom = jnp.where(mine, do, jnp.zeros_like(do))
                sc = jnp.where(ok, dot_nt(k, qm) * scale, -1e30)
                e = jnp.exp(sc - jnp.max(sc, axis=0, keepdims=True))
                p = e * (1.0 / jnp.sum(e, axis=0, keepdims=True))
                dp = dot_nt(v, dom)
                ds = to_low(p * (dp - jnp.sum(p * dp, axis=0, keepdims=True)))
                dv_h = dot_f32(to_low(p), do)
                dq_h = dot_tn(ds, k)
                dk_h = dot_f32(ds, q)
                dq = dq_h if dq is None else jnp.where(mine, dq_h, dq)
                dk = dk_h if dk is None else jnp.where(mine, dk_h, dk)
                dv = dv_h if dv is None else jnp.where(mine, dv_h, dv)
            out[:, at] = to_low(dq * scale)
            out[:, d + t * 128 : d + (t + 1) * 128] = to_low(dk * scale)
            out[:, 2 * d + t * 128 : 2 * d + (t + 1) * 128] = to_low(dv)

    m = qkv.shape[0]
    rows = lambda n: pl.BlockSpec((length, n), lambda i, *_: (i + first, 0))
    ins = [(qkv, rows(3 * d)), (d_mixed, rows(d))] + ([] if so_far is None else [(so_far, hbm_spec())])
    return run_kernel(
        body, "attn_backward", (clips,), [lengths], ins, [], [((m, 3 * d), BF16, rows(3 * d))], [],
        10 * clips * length * length * 256 * heads, None if so_far is None else 2,
    )[0]


def norm_back(resid, gain, d_out):
    center = resid - jnp.mean(resid, axis=-1, keepdims=True)
    rate = lax.rsqrt(jnp.mean(center * center, axis=-1, keepdims=True) + NORM_EPS)
    unit = center * rate
    d_unit = d_out * gain
    tail = unit * jnp.mean(d_unit * unit, axis=-1, keepdims=True)
    return rate * (d_unit - jnp.mean(d_unit, axis=-1, keepdims=True) - tail), jnp.sum(d_out * unit, axis=0, keepdims=True)


def packed_rows(parts):
    return sum(k // 8 * n // w for k, n, w in parts)


def gradient_outs(parts, fast):
    if not fast:
        return [((k, n), F32, full_spec((k, n))) for k, n, _ in parts]
    shape = (4, packed_rows(parts), parts[0][2])
    return [(shape, BF16, full_spec(shape)), (shape, F32, full_spec(shape))]


def emit_gradients(parts, accs, outs, core, fast):
    if not fast:
        for acc, out in zip(accs, outs):
            out[...] = acc[...]
        return
    for yx in range(4):
        for out, c in ((outs[0], 1 - core), (outs[1], core)):
            at = 0
            for (k, n, width), acc in zip(parts, accs):
                rows = k // 8
                first = pl.multiple_of((2 * yx + c) * rows, rows)
                for j in range(n // width):
                    out[yx, at : at + rows, :] = acc[pl.ds(first, rows), j * width : (j + 1) * width].astype(out.dtype)
                    at += rows
                rest = n % width
                if rest:
                    k2 = width // rest
                    for i in range(k2):
                        sub = rows // k2
                        part = acc[pl.ds(pl.multiple_of(first + i * sub, sub), sub), n - rest : n]
                        out[yx, at : at + sub, i * rest : (i + 1) * rest] = part.astype(out.dtype)
                    at += rows // k2


def contrast_back(joined, embed_raw, first_row, pj, micro, per):
    rows = joined.shape[1]
    row = lax.broadcasted_iota(jnp.int32, (rows, rows), 0)
    col = lax.broadcasted_iota(jnp.int32, (rows, rows), 1)
    same = row == col
    lane = lax.broadcasted_iota(jnp.int32, (rows, 128), 1)
    allowed, count = [], 0.0
    for m in range(micro):
        ids = joined[m, :, 2 * pj :].astype(F32)
        left = jnp.where(lane == 0, ids, jnp.where(lane == 1, 1.0, 0.0))
        right = jnp.where(lane == 0, 1.0, jnp.where(lane == 1, -ids, 0.0))
        allowed.append((dot_nt(to_low(left), to_low(right)) != 0.0) | same)
        count = count + jnp.sum(allowed[m].astype(F32))
    scale = rows / count
    total, d_embed = 0.0, None
    pick_row = lax.broadcasted_iota(jnp.int32, (micro * per, rows), 0)
    pick_col = lax.broadcasted_iota(jnp.int32, (micro * per, rows), 1)
    for m in range(micro):
        image = joined[m, :, pj : 2 * pj]
        logits = dot_nt(joined[m, :, :pj], image) * LOGIT_SCALE
        masked = jnp.where(allowed[m], logits, -1e30)
        row_top, col_top = jnp.max(masked, axis=1, keepdims=True), jnp.max(masked, axis=0, keepdims=True)
        row_lse = row_top + jnp.log(jnp.sum(jnp.exp(masked - row_top), axis=1, keepdims=True))
        col_lse = col_top + jnp.log(jnp.sum(jnp.exp(masked - col_top), axis=0, keepdims=True))
        matched = jnp.sum(jnp.where(same, logits, 0.0))
        total = total + (jnp.sum(row_lse) - matched) + (jnp.sum(col_lse) - matched)
        d_logits = jnp.exp(masked - row_lse) + jnp.exp(masked - col_lse) - jnp.where(same, 2.0, 0.0)
        here = (pick_row >= m * per) & (pick_row < (m + 1) * per) & (pick_col == first_row + pick_row - m * per)
        own = jnp.dot(here.astype(F32), d_logits * (scale * LOGIT_SCALE), precision=HIGHEST, preferred_element_type=F32)
        part = jnp.dot(own, image.astype(F32), precision=HIGHEST, preferred_element_type=F32)
        d_embed = part if d_embed is None else d_embed + part
    rate = lax.rsqrt(jnp.sum(embed_raw * embed_raw, axis=-1, keepdims=True) + NORM_EPS)
    inner = jnp.sum(embed_raw * d_embed, axis=-1, keepdims=True)
    return total * scale, rate * d_embed - embed_raw * (rate * rate * rate * inner)


def down_backward(joined, embed_raw, pooled, resid_out, hidden, slope, gains, lengths, place, w, w_proj, clips, length,
                  fast):
    k, d, pj = w.k, w.n, w_proj.n
    kt = d
    parts = [(k, d, d), (d, pj, d)]

    def body(s_refs, ins, outs, scr, wb, wait):
        g = pl.program_id(0)
        sizes, at = s_refs
        joined_ref, raw_ref, pooled_ref, x2_ref, u_ref, slope_ref, gain_ref = ins
        loss_ref, dpre_ref, dout_ref, g3_ref = outs[:4]
        d_pooled, d_raw_ref, acc = scr
        wait(1, 0)

        @pl.when(g == 0)
        def _():
            loss, d_raw = contrast_back(joined_ref[...], raw_ref[...], at[1], pj, MICRO, clips // MICRO)
            loss_ref[...] = jnp.full((1, 128), loss, F32)
            d_raw_ref[...] = to_low(d_raw)
            d_pooled[...] = dot_nt(to_low(d_raw), wb[1][...])
            acc[...] = jnp.zeros_like(acc)
            g3_ref[...] = jnp.zeros_like(g3_ref)

        size = sizes[g]
        row = lax.broadcasted_iota(jnp.int32, (length, 1), 0)
        weight = jnp.where(row < size, 1.0 / size.astype(F32), 0.0)
        d_out, g_three = norm_back(x2_ref[...], gain_ref[2:3, :], d_pooled[pl.ds(g, 1), :] * weight)
        g3_ref[...] += g_three
        dout_ref[...] = d_out
        d_low = to_low(d_out)
        wait(0, 0)

        def step(t, c):
            cols = pl.ds(pl.multiple_of(t * kt, kt), kt)
            d_hidden = dot_nt(d_low, wb[0][cols, :])
            dpre_ref[:, cols] = to_low(d_hidden * slope_ref[:, cols].astype(F32))
            acc[cols, :] += dot_tn(u_ref[:, cols], d_low)
            return c

        lax.fori_loop(0, k // kt, step, 0)

        @pl.when(g == clips - 1)
        def _():
            g_proj = dot_tn(to_low(pooled_ref[...]), d_raw_ref[...])
            outs[6][...] = g_proj
            emit_gradients(parts, [acc, outs[6]], outs[4:6], at[0], fast)

    m = clips * length
    outs = [((1, 128), F32, full_spec((1, 128))), ((m, k), BF16, rows_spec(length, k)),
            ((m, d), F32, rows_spec(length, d)), ((1, d), F32, full_spec((1, d)))]
    outs += gradient_outs(parts, fast) + [((d, pj), F32, full_spec((d, pj)))]
    ins = [(joined, full_spec(joined.shape)), (embed_raw, full_spec((clips, pj))), (pooled, full_spec((clips, d))),
           (resid_out, rows_spec(length, d)), (hidden, rows_spec(length, k)), (slope, rows_spec(length, k)),
           (gains, full_spec((3, d)))]
    return run_kernel(
        body, "down_backward", (clips,), [lengths, place], ins, [(w, d), (w_proj, pj)], outs,
        [pltpu.VMEM((clips, d), F32), pltpu.VMEM((clips, pj), BF16), pltpu.VMEM((k, d), F32)], 4 * m * d * k,
    )


def up_backward(d_pre, h_two, resid_mid, d_out, mixed, gains, place, w, w_out, clips, length, kt, fast):
    d, n = w.k, w.n
    parts = [(d, n, d), (d, d, d)]

    def body(s_refs, ins, outs, scr, wb, wait):
        g = pl.program_id(0)
        (at,) = s_refs
        dpre_ref, h_ref, x1_ref, dout_ref, o_ref, gain_ref = ins
        dmid_ref, dmix_ref, g2_ref = outs[:3]
        acc, acc_out, back = scr

        @pl.when(g == 0)
        def _():
            acc[...] = jnp.zeros_like(acc)
            acc_out[...] = jnp.zeros_like(acc_out)
            g2_ref[...] = jnp.zeros_like(g2_ref)

        h = h_ref[...]
        back[...] = jnp.zeros_like(back)

        def step(t, c):
            cols = pl.ds(pl.multiple_of(t * kt, kt), kt)
            wait(0, t)
            dp = dpre_ref[:, cols]
            acc[:, cols] += dot_tn(h, dp)
            back[...] += dot_nt(dp, wb[0][:, cols])
            return c

        lax.fori_loop(0, n // kt, step, 0)
        d_ln, g_two = norm_back(x1_ref[...], gain_ref[1:2, :], back[...])
        g2_ref[...] += g_two
        d_mid = dout_ref[...] + d_ln
        dmid_ref[...] = d_mid
        d_low = to_low(d_mid)
        wait(1, 0)
        acc_out[...] += dot_tn(o_ref[...], d_low)
        dmix_ref[...] = to_low(dot_nt(d_low, wb[1][...]))

        @pl.when(g == clips - 1)
        def _():
            emit_gradients(parts, [acc, acc_out], outs[3:5], at[0], fast)

    m = clips * length
    rows = rows_spec(length, d)
    outs = [((m, d), F32, rows), ((m, d), BF16, rows), ((1, d), F32, full_spec((1, d)))] + gradient_outs(parts, fast)
    ins = [(d_pre, rows_spec(length, n)), (h_two, rows), (resid_mid, rows), (d_out, rows), (mixed, rows),
           (gains, full_spec((3, d)))]
    return run_kernel(
        body, "up_backward", (clips,), [place], ins, [(w, kt), (w_out, d)], outs,
        [pltpu.VMEM((d, n), F32), pltpu.VMEM((d, d), F32), pltpu.VMEM((length, d), F32)], 4 * m * d * (n + d),
    )


def qkv_backward(d_qkv, h_one, resid_in, d_mid, patches, gains, g_two, g_three, place, w, clips, length, fast):
    d, n, pk = w.k, w.n, patches.shape[1]
    parts = [(d, n, d), (pk, d, d)]
    extra = 16

    def body(s_refs, ins, outs, scr, wb, wait):
        g = pl.program_id(0)
        (at,) = s_refs
        dqkv_ref, h_ref, x0_ref, dmid_ref, patch_ref, gain_ref, g2_ref, g3_ref = ins
        acc, acc_patch, back, acc_gain = scr

        @pl.when(g == 0)
        def _():
            acc[...] = jnp.zeros_like(acc)
            acc_patch[...] = jnp.zeros_like(acc_patch)
            acc_gain[...] = jnp.zeros_like(acc_gain)
            acc_gain[1:2, :] = g2_ref[...]
            acc_gain[2:3, :] = g3_ref[...]

        h = h_ref[...]
        back[...] = jnp.zeros_like(back)

        def step(t, c):
            cols = pl.ds(pl.multiple_of(t * d, d), d)
            wait(0, t)
            dq = dqkv_ref[:, cols]
            acc[:, cols] += dot_tn(h, dq)
            back[...] += dot_nt(dq, wb[0][:, cols])
            return c

        lax.fori_loop(0, n // d, step, 0)
        d_ln, g_one = norm_back(x0_ref[...], gain_ref[0:1, :], back[...])
        acc_gain[0:1, :] += g_one
        acc_patch[...] += dot_tn(patch_ref[...], to_low(dmid_ref[...] + d_ln))

        @pl.when(g == clips - 1)
        def _():
            emit_gradients(parts, [acc, acc_patch], outs[:2], at[0], fast)
            if fast:
                rows = packed_rows(parts)
                for yx in range(4):
                    for out in outs[:2]:
                        out[yx, rows : rows + extra, :] = acc_gain[...].astype(out.dtype)
            else:
                outs[2][...] = acc_gain[...]

    m = clips * length
    rows = rows_spec(length, d)
    if fast:
        shape = (4, packed_rows(parts) + extra, d)
        outs = [(shape, BF16, full_spec(shape)), (shape, F32, full_spec(shape))]
    else:
        outs = gradient_outs(parts, fast) + [((extra, d), F32, full_spec((extra, d)))]
    ins = [(d_qkv, rows_spec(length, n)), (h_one, rows), (resid_in, rows), (d_mid, rows),
           (patches, rows_spec(length, pk)), (gains, full_spec((3, d))), (g_two, full_spec((1, d))),
           (g_three, full_spec((1, d)))]
    return run_kernel(
        body, "qkv_backward", (clips,), [place], ins, [(w, d)], outs,
        [pltpu.VMEM((d, n), F32), pltpu.VMEM((pk, d), F32), pltpu.VMEM((length, d), F32), pltpu.VMEM((extra, d), F32)],
        4 * m * d * n,
    )


AXES = ("dp", "rep")


def joint_perm(reps, fn):
    out = []
    for dp in range(8):
        for z in range(reps):
            dst = fn(dp, z)
            if dst is not None:
                out.append((dp * reps + z, dst[0] * reps + dst[1]))
    return out


def send(value, reps, fn):
    return lax.ppermute(value, AXES, joint_perm(reps, fn))


class Ring:
    def __init__(self, packed, col, width, reps):
        self.own, self.col, self.width, self.reps = packed, col, width, reps
        self.mine = packed[:, col : col + width]

    def first(self):
        self.near = send(self.mine, self.reps, lambda dp, z: (dp ^ (2 if z % 2 == 0 else 4), z))

    def second(self):
        self.diag = send(self.near, self.reps, lambda dp, z: (dp ^ (4 if z % 2 == 0 else 2), z))
        self.other = send(self.near, self.reps, lambda dp, z: (dp, z ^ 1))

    def twin(self, *names):
        for name in names:
            setattr(self, name + "_twin", send(getattr(self, name), self.reps, lambda dp, z: (dp ^ 1, z)))

    def group(self, own_twin):
        odd = lax.axis_index("rep") % 2 == 1
        x, y = jnp.int32(2), jnp.int32(4)
        flip = jnp.stack([jnp.int32(0), jnp.where(odd, y, x), jnp.int32(6), jnp.where(odd, x, y)])
        base = jnp.bitwise_xor(flip, lax.axis_index("dp").astype(jnp.int32))
        arrays = [self.own, self.near, self.diag, self.other, own_twin, self.near_twin, self.diag_twin, self.other_twin]
        index = jnp.concatenate([base, jnp.bitwise_xor(base, 1)])
        return Group(arrays, index, self.own.shape[0], (self.col, 0, 0, 0) * 2)


def fence(held, values):
    flat = [(r, n) for r, names in held for n in names.split()]
    out = lax.optimization_barrier(tuple(getattr(r, n) for r, n in flat) + tuple(values))
    for (r, n), v in zip(flat, out):
        setattr(r, n, v)
    return out[len(flat) :]


def take(v, i, axis):
    return lax.dynamic_index_in_dim(v, i, axis, keepdims=False)


def from_width(v, rows, n):
    width = v.shape[-1]
    full = n // width
    blocks = [v[i * rows : (i + 1) * rows] for i in range(full)]
    rest = n % width
    if rest:
        last, k = v[full * rows :], width // rest
        blocks.append(jnp.concatenate([last[:, i * rest : (i + 1) * rest] for i in range(k)], axis=0))
    return jnp.concatenate(blocks, axis=1)


class Sum:
    def __init__(self, leave, stay, parts, reps):
        self.reps, self.leave, self.stay, self.parts = reps, leave, stay, parts
        me = lax.axis_index("dp")
        self.y, self.x = me // 4, (me // 2) % 2
        self.odd = lax.axis_index("rep") % 2 == 1

    def hops(self, *pairs):
        self.due = [(to_low(v), fn) for v, fn in pairs]

    def core(self):
        self.hops((self.leave, lambda dp, z: (dp ^ 1, z)))

    def plane(self):
        s = (self.stay + self.got[0].astype(F32)).reshape((2, 2) + self.stay.shape[1:])
        half = s.shape[-2] // 2
        self.a, self.b = s[:, :, :half], s[:, :, half:]
        self.hops((take(self.a, 1 - self.x, 1), lambda dp, z: (dp ^ 2, z)),
                  (take(self.b, 1 - self.y, 0), lambda dp, z: (dp ^ 4, z)))

    def plane_again(self):
        self.a = take(self.a, self.x, 1) + self.got[0].astype(F32)
        self.b = take(self.b, self.y, 0) + self.got[1].astype(F32)
        self.hops((take(self.a, 1 - self.y, 0), lambda dp, z: (dp ^ 4, z)),
                  (take(self.b, 1 - self.x, 0), lambda dp, z: (dp ^ 2, z)))

    def pair(self):
        a = take(self.a, self.y, 0) + self.got[0].astype(F32)
        b = take(self.b, self.x, 0) + self.got[1].astype(F32)
        self.a = jnp.where(self.odd, b, a)
        self.hops((jnp.where(self.odd, a, b), lambda dp, z: (dp, z ^ 1)))

    def across(self):
        self.a = to_low(self.a + self.got[0].astype(F32))
        self.hops((self.a, lambda dp, z: (dp, z ^ 2)))

    def share(self):
        self.a = to_low(self.a.astype(F32) + self.got[0].astype(F32))
        self.hops((self.a, lambda dp, z: (dp, z ^ 1)))

    def result(self):
        other = self.got[0]
        total = jnp.concatenate([jnp.where(self.odd, other, self.a), jnp.where(self.odd, self.a, other)], axis=0)
        total, out, at = total.astype(F32), [], 0
        for k, n, width in self.parts:
            rows = k // 8
            size = rows * n // width
            out.append(from_width(total[at : at + size], rows, n))
            at += size
        return out


def go(sums, *values):
    flat = [v for s in sums for v, _ in s.due]
    out = lax.optimization_barrier(tuple(flat) + values)
    at = 0
    for s in sums:
        s.got = tuple(send(out[at + i], s.reps, fn) for i, (_, fn) in enumerate(s.due))
        at += len(s.due)
    return out[at:]


def order(sums, *values):
    flat = [g for s in sums for g in s.got]
    out = lax.optimization_barrier(tuple(flat) + values)
    at = 0
    for s in sums:
        s.got = out[at : at + len(s.got)]
        at += len(s.got)
    return out[at:]


def adam_step(weight, gradient, moment_one, moment_two, step_rate, decay):
    first_new = BETA_ONE * moment_one + (1.0 - BETA_ONE) * gradient
    second_new = BETA_TWO * moment_two + (1.0 - BETA_TWO) * gradient * gradient
    fixed_one = first_new / (1.0 - BETA_ONE**STEP)
    fixed_two = second_new / (1.0 - BETA_TWO**STEP)
    update = fixed_one / (jnp.sqrt(fixed_two) + ADAM_EPS) + decay * weight
    return (weight - step_rate * update, first_new, second_new)


def as_columns(v, rows):
    return jnp.concatenate([v[i * rows : (i + 1) * rows] for i in range(v.shape[0] // rows)], axis=1)


def local(dp_size, rep_size, *args):
    (audio_patches, clip_lengths, video_ids, image_tokens, i_qkv, i_out, i_up, i_down, i_proj, i_gains) = args[:10]
    masters, firsts_in, seconds_in = args[10:17], args[17:24], args[24:31]
    a_patch, a_qkv, a_out, a_up, a_down, a_proj, a_gains = (to_low(w) for w in masters)
    fast = dp_size == 8 and rep_size == 4
    clip_dev = audio_patches.shape[1]
    clips = MICRO * clip_dev
    d_i, d_a, ff_a, pj = i_out.shape[1], a_out.shape[1], a_up.shape[1], a_proj.shape[1]
    ff_i = i_up.shape[1]

    rp = a_patch.shape[0]
    small = jnp.concatenate(
        [a_patch, jnp.pad(a_gains.reshape(1, -1), ((0, 0), (0, d_a - a_gains.size))),
         jnp.pad(i_gains.reshape(1, -1), ((0, 0), (0, d_a - i_gains.size)))], axis=0)
    small = lax.all_gather(small, "dp", axis=0)
    img_sizes = jnp.full((clips,), IMG_LEN, jnp.int32)
    tokens = image_tokens.reshape(clips * IMG_LEN, d_i)
    sizes = clip_lengths.reshape(clips)
    patches = jnp.pad(audio_patches.reshape(clips, LEN, -1), ((0, 0), (0, PAD_LEN - LEN), (0, 0)))
    patches = patches.reshape(clips * PAD_LEN, -1)
    half, sub_i, sub_a = ff_i // 2, ff_i // d_i, ff_a // d_a
    dl = d_i * 3 // 5
    if fast:
        down_a = as_columns(a_down, a_qkv.shape[0])
        own_a = jnp.concatenate([a_qkv, a_out, a_up, down_a, a_proj], axis=1)
        small, own_a, i_qkv, i_out, i_up, i_down, i_proj = lax.optimization_barrier(
            (small, own_a, i_qkv, i_out, i_up, i_down, i_proj))
        down_i = as_columns(i_down, i_qkv.shape[0])
        left = [down_i[:, j * d_i : j * d_i + dl] for j in range(sub_i)]
        right = [down_i[:, j * d_i + dl : (j + 1) * d_i] for j in range(sub_i)]
        own_i = jnp.concatenate([i_qkv, i_out, i_up, i_proj] + left + right, axis=1)
        cut_a = 4 * d_a
        ca = Ring(own_a, 0, cut_a, rep_size), Ring(own_a, cut_a, own_a.shape[1] - cut_a, rep_size)
        widths, at, ci = [3 * d_i, d_i + half, half + pj, sub_i * dl, sub_i * (d_i - dl)], 0, []
        for wd in widths:
            ci.append(Ring(own_i, at, wd, rep_size))
            at += wd
        swap = lambda v: send(v, rep_size, lambda dp, z: (dp ^ 1, z))
        twin_a = swap(own_a)

        ca[0].first()
        (own_i,) = fence([(ca[0], "near"), (ca[1], "mine")] + [(c, "mine") for c in ci], (own_i,))
        ca[0].second()
        ca[0].twin("near")
        ca[1].first()
        patches, twin_a = fence([(ca[0], "diag other near_twin"), (ca[1], "near"), (ci[0], "mine")], (patches, twin_a))
        ca[0].twin("diag", "other")
        ca[1].second()
        ca[1].twin("near")
        ci[0].first()
        ga0 = ca[0].group(twin_a)
        wa_qkv = Weight(d_a, 3 * d_a, [(ga0, 0, 3 * d_a, 0, 0)])
        wa_out = Weight(d_a, d_a, [(ga0, 3 * d_a, d_a, 0, 0)])
    else:
        whole = lambda v: lax.all_gather(v, "dp", axis=0, tiled=True)
        make = lambda v: Weight(v.shape[0] * dp_size, v.shape[1], whole=whole(v))
        cut = lambda v: Weight(v.shape[0], v.shape[1], whole=v)
        wi_qkv, wi_out, wi_up, wi_proj = (make(v) for v in (i_qkv, i_out, i_up, i_proj))
        wi_left, wi_right = cut(whole(i_down)[:, :dl]), cut(whole(i_down)[:, dl:])
        wa_qkv, wa_out, wa_up, wa_down, wa_proj = (make(v) for v in (a_qkv, a_out, a_up, a_down, a_proj))

    w_patch = small[:, :rp].reshape(rp * dp_size, d_a)
    unpack = lambda v, g: v[:, : g.size].reshape(dp_size, 3, -1).transpose(1, 0, 2).reshape(3, -1).astype(F32)
    gains_a, gains_i = unpack(small[:, rp], a_gains), unpack(small[:, rp + 1], i_gains)

    resid_in, h_one, qkv, mixed, resid_mid, h_two = audio_attention(
        patches, w_patch, gains_a, sizes, wa_qkv, wa_out, clips, PAD_LEN, HEADS_A)

    if fast:
        (h_two,) = fence([(ca[1], "diag other near_twin"), (ci[0], "near"), (ci[1], "mine")], (h_two,))
        ca[1].twin("diag", "other")
        ci[0].second()
        ci[0].twin("near")
        ci[1].first()
        twin_i = swap(own_i)
        ga1 = ca[1].group(twin_a)
        wa_up = Weight(d_a, ff_a, [(ga1, 0, ff_a, 0, 0)])
        wa_down = Weight(ff_a, d_a, [(ga1, ff_a + j * d_a, d_a, 0, j) for j in range(sub_a)], sub=sub_a)
        wa_proj = Weight(d_a, pj, [(ga1, 2 * ff_a, pj, 0, 0)])
    got = up_gelu(h_two, wa_up, clips, PAD_LEN, 1024, True)
    hidden, slope = got[:2]

    if fast:
        hidden, tokens, twin_i = fence(
            [(ci[0], "diag other near_twin"), (ci[1], "near"), (ci[2], "mine")], (hidden, tokens, twin_i))
        ci[0].twin("diag", "other")
        ci[1].second()
        ci[1].twin("near")
        ci[2].first()
        gi = [ci[0].group(twin_i)]
        wi_qkv = Weight(d_i, 3 * d_i, [(gi[0], 0, 3 * d_i, 0, 0)])
    mixed_i = image_attention(tokens, gains_i, wi_qkv, clips, IMG_LEN, HEADS_I, d_i)

    if fast:
        mixed_i, hidden = fence(
            [(ci[1], "diag other near_twin"), (ci[2], "near"), (ci[3], "mine")], (mixed_i, hidden))
        ci[1].twin("diag", "other")
        ci[2].second()
        ci[2].twin("near")
        ci[3].first()
        gi.append(ci[1].group(twin_i))
        wi_out = Weight(d_i, d_i, [(gi[1], 0, d_i, 0, 0)])
    got = down_embed(hidden, resid_mid, None, gains_a, sizes, wa_down, wa_proj, clips, PAD_LEN, d_a, True)
    aud_emb, embed_raw, pooled, resid_out = got[:4]
    mid_i, h_two_i = out_norm(mixed_i, tokens, gains_i, wi_out, clips, IMG_LEN)

    if fast:
        h_two_i, aud_emb = fence(
            [(ci[2], "diag other near_twin"), (ci[3], "near"), (ci[4], "mine")], (h_two_i, aud_emb))
        ci[2].twin("diag", "other")
        ci[3].second()
        ci[3].twin("near")
        ci[4].first()
        gi.append(ci[2].group(twin_i))
        wi_up = Weight(d_i, ff_i, [(gi[1], d_i, half, 0, 0), (gi[2], 0, half, half, 0)])
        wi_proj = Weight(d_i, pj, [(gi[2], half, pj, 0, 0)])
    hidden_i = up_gelu(h_two_i, wi_up, clips, IMG_LEN, d_i, False)[0]

    if fast:
        (hidden_i,) = fence([(ci[3], "diag other near_twin"), (ci[4], "near")], (hidden_i,))
        ci[3].twin("diag", "other")
        ci[4].second()
        ci[4].twin("near")
        gi.append(ci[3].group(twin_i))
        wi_left = Weight(ff_i, dl, [(gi[3], j * dl, dl, 0, j) for j in range(sub_i)], sub=sub_i)
    left_i = down_left(hidden_i, mid_i, wi_left, clips, IMG_LEN, d_i)

    if fast:
        (left_i,) = fence([(ci[4], "diag other near_twin")], (left_i,))
        ci[4].twin("diag", "other")
        gi.append(ci[4].group(twin_i))
        dr = d_i - dl
        wi_right = Weight(ff_i, dr, [(gi[4], j * dr, dr, 0, j) for j in range(sub_i)], sub=sub_i)
    img_emb = down_embed(hidden_i, mid_i, left_i, gains_i, img_sizes, wi_right, wi_proj, clips, IMG_LEN, d_i, False)[0]

    ids_low = jnp.broadcast_to(to_low(video_ids.reshape(clips, 1)), (clips, 128))
    joined = jnp.concatenate([aud_emb, img_emb, ids_low], axis=1).reshape(MICRO, clip_dev, 2 * pj + 128)
    joined = lax.all_gather(lax.all_gather(joined, "rep", axis=1, tiled=True), "dp", axis=1, tiled=True)
    me = lax.axis_index("dp").astype(jnp.int32)
    first_row = lax.axis_index(AXES).astype(jnp.int32) * clip_dev
    place = jnp.stack([me % 2, first_row])
    got = down_backward(joined, embed_raw, pooled, resid_out, hidden, slope, gains_a, sizes, place, wa_down, wa_proj,
                        clips, PAD_LEN, fast)
    loss, d_pre, d_out, g_three = got[0][0, 0], *got[1:4]
    if fast:
        s_down = Sum(got[4], got[5], [(ff_a, d_a, d_a), (d_a, pj, d_a)], rep_size)
        s_down.core()
        (d_pre,) = go([s_down], d_pre)
    up = up_backward(d_pre, h_two, resid_mid, d_out, mixed, gains_a, place, wa_up, wa_out, clips, PAD_LEN, 1024, fast)
    d_mid, d_mixed, g_two = up[:3]
    if fast:
        (d_mixed,) = order([s_down], d_mixed)
        s_down.plane()
        s_up = Sum(up[3], up[4], [(d_a, ff_a, d_a), (d_a, d_a, d_a)], rep_size)
        s_up.core()
        (d_mixed,) = go([s_down, s_up], d_mixed)
    d_qkv = attn_backward(qkv, d_mixed, sizes, clip_dev, PAD_LEN, HEADS_A)
    if fast:
        d_qkv, d_mixed = order([s_down, s_up], d_qkv, d_mixed)
        s_down.plane_again()
        s_up.plane()
        d_qkv, d_mixed = go([s_down, s_up], d_qkv, d_mixed)
    d_qkv = attn_backward(qkv, d_mixed, sizes, clips - clip_dev, PAD_LEN, HEADS_A, clip_dev, d_qkv)
    if fast:
        (d_qkv,) = order([s_down, s_up], d_qkv)
        s_down.pair()
        s_up.plane_again()
        (d_qkv,) = go([s_down, s_up], d_qkv)
    last = qkv_backward(d_qkv, h_one, resid_in, d_mid, patches, gains_a, g_two, g_three, place, wa_qkv, clips, PAD_LEN,
                        fast)
    share = d_a // dp_size
    mine = lambda v: lax.dynamic_slice_in_dim(v[:3], me * share, share, 1)
    if fast:
        leave, stay = order([s_down, s_up], last[0], last[1])
        s_qkv = Sum(leave, stay, [(d_a, 3 * d_a, d_a), (w_patch.shape[0], d_a, d_a), (128, d_a, d_a)], rep_size)
        s_qkv.core()
        s_down.across()
        s_up.pair()
        go([s_qkv, s_down, s_up])
        order([s_qkv])
        s_qkv.plane()
        go([s_qkv])
        order([s_down, s_up])
        s_up.across()
        s_down.share()
        go([s_up, s_down])
        order([s_qkv])
        s_qkv.plane_again()
        go([s_qkv])
        order([s_qkv, s_up])
        s_qkv.pair()
        s_up.share()
        go([s_qkv, s_up])
        order([s_qkv])
        s_qkv.across()
        go([s_qkv])
        s_qkv.share()
        go([s_qkv])
        r_down, r_proj = s_down.result()
        r_up, r_out = s_up.result()
        r_qkv, r_patch, r_gain = s_qkv.result()
        summed = [r_patch, r_qkv, r_out, r_up, r_down, r_proj, mine(r_gain)]
    else:
        grads = (last[1], last[0], up[4], up[3], got[4], got[5])
        summed = [lax.psum(lax.psum_scatter(v, "dp", scatter_dimension=0, tiled=True), "rep") for v in grads]
        summed.append(mine(lax.psum(last[2], AXES)))
    local_squares = sum(jnp.sum(v * v) for v in summed)
    grad_norm = jnp.sqrt(lax.psum(local_squares, "dp"))
    factor = jnp.minimum(1.0, CLIP_NORM / grad_norm)
    results = []
    for index in range(7):
        step_rate = RATE_GAIN if index == 6 else RATE_MATRIX
        decay = 0.0 if index == 6 else WEIGHT_DECAY
        results.append(
            adam_step(masters[index], summed[index] * factor, firsts_in[index], seconds_in[index], step_rate, decay)
        )
    return (loss, grad_norm, *(r[0] for r in results), *(r[1] for r in results), *(r[2] for r in results))


def solution(mesh):
    batch4 = P(None, AXES, None, None)
    batch2 = P(None, AXES)
    split = P("dp", None)
    gain = P(None, "dp")
    weights = (split,) * 6 + (gain,)
    placed = (batch4, batch2, batch2, batch4) + (split,) * 5 + (gain,) + weights * 3
    return jax.shard_map(
        functools.partial(local, mesh.shape["dp"], mesh.shape["rep"]),
        mesh=mesh,
        in_specs=placed,
        out_specs=(P(), P()) + weights * 3,
        check_vma=False,
    )
```

```python
import functools

import jax
import jax.numpy as jnp
from jax import lax
from jax.experimental import pallas as pl
from jax.experimental.pallas import tpu as pltpu
from jax.sharding import PartitionSpec as P

HEADS_A = 12
HEADS_I = 16
LEN = 228
IMG_LEN = 256
MICRO = 2
STEP = 7

HIGHEST = lax.Precision.HIGHEST
F32 = jnp.float32
BF16 = jnp.bfloat16
NORM_EPS = 1e-06
LOGIT_SCALE = 50.0
CLIP_NORM = 0.01
BETA_ONE = 0.9
BETA_TWO = 0.999
ADAM_EPS = 1e-08
WEIGHT_DECAY = 0.1
RATE_MATRIX = 0.05
RATE_GAIN = 0.3
PAD_LEN = 240
GELU_C = 0.7978845608028654
GELU_A = 0.044715
VMEM_GRANT = 60 << 20


def to_low(v):
    return v.astype(BF16)


def normed(resid, gain):
    center = resid - jnp.mean(resid, axis=-1, keepdims=True)
    spread = jnp.mean(center * center, axis=-1, keepdims=True)
    return center * lax.rsqrt(spread + NORM_EPS) * gain


def unit_rows(embed_raw):
    return embed_raw * lax.rsqrt(jnp.sum(embed_raw * embed_raw, axis=-1, keepdims=True) + NORM_EPS)


def dot_f32(a, b):
    return lax.dot_general(a, b, (((1,), (0,)), ((), ())), preferred_element_type=F32)


def dot_nt(a, b):
    return lax.dot_general(a, b, (((1,), (1,)), ((), ())), preferred_element_type=F32)


def dot_tn(a, b):
    return lax.dot_general(a, b, (((0,), (0,)), ((), ())), preferred_element_type=F32)


class Group:
    def __init__(self, arrays, index, rows, cols):
        self.arrays, self.index, self.rows, self.cols = arrays, index, rows, cols


class Weight:
    def __init__(self, k, n, segs=None, sub=1, whole=None):
        self.k, self.n, self.segs, self.sub, self.whole = k, n, segs, sub, whole

    def groups(self):
        seen = []
        for seg in self.segs:
            if seg[0] not in seen:
                seen.append(seg[0])
        return seen

    def operands(self):
        if self.whole is not None:
            return [self.whole]
        return [v for g in self.groups() for v in g.arrays]

    def indices(self):
        return [] if self.whole is not None else [g.index for g in self.groups()]

    def entries(self, tn):
        groups, out = self.groups(), []
        for g, col, width, dst, part in self.segs:
            assert width % tn == 0
            out += [(groups.index(g), col + t * tn, dst + t * tn, part) for t in range(width // tn)]
        return sorted(out, key=lambda e: (e[2], e[3]))


def start_weight(w, tn, refs, idx, wbuf, sem):
    if w.whole is not None:
        for t in range(w.n // tn):
            cols = pl.ds(t * tn, tn)
            pltpu.make_async_copy(refs[0].at[:, cols], wbuf.at[:, cols], sem.at[t, 0]).start()
        return
    for e, (gi, col, dst, part) in enumerate(w.entries(tn)):
        rows = w.groups()[gi].rows
        for p in range(8):
            at = pl.multiple_of(idx[gi][p] * (rows * w.sub) + part * rows, rows)
            pltpu.make_async_copy(
                refs[8 * gi + p].at[:, pl.ds(w.groups()[gi].cols[p] + col, tn)],
                wbuf.at[pl.ds(at, rows), pl.ds(dst, tn)],
                sem.at[e, p],
            ).start()


def wait_weight(w, tn, refs, idx, wbuf, sem, t):
    cols = pl.ds(pl.multiple_of(t * tn, tn), tn)
    if w.whole is not None:
        pltpu.make_async_copy(refs[0].at[:, pl.ds(0, tn)], wbuf.at[:, cols], sem.at[t, 0]).wait()
        return
    rows = w.groups()[0].rows
    for part in range(w.sub):
        for p in range(8):
            pltpu.make_async_copy(
                refs[p].at[:, pl.ds(0, tn)], wbuf.at[pl.ds((p * w.sub + part) * rows, rows), cols],
                sem.at[t * w.sub + part, p],
            ).wait()


def weight_sems(w, tn):
    tiles = w.n // tn
    return pltpu.SemaphoreType.DMA((tiles, 1) if w.whole is not None else (tiles * w.sub, 8))


HBM = pltpu.MemorySpace.HBM


def hbm_spec():
    return pl.BlockSpec(memory_space=HBM)


def full_spec(shape):
    return pl.BlockSpec(shape, lambda *_: (0,) * len(shape))


def run_kernel(body, name, grid, scalars, ins, weights, outs, scratch, flops, alias=None):
    scal = list(scalars)
    for w, _ in weights:
        scal += w.indices()
    n_scal, n_user = len(scal), len(scalars)
    operands = [a for a, _ in ins]
    specs = [s for _, s in ins]
    for w, _ in weights:
        ops = w.operands()
        operands += ops
        specs += [hbm_spec()] * len(ops)
    n_in = len(ins)
    scr = list(scratch)
    for w, tn in weights:
        scr += [pltpu.VMEM((w.k, w.n), BF16), weight_sems(w, tn)]

    def kernel(*refs):
        s = refs[:n_scal]
        user_s, s = s[:n_user], s[n_user:]
        pos = n_scal
        in_refs = refs[pos : pos + n_in]
        pos += n_in
        w_refs = []
        for w, _ in weights:
            m = len(w.operands())
            w_refs.append(refs[pos : pos + m])
            pos += m
        out_refs = refs[pos : pos + len(outs)]
        pos += len(outs)
        scr_refs = refs[pos : pos + len(scratch)]
        pos += len(scratch)
        handles = []
        si = 0
        for wi, (w, tn) in enumerate(weights):
            gi = len(w.indices())
            handles.append((w, tn, w_refs[wi], s[si : si + gi], refs[pos], refs[pos + 1]))
            si += gi
            pos += 2
        first = pl.program_id(0) == 0

        @pl.when(first)
        def _():
            for h in handles:
                start_weight(*h)

        def wait(k, t):
            @pl.when(first)
            def _():
                wait_weight(*handles[k], t)

        body(user_s, in_refs, out_refs, scr_refs, [h[4] for h in handles], wait)

    bytes_acc = sum(int(a.size) * a.dtype.itemsize for a in operands) + sum(
        functools.reduce(lambda x, y: x * y, o[0], 1) * jnp.dtype(o[1]).itemsize for o in outs
    )
    return pl.pallas_call(
        kernel,
        grid_spec=pltpu.PrefetchScalarGridSpec(
            num_scalar_prefetch=n_scal,
            grid=grid,
            in_specs=specs,
            out_specs=[o[2] for o in outs],
            scratch_shapes=scr,
        ),
        out_shape=[jax.ShapeDtypeStruct(o[0], o[1]) for o in outs],
        input_output_aliases={} if alias is None else {n_scal + alias: 0},
        compiler_params=pltpu.CompilerParams(vmem_limit_bytes=VMEM_GRANT),
        cost_estimate=pl.CostEstimate(flops=flops, bytes_accessed=bytes_acc, transcendentals=0),
        name=name,
    )(*scal, *operands)


def rows_spec(length, width):
    return pl.BlockSpec((length, width), lambda i, *_: (i, 0))


def attend(qkv_ref, out, d, heads, size):
    length = qkv_ref.shape[0]
    hd = d // heads
    scale = hd ** (-0.5)
    lane = lax.broadcasted_iota(jnp.int32, (1, 128), 1)
    if size is not None:
        ok = lax.broadcasted_iota(jnp.int32, (1, length), 1) < size
    acc = {}
    for h in range(heads):
        lo, hi = h * hd, (h + 1) * hd
        t0, t1 = lo // 128, (hi - 1) // 128
        wide = (t1 - t0 + 1) * 128
        col = lax.broadcasted_iota(jnp.int32, (1, wide), 1) + t0 * 128
        q = qkv_ref[:, t0 * 128 : t0 * 128 + wide]
        q = jnp.where((col >= lo) & (col < hi), q, jnp.zeros_like(q))
        k = qkv_ref[:, d + t0 * 128 : d + t0 * 128 + wide]
        v = qkv_ref[:, 2 * d + t0 * 128 : 2 * d + t0 * 128 + wide]
        sc = dot_nt(q, k) * scale
        if size is not None:
            sc = jnp.where(ok, sc, -1e30)
        e = jnp.exp(sc - jnp.max(sc, axis=-1, keepdims=True))
        p = to_low(e * (1.0 / jnp.sum(e, axis=-1, keepdims=True)))
        o = dot_f32(p, v)
        for t in range(t0, t1 + 1):
            part = o[:, (t - t0) * 128 : (t - t0 + 1) * 128]
            full = lane + t * 128
            acc[t] = jnp.where((full >= lo) & (full < hi), part, acc[t]) if t in acc else part
            if min((t + 1) * 128, d) <= hi:
                out[:, t * 128 : (t + 1) * 128] = to_low(acc.pop(t))


def image_attention(tokens, gains, w, clips, length, heads, tn):
    d, n = w.k, w.n

    def body(_s, ins, outs, scr, wb, wait):
        h = to_low(normed(ins[0][...].astype(F32), ins[1][0:1, :]))

        def step(t, c):
            wait(0, t)
            at = pl.ds(pl.multiple_of(t * tn, tn), tn)
            scr[0][:, at] = to_low(dot_f32(h, wb[0][:, at]))
            return c

        lax.fori_loop(0, n // tn, step, 0)
        attend(scr[0], outs[0], d, heads, None)

    m = clips * length
    return run_kernel(
        body, "image_attention", (clips,), [],
        [(tokens, rows_spec(length, d)), (gains, full_spec((3, d)))], [(w, tn)],
        [((m, d), BF16, rows_spec(length, d))], [pltpu.VMEM((length, n), BF16)], 2 * m * d * n,
    )[0]


def audio_attention(patches, w_patch, gains, lengths, w, w_out, clips, length, heads):
    d, n, pk = w.k, w.n, w_patch.shape[0]

    def body(s_refs, ins, outs, _scr, wb, wait):
        x0_ref, h_ref, qkv_ref, mixed_ref, x1_ref, h2_ref = outs
        x0 = dot_f32(ins[0][...], ins[1][...])
        x0_ref[...] = x0
        h = to_low(normed(x0, ins[2][0:1, :]))
        h_ref[...] = h

        def step(t, c):
            wait(0, t)
            at = pl.ds(pl.multiple_of(t * d, d), d)
            qkv_ref[:, at] = to_low(dot_f32(h, wb[0][:, at]))
            return c

        lax.fori_loop(0, n // d, step, 0)
        attend(qkv_ref, mixed_ref, d, heads, s_refs[0][pl.program_id(0)])
        wait(1, 0)
        x1 = x0_ref[...] + dot_f32(mixed_ref[...], wb[1][...])
        x1_ref[...] = x1
        h2_ref[...] = to_low(normed(x1, ins[2][1:2, :]))

    m = clips * length
    rows = rows_spec(length, d)
    return run_kernel(
        body, "audio_attention", (clips,), [lengths],
        [(patches, rows_spec(length, pk)), (w_patch, full_spec((pk, d))), (gains, full_spec((3, d)))],
        [(w, d), (w_out, d)],
        [((m, d), F32, rows), ((m, d), BF16, rows), ((m, n), BF16, rows_spec(length, n)), ((m, d), BF16, rows),
         ((m, d), F32, rows), ((m, d), BF16, rows)],
        [], 2 * m * d * (n + pk + d),
    )


def out_norm(mixed, resid, gains, w, clips, length):
    d = w.n

    def body(_s, ins, outs, _scr, wb, wait):
        wait(0, 0)
        x1 = ins[1][...].astype(F32) + dot_f32(ins[0][...], wb[0][...])
        outs[0][...] = x1
        outs[1][...] = to_low(normed(x1, ins[2][1:2, :]))

    m = clips * length
    outs = [((m, d), F32, rows_spec(length, d)), ((m, d), BF16, rows_spec(length, d))]
    return run_kernel(
        body, "out_norm", (clips,), [],
        [(mixed, rows_spec(length, d)), (resid, rows_spec(length, d)), (gains, full_spec((3, d)))], [(w, d)],
        outs, [], 2 * m * d * d,
    )


def gelu_parts(z):
    zz = z * z
    t = jnp.tanh(z * (GELU_C + (GELU_C * GELU_A) * zz))
    hz = 0.5 * z
    return hz + hz * t, hz, t, zz


def up_gelu(h_two, w, clips, length, tn, keep):
    d, n = w.k, w.n

    def body(_s, ins, outs, _scr, wb, wait):
        h = ins[0][...]

        def step(t, c):
            wait(0, t)
            at = pl.ds(pl.multiple_of(t * tn, tn), tn)
            z = dot_f32(h, wb[0][:, at])
            u, hz, tz, zz = gelu_parts(z)
            outs[0][:, at] = to_low(u)
            if keep:
                slope = 0.5 + 0.5 * tz + (hz - hz * (tz * tz)) * (GELU_C + (3.0 * GELU_C * GELU_A) * zz)
                outs[1][:, at] = to_low(slope)
            return c

        lax.fori_loop(0, n // tn, step, 0)

    m = clips * length
    outs = [((m, n), BF16, rows_spec(length, n))]
    if keep:
        outs += [((m, n), BF16, rows_spec(length, n))]
    return run_kernel(
        body, "up_gelu", (clips,), [], [(h_two, rows_spec(length, d))], [(w, tn)], outs, [], 2 * m * d * n,
    )


def down_left(hidden, resid, w, clips, length, kt):
    k, n = w.k, w.n

    def body(_s, ins, outs, _scr, wb, wait):
        wait(0, 0)
        outs[0][...] = ins[1][...]

        def step(t, c):
            at = pl.ds(pl.multiple_of(t * kt, kt), kt)
            outs[0][...] += dot_f32(ins[0][:, at], wb[0][at, :])
            return c

        lax.fori_loop(0, k // kt, step, 0)

    m = clips * length
    return run_kernel(
        body, "down_left", (clips,), [], [(hidden, rows_spec(length, k)), (resid, rows_spec(length, n))],
        [(w, n)], [((m, n), F32, rows_spec(length, n))], [], 2 * m * n * k,
    )[0]


def down_embed(hidden, resid, left, gains, lengths, w, w_proj, clips, length, kt, keep):
    d, k, pj, n = resid.shape[1], w.k, w_proj.n, w.n
    have = d - n

    def body(s_refs, ins, outs, scr, wb, wait):
        g = pl.program_id(0)
        wait(0, 0)
        if have:
            scr[0][:, :have] = ins[3][...]
        scr[0][:, have:] = ins[1][:, have:]

        def step(t, c):
            at = pl.ds(pl.multiple_of(t * kt, kt), kt)
            scr[0][:, have:] += dot_f32(ins[0][:, at], wb[0][at, :])
            return c

        lax.fori_loop(0, k // kt, step, 0)
        x2 = scr[0][...]
        size = s_refs[0][g]
        row = lax.broadcasted_iota(jnp.int32, (length, 1), 0)
        weight = jnp.where(row < size, 1.0 / size.astype(F32), 0.0)
        pooled = jnp.sum(normed(x2, ins[2][2:3, :]) * weight, axis=0, keepdims=True)
        scr[1][pl.ds(g, 1), :] = pooled
        if keep:
            outs[3][...] = x2
        wait(1, 0)

        @pl.when(g == clips - 1)
        def _():
            pool_all = scr[1][...]
            raw = dot_f32(to_low(pool_all), wb[1][...])
            outs[0][...] = to_low(unit_rows(raw))
            outs[1][...] = raw
            outs[2][...] = pool_all

    m = clips * length
    outs = [((clips, pj), BF16, full_spec((clips, pj))), ((clips, pj), F32, full_spec((clips, pj))),
            ((clips, d), F32, full_spec((clips, d)))]
    if keep:
        outs += [((m, d), F32, rows_spec(length, d))]
    ins = [(hidden, rows_spec(length, k)), (resid, rows_spec(length, d)), (gains, full_spec((3, d)))]
    if have:
        ins.append((left, rows_spec(length, have)))
    return run_kernel(
        body, "down_embed", (clips,), [lengths], ins, [(w, n), (w_proj, pj)], outs,
        [pltpu.VMEM((length, d), F32), pltpu.VMEM((clips, d), F32)], 2 * m * n * k,
    )


def attn_backward(qkv, d_mixed, lengths, clips, length, heads, first=0, so_far=None):
    d = qkv.shape[1] // 3
    hd = d // heads
    scale = hd ** (-0.5)
    per = 128 // hd

    def body(s_refs, ins, outs, _scr, _wb, _wait):
        qkv_ref, do_ref, out = ins[0], ins[1], outs[0]
        lane = lax.broadcasted_iota(jnp.int32, (1, 128), 1)
        ok = lax.broadcasted_iota(jnp.int32, (length, 1), 0) < s_refs[0][pl.program_id(0) + first]
        for t in range(d // 128):
            at = slice(t * 128, (t + 1) * 128)
            q, do = qkv_ref[:, at], do_ref[:, at]
            k = qkv_ref[:, d + t * 128 : d + (t + 1) * 128]
            v = qkv_ref[:, 2 * d + t * 128 : 2 * d + (t + 1) * 128]
            dq = dk = dv = None
            for h in range(per):
                mine = (lane >= h * hd) & (lane < (h + 1) * hd)
                qm = jnp.where(mine, q, jnp.zeros_like(q))
                dom = jnp.where(mine, do, jnp.zeros_like(do))
                sc = jnp.where(ok, dot_nt(k, qm) * scale, -1e30)
                e = jnp.exp(sc - jnp.max(sc, axis=0, keepdims=True))
                p = e * (1.0 / jnp.sum(e, axis=0, keepdims=True))
                dp = dot_nt(v, dom)
                ds = to_low(p * (dp - jnp.sum(p * dp, axis=0, keepdims=True)))
                dv_h = dot_f32(to_low(p), do)
                dq_h = dot_tn(ds, k)
                dk_h = dot_f32(ds, q)
                dq = dq_h if dq is None else jnp.where(mine, dq_h, dq)
                dk = dk_h if dk is None else jnp.where(mine, dk_h, dk)
                dv = dv_h if dv is None else jnp.where(mine, dv_h, dv)
            out[:, at] = to_low(dq * scale)
            out[:, d + t * 128 : d + (t + 1) * 128] = to_low(dk * scale)
            out[:, 2 * d + t * 128 : 2 * d + (t + 1) * 128] = to_low(dv)

    m = qkv.shape[0]
    rows = lambda n: pl.BlockSpec((length, n), lambda i, *_: (i + first, 0))
    ins = [(qkv, rows(3 * d)), (d_mixed, rows(d))] + ([] if so_far is None else [(so_far, hbm_spec())])
    return run_kernel(
        body, "attn_backward", (clips,), [lengths], ins, [], [((m, 3 * d), BF16, rows(3 * d))], [],
        10 * clips * length * length * 256 * heads, None if so_far is None else 2,
    )[0]


def norm_back(resid, gain, d_out):
    center = resid - jnp.mean(resid, axis=-1, keepdims=True)
    rate = lax.rsqrt(jnp.mean(center * center, axis=-1, keepdims=True) + NORM_EPS)
    unit = center * rate
    d_unit = d_out * gain
    tail = unit * jnp.mean(d_unit * unit, axis=-1, keepdims=True)
    return rate * (d_unit - jnp.mean(d_unit, axis=-1, keepdims=True) - tail), jnp.sum(d_out * unit, axis=0, keepdims=True)


def packed_rows(parts):
    return sum(k // 8 * n // w for k, n, w in parts)


def gradient_outs(parts, fast):
    if not fast:
        return [((k, n), F32, full_spec((k, n))) for k, n, _ in parts]
    shape = (4, packed_rows(parts), parts[0][2])
    return [(shape, BF16, full_spec(shape)), (shape, F32, full_spec(shape))]


def emit_gradients(parts, accs, outs, core, fast):
    if not fast:
        for acc, out in zip(accs, outs):
            out[...] = acc[...]
        return
    for yx in range(4):
        for out, c in ((outs[0], 1 - core), (outs[1], core)):
            at = 0
            for (k, n, width), acc in zip(parts, accs):
                rows = k // 8
                first = pl.multiple_of((2 * yx + c) * rows, rows)
                for j in range(n // width):
                    out[yx, at : at + rows, :] = acc[pl.ds(first, rows), j * width : (j + 1) * width].astype(out.dtype)
                    at += rows
                rest = n % width
                if rest:
                    k2 = width // rest
                    for i in range(k2):
                        sub = rows // k2
                        part = acc[pl.ds(pl.multiple_of(first + i * sub, sub), sub), n - rest : n]
                        out[yx, at : at + sub, i * rest : (i + 1) * rest] = part.astype(out.dtype)
                    at += rows // k2


def contrast_back(joined, embed_raw, first_row, pj, micro, per):
    rows = joined.shape[1]
    row = lax.broadcasted_iota(jnp.int32, (rows, rows), 0)
    col = lax.broadcasted_iota(jnp.int32, (rows, rows), 1)
    same = row == col
    lane = lax.broadcasted_iota(jnp.int32, (rows, 128), 1)
    allowed, count = [], 0.0
    for m in range(micro):
        ids = joined[m, :, 2 * pj :].astype(F32)
        left = jnp.where(lane == 0, ids, jnp.where(lane == 1, 1.0, 0.0))
        right = jnp.where(lane == 0, 1.0, jnp.where(lane == 1, -ids, 0.0))
        allowed.append((dot_nt(to_low(left), to_low(right)) != 0.0) | same)
        count = count + jnp.sum(allowed[m].astype(F32))
    scale = rows / count
    total, d_embed = 0.0, None
    pick_row = lax.broadcasted_iota(jnp.int32, (micro * per, rows), 0)
    pick_col = lax.broadcasted_iota(jnp.int32, (micro * per, rows), 1)
    for m in range(micro):
        image = joined[m, :, pj : 2 * pj]
        logits = dot_nt(joined[m, :, :pj], image) * LOGIT_SCALE
        masked = jnp.where(allowed[m], logits, -1e30)
        row_top, col_top = jnp.max(masked, axis=1, keepdims=True), jnp.max(masked, axis=0, keepdims=True)
        row_lse = row_top + jnp.log(jnp.sum(jnp.exp(masked - row_top), axis=1, keepdims=True))
        col_lse = col_top + jnp.log(jnp.sum(jnp.exp(masked - col_top), axis=0, keepdims=True))
        matched = jnp.sum(jnp.where(same, logits, 0.0))
        total = total + (jnp.sum(row_lse) - matched) + (jnp.sum(col_lse) - matched)
        d_logits = jnp.exp(masked - row_lse) + jnp.exp(masked - col_lse) - jnp.where(same, 2.0, 0.0)
        here = (pick_row >= m * per) & (pick_row < (m + 1) * per) & (pick_col == first_row + pick_row - m * per)
        own = jnp.dot(here.astype(F32), d_logits * (scale * LOGIT_SCALE), precision=HIGHEST, preferred_element_type=F32)
        part = jnp.dot(own, image.astype(F32), precision=HIGHEST, preferred_element_type=F32)
        d_embed = part if d_embed is None else d_embed + part
    rate = lax.rsqrt(jnp.sum(embed_raw * embed_raw, axis=-1, keepdims=True) + NORM_EPS)
    inner = jnp.sum(embed_raw * d_embed, axis=-1, keepdims=True)
    return total * scale, rate * d_embed - embed_raw * (rate * rate * rate * inner)


def down_backward(joined, embed_raw, pooled, resid_out, hidden, slope, gains, lengths, place, w, w_proj, clips, length,
                  fast):
    k, d, pj = w.k, w.n, w_proj.n
    kt = d
    parts = [(k, d, d), (d, pj, d)]

    def body(s_refs, ins, outs, scr, wb, wait):
        g = pl.program_id(0)
        sizes, at = s_refs
        joined_ref, raw_ref, pooled_ref, x2_ref, u_ref, slope_ref, gain_ref = ins
        loss_ref, dpre_ref, dout_ref, g3_ref = outs[:4]
        d_pooled, d_raw_ref, acc = scr
        wait(1, 0)

        @pl.when(g == 0)
        def _():
            loss, d_raw = contrast_back(joined_ref[...], raw_ref[...], at[1], pj, MICRO, clips // MICRO)
            loss_ref[...] = jnp.full((1, 128), loss, F32)
            d_raw_ref[...] = to_low(d_raw)
            d_pooled[...] = dot_nt(to_low(d_raw), wb[1][...])
            acc[...] = jnp.zeros_like(acc)
            g3_ref[...] = jnp.zeros_like(g3_ref)

        size = sizes[g]
        row = lax.broadcasted_iota(jnp.int32, (length, 1), 0)
        weight = jnp.where(row < size, 1.0 / size.astype(F32), 0.0)
        d_out, g_three = norm_back(x2_ref[...], gain_ref[2:3, :], d_pooled[pl.ds(g, 1), :] * weight)
        g3_ref[...] += g_three
        dout_ref[...] = d_out
        d_low = to_low(d_out)
        wait(0, 0)

        def step(t, c):
            cols = pl.ds(pl.multiple_of(t * kt, kt), kt)
            d_hidden = dot_nt(d_low, wb[0][cols, :])
            dpre_ref[:, cols] = to_low(d_hidden * slope_ref[:, cols].astype(F32))
            acc[cols, :] += dot_tn(u_ref[:, cols], d_low)
            return c

        lax.fori_loop(0, k // kt, step, 0)

        @pl.when(g == clips - 1)
        def _():
            g_proj = dot_tn(to_low(pooled_ref[...]), d_raw_ref[...])
            outs[6][...] = g_proj
            emit_gradients(parts, [acc, outs[6]], outs[4:6], at[0], fast)

    m = clips * length
    outs = [((1, 128), F32, full_spec((1, 128))), ((m, k), BF16, rows_spec(length, k)),
            ((m, d), F32, rows_spec(length, d)), ((1, d), F32, full_spec((1, d)))]
    outs += gradient_outs(parts, fast) + [((d, pj), F32, full_spec((d, pj)))]
    ins = [(joined, full_spec(joined.shape)), (embed_raw, full_spec((clips, pj))), (pooled, full_spec((clips, d))),
           (resid_out, rows_spec(length, d)), (hidden, rows_spec(length, k)), (slope, rows_spec(length, k)),
           (gains, full_spec((3, d)))]
    return run_kernel(
        body, "down_backward", (clips,), [lengths, place], ins, [(w, d), (w_proj, pj)], outs,
        [pltpu.VMEM((clips, d), F32), pltpu.VMEM((clips, pj), BF16), pltpu.VMEM((k, d), F32)], 4 * m * d * k,
    )


def up_backward(d_pre, h_two, resid_mid, d_out, mixed, gains, place, w, w_out, clips, length, kt, fast):
    d, n = w.k, w.n
    parts = [(d, n, d), (d, d, d)]

    def body(s_refs, ins, outs, scr, wb, wait):
        g = pl.program_id(0)
        (at,) = s_refs
        dpre_ref, h_ref, x1_ref, dout_ref, o_ref, gain_ref = ins
        dmid_ref, dmix_ref, g2_ref = outs[:3]
        acc, acc_out, back = scr

        @pl.when(g == 0)
        def _():
            acc[...] = jnp.zeros_like(acc)
            acc_out[...] = jnp.zeros_like(acc_out)
            g2_ref[...] = jnp.zeros_like(g2_ref)

        h = h_ref[...]
        back[...] = jnp.zeros_like(back)

        def step(t, c):
            cols = pl.ds(pl.multiple_of(t * kt, kt), kt)
            wait(0, t)
            dp = dpre_ref[:, cols]
            acc[:, cols] += dot_tn(h, dp)
            back[...] += dot_nt(dp, wb[0][:, cols])
            return c

        lax.fori_loop(0, n // kt, step, 0)
        d_ln, g_two = norm_back(x1_ref[...], gain_ref[1:2, :], back[...])
        g2_ref[...] += g_two
        d_mid = dout_ref[...] + d_ln
        dmid_ref[...] = d_mid
        d_low = to_low(d_mid)
        wait(1, 0)
        acc_out[...] += dot_tn(o_ref[...], d_low)
        dmix_ref[...] = to_low(dot_nt(d_low, wb[1][...]))

        @pl.when(g == clips - 1)
        def _():
            emit_gradients(parts, [acc, acc_out], outs[3:5], at[0], fast)

    m = clips * length
    rows = rows_spec(length, d)
    outs = [((m, d), F32, rows), ((m, d), BF16, rows), ((1, d), F32, full_spec((1, d)))] + gradient_outs(parts, fast)
    ins = [(d_pre, rows_spec(length, n)), (h_two, rows), (resid_mid, rows), (d_out, rows), (mixed, rows),
           (gains, full_spec((3, d)))]
    return run_kernel(
        body, "up_backward", (clips,), [place], ins, [(w, kt), (w_out, d)], outs,
        [pltpu.VMEM((d, n), F32), pltpu.VMEM((d, d), F32), pltpu.VMEM((length, d), F32)], 4 * m * d * (n + d),
    )


def qkv_backward(d_qkv, h_one, resid_in, d_mid, patches, gains, g_two, g_three, place, w, clips, length, fast):
    d, n, pk = w.k, w.n, patches.shape[1]
    parts = [(d, n, d), (pk, d, d)]
    extra = 16

    def body(s_refs, ins, outs, scr, wb, wait):
        g = pl.program_id(0)
        (at,) = s_refs
        dqkv_ref, h_ref, x0_ref, dmid_ref, patch_ref, gain_ref, g2_ref, g3_ref = ins
        acc, acc_patch, back, acc_gain = scr

        @pl.when(g == 0)
        def _():
            acc[...] = jnp.zeros_like(acc)
            acc_patch[...] = jnp.zeros_like(acc_patch)
            acc_gain[...] = jnp.zeros_like(acc_gain)
            acc_gain[1:2, :] = g2_ref[...]
            acc_gain[2:3, :] = g3_ref[...]

        h = h_ref[...]
        back[...] = jnp.zeros_like(back)

        def step(t, c):
            cols = pl.ds(pl.multiple_of(t * d, d), d)
            wait(0, t)
            dq = dqkv_ref[:, cols]
            acc[:, cols] += dot_tn(h, dq)
            back[...] += dot_nt(dq, wb[0][:, cols])
            return c

        lax.fori_loop(0, n // d, step, 0)
        d_ln, g_one = norm_back(x0_ref[...], gain_ref[0:1, :], back[...])
        acc_gain[0:1, :] += g_one
        acc_patch[...] += dot_tn(patch_ref[...], to_low(dmid_ref[...] + d_ln))

        @pl.when(g == clips - 1)
        def _():
            emit_gradients(parts, [acc, acc_patch], outs[:2], at[0], fast)
            if fast:
                rows = packed_rows(parts)
                for yx in range(4):
                    for out in outs[:2]:
                        out[yx, rows : rows + extra, :] = acc_gain[...].astype(out.dtype)
            else:
                outs[2][...] = acc_gain[...]

    m = clips * length
    rows = rows_spec(length, d)
    if fast:
        shape = (4, packed_rows(parts) + extra, d)
        outs = [(shape, BF16, full_spec(shape)), (shape, F32, full_spec(shape))]
    else:
        outs = gradient_outs(parts, fast) + [((extra, d), F32, full_spec((extra, d)))]
    ins = [(d_qkv, rows_spec(length, n)), (h_one, rows), (resid_in, rows), (d_mid, rows),
           (patches, rows_spec(length, pk)), (gains, full_spec((3, d))), (g_two, full_spec((1, d))),
           (g_three, full_spec((1, d)))]
    return run_kernel(
        body, "qkv_backward", (clips,), [place], ins, [(w, d)], outs,
        [pltpu.VMEM((d, n), F32), pltpu.VMEM((pk, d), F32), pltpu.VMEM((length, d), F32), pltpu.VMEM((extra, d), F32)],
        4 * m * d * n,
    )


AXES = ("dp", "rep")


def joint_perm(reps, fn):
    out = []
    for dp in range(8):
        for z in range(reps):
            dst = fn(dp, z)
            if dst is not None:
                out.append((dp * reps + z, dst[0] * reps + dst[1]))
    return out


def send(value, reps, fn):
    return lax.ppermute(value, AXES, joint_perm(reps, fn))


class Ring:
    def __init__(self, packed, col, width, reps):
        self.own, self.col, self.width, self.reps = packed, col, width, reps
        self.mine = packed[:, col : col + width]

    def first(self):
        self.near = send(self.mine, self.reps, lambda dp, z: (dp ^ (2 if z % 2 == 0 else 4), z))

    def second(self):
        self.diag = send(self.near, self.reps, lambda dp, z: (dp ^ (4 if z % 2 == 0 else 2), z))
        self.other = send(self.near, self.reps, lambda dp, z: (dp, z ^ 1))

    def twin(self, *names):
        for name in names:
            setattr(self, name + "_twin", send(getattr(self, name), self.reps, lambda dp, z: (dp ^ 1, z)))

    def group(self, own_twin):
        odd = lax.axis_index("rep") % 2 == 1
        x, y = jnp.int32(2), jnp.int32(4)
        flip = jnp.stack([jnp.int32(0), jnp.where(odd, y, x), jnp.int32(6), jnp.where(odd, x, y)])
        base = jnp.bitwise_xor(flip, lax.axis_index("dp").astype(jnp.int32))
        arrays = [self.own, self.near, self.diag, self.other, own_twin, self.near_twin, self.diag_twin, self.other_twin]
        index = jnp.concatenate([base, jnp.bitwise_xor(base, 1)])
        return Group(arrays, index, self.own.shape[0], (self.col, 0, 0, 0) * 2)


def fence(held, values):
    flat = [(r, n) for r, names in held for n in names.split()]
    out = lax.optimization_barrier(tuple(getattr(r, n) for r, n in flat) + tuple(values))
    for (r, n), v in zip(flat, out):
        setattr(r, n, v)
    return out[len(flat) :]


def take(v, i, axis):
    return lax.dynamic_index_in_dim(v, i, axis, keepdims=False)


def from_width(v, rows, n):
    width = v.shape[-1]
    full = n // width
    blocks = [v[i * rows : (i + 1) * rows] for i in range(full)]
    rest = n % width
    if rest:
        last, k = v[full * rows :], width // rest
        blocks.append(jnp.concatenate([last[:, i * rest : (i + 1) * rest] for i in range(k)], axis=0))
    return jnp.concatenate(blocks, axis=1)


class Sum:
    def __init__(self, leave, stay, parts, reps):
        self.reps, self.leave, self.stay, self.parts = reps, leave, stay, parts
        me = lax.axis_index("dp")
        self.y, self.x = me // 4, (me // 2) % 2
        self.odd = lax.axis_index("rep") % 2 == 1

    def hops(self, *pairs):
        self.due = [(to_low(v), fn) for v, fn in pairs]

    def core(self):
        self.hops((self.leave, lambda dp, z: (dp ^ 1, z)))

    def plane(self):
        s = (self.stay + self.got[0].astype(F32)).reshape((2, 2) + self.stay.shape[1:])
        half = s.shape[-2] // 2
        self.a, self.b = s[:, :, :half], s[:, :, half:]
        self.hops((take(self.a, 1 - self.x, 1), lambda dp, z: (dp ^ 2, z)),
                  (take(self.b, 1 - self.y, 0), lambda dp, z: (dp ^ 4, z)))

    def plane_again(self):
        self.a = take(self.a, self.x, 1) + self.got[0].astype(F32)
        self.b = take(self.b, self.y, 0) + self.got[1].astype(F32)
        self.hops((take(self.a, 1 - self.y, 0), lambda dp, z: (dp ^ 4, z)),
                  (take(self.b, 1 - self.x, 0), lambda dp, z: (dp ^ 2, z)))

    def pair(self):
        a = take(self.a, self.y, 0) + self.got[0].astype(F32)
        b = take(self.b, self.x, 0) + self.got[1].astype(F32)
        self.a = jnp.where(self.odd, b, a)
        self.hops((jnp.where(self.odd, a, b), lambda dp, z: (dp, z ^ 1)))

    def across(self):
        self.a = to_low(self.a + self.got[0].astype(F32))
        self.hops((self.a, lambda dp, z: (dp, z ^ 2)))

    def share(self):
        self.a = to_low(self.a.astype(F32) + self.got[0].astype(F32))
        self.hops((self.a, lambda dp, z: (dp, z ^ 1)))

    def result(self):
        other = self.got[0]
        total = jnp.concatenate([jnp.where(self.odd, other, self.a), jnp.where(self.odd, self.a, other)], axis=0)
        total, out, at = total.astype(F32), [], 0
        for k, n, width in self.parts:
            rows = k // 8
            size = rows * n // width
            out.append(from_width(total[at : at + size], rows, n))
            at += size
        return out


def go(sums, *values):
    flat = [v for s in sums for v, _ in s.due]
    out = lax.optimization_barrier(tuple(flat) + values)
    at = 0
    for s in sums:
        s.got = tuple(send(out[at + i], s.reps, fn) for i, (_, fn) in enumerate(s.due))
        at += len(s.due)
    return out[at:]


def order(sums, *values):
    flat = [g for s in sums for g in s.got]
    out = lax.optimization_barrier(tuple(flat) + values)
    at = 0
    for s in sums:
        s.got = out[at : at + len(s.got)]
        at += len(s.got)
    return out[at:]


def adam_step(weight, gradient, moment_one, moment_two, step_rate, decay):
    first_new = BETA_ONE * moment_one + (1.0 - BETA_ONE) * gradient
    second_new = BETA_TWO * moment_two + (1.0 - BETA_TWO) * gradient * gradient
    fixed_one = first_new / (1.0 - BETA_ONE**STEP)
    fixed_two = second_new / (1.0 - BETA_TWO**STEP)
    update = fixed_one / (jnp.sqrt(fixed_two) + ADAM_EPS) + decay * weight
    return (weight - step_rate * update, first_new, second_new)


def as_columns(v, rows):
    return jnp.concatenate([v[i * rows : (i + 1) * rows] for i in range(v.shape[0] // rows)], axis=1)


def local(dp_size, rep_size, *args):
    (audio_patches, clip_lengths, video_ids, image_tokens, i_qkv, i_out, i_up, i_down, i_proj, i_gains) = args[:10]
    masters, firsts_in, seconds_in = args[10:17], args[17:24], args[24:31]
    a_patch, a_qkv, a_out, a_up, a_down, a_proj, a_gains = (to_low(w) for w in masters)
    fast = dp_size == 8 and rep_size == 4
    clip_dev = audio_patches.shape[1]
    clips = MICRO * clip_dev
    d_i, d_a, ff_a, pj = i_out.shape[1], a_out.shape[1], a_up.shape[1], a_proj.shape[1]
    ff_i = i_up.shape[1]

    rp = a_patch.shape[0]
    small = jnp.concatenate(
        [a_patch, jnp.pad(a_gains.reshape(1, -1), ((0, 0), (0, d_a - a_gains.size))),
         jnp.pad(i_gains.reshape(1, -1), ((0, 0), (0, d_a - i_gains.size)))], axis=0)
    small = lax.all_gather(small, "dp", axis=0)
    img_sizes = jnp.full((clips,), IMG_LEN, jnp.int32)
    tokens = image_tokens.reshape(clips * IMG_LEN, d_i)
    sizes = clip_lengths.reshape(clips)
    patches = jnp.pad(audio_patches.reshape(clips, LEN, -1), ((0, 0), (0, PAD_LEN - LEN), (0, 0)))
    patches = patches.reshape(clips * PAD_LEN, -1)
    half, sub_i, sub_a = ff_i // 2, ff_i // d_i, ff_a // d_a
    dl = d_i * 3 // 5
    if fast:
        down_a = as_columns(a_down, a_qkv.shape[0])
        own_a = jnp.concatenate([a_qkv, a_out, a_up, down_a, a_proj], axis=1)
        small, own_a, i_qkv, i_out, i_up, i_down, i_proj = lax.optimization_barrier(
            (small, own_a, i_qkv, i_out, i_up, i_down, i_proj))
        down_i = as_columns(i_down, i_qkv.shape[0])
        left = [down_i[:, j * d_i : j * d_i + dl] for j in range(sub_i)]
        right = [down_i[:, j * d_i + dl : (j + 1) * d_i] for j in range(sub_i)]
        own_i = jnp.concatenate([i_qkv, i_out, i_up, i_proj] + left + right, axis=1)
        cut_a = 4 * d_a
        ca = Ring(own_a, 0, cut_a, rep_size), Ring(own_a, cut_a, own_a.shape[1] - cut_a, rep_size)
        widths, at, ci = [3 * d_i, d_i + half, half + pj, sub_i * dl, sub_i * (d_i - dl)], 0, []
        for wd in widths:
            ci.append(Ring(own_i, at, wd, rep_size))
            at += wd
        swap = lambda v: send(v, rep_size, lambda dp, z: (dp ^ 1, z))
        twin_a = swap(own_a)

        ca[0].first()
        (own_i,) = fence([(ca[0], "near"), (ca[1], "mine")] + [(c, "mine") for c in ci], (own_i,))
        ca[0].second()
        ca[0].twin("near")
        ca[1].first()
        patches, twin_a = fence([(ca[0], "diag other near_twin"), (ca[1], "near"), (ci[0], "mine")], (patches, twin_a))
        ca[0].twin("diag", "other")
        ca[1].second()
        ca[1].twin("near")
        ci[0].first()
        ga0 = ca[0].group(twin_a)
        wa_qkv = Weight(d_a, 3 * d_a, [(ga0, 0, 3 * d_a, 0, 0)])
        wa_out = Weight(d_a, d_a, [(ga0, 3 * d_a, d_a, 0, 0)])
    else:
        whole = lambda v: lax.all_gather(v, "dp", axis=0, tiled=True)
        make = lambda v: Weight(v.shape[0] * dp_size, v.shape[1], whole=whole(v))
        cut = lambda v: Weight(v.shape[0], v.shape[1], whole=v)
        wi_qkv, wi_out, wi_up, wi_proj = (make(v) for v in (i_qkv, i_out, i_up, i_proj))
        wi_left, wi_right = cut(whole(i_down)[:, :dl]), cut(whole(i_down)[:, dl:])
        wa_qkv, wa_out, wa_up, wa_down, wa_proj = (make(v) for v in (a_qkv, a_out, a_up, a_down, a_proj))

    w_patch = small[:, :rp].reshape(rp * dp_size, d_a)
    unpack = lambda v, g: v[:, : g.size].reshape(dp_size, 3, -1).transpose(1, 0, 2).reshape(3, -1).astype(F32)
    gains_a, gains_i = unpack(small[:, rp], a_gains), unpack(small[:, rp + 1], i_gains)

    resid_in, h_one, qkv, mixed, resid_mid, h_two = audio_attention(
        patches, w_patch, gains_a, sizes, wa_qkv, wa_out, clips, PAD_LEN, HEADS_A)

    if fast:
        (h_two,) = fence([(ca[1], "diag other near_twin"), (ci[0], "near"), (ci[1], "mine")], (h_two,))
        ca[1].twin("diag", "other")
        ci[0].second()
        ci[0].twin("near")
        ci[1].first()
        twin_i = swap(own_i)
        ga1 = ca[1].group(twin_a)
        wa_up = Weight(d_a, ff_a, [(ga1, 0, ff_a, 0, 0)])
        wa_down = Weight(ff_a, d_a, [(ga1, ff_a + j * d_a, d_a, 0, j) for j in range(sub_a)], sub=sub_a)
        wa_proj = Weight(d_a, pj, [(ga1, 2 * ff_a, pj, 0, 0)])
    got = up_gelu(h_two, wa_up, clips, PAD_LEN, 1024, True)
    hidden, slope = got[:2]

    if fast:
        hidden, tokens, twin_i = fence(
            [(ci[0], "diag other near_twin"), (ci[1], "near"), (ci[2], "mine")], (hidden, tokens, twin_i))
        ci[0].twin("diag", "other")
        ci[1].second()
        ci[1].twin("near")
        ci[2].first()
        gi = [ci[0].group(twin_i)]
        wi_qkv = Weight(d_i, 3 * d_i, [(gi[0], 0, 3 * d_i, 0, 0)])
    mixed_i = image_attention(tokens, gains_i, wi_qkv, clips, IMG_LEN, HEADS_I, d_i)

    if fast:
        mixed_i, hidden = fence(
            [(ci[1], "diag other near_twin"), (ci[2], "near"), (ci[3], "mine")], (mixed_i, hidden))
        ci[1].twin("diag", "other")
        ci[2].second()
        ci[2].twin("near")
        ci[3].first()
        gi.append(ci[1].group(twin_i))
        wi_out = Weight(d_i, d_i, [(gi[1], 0, d_i, 0, 0)])
    got = down_embed(hidden, resid_mid, None, gains_a, sizes, wa_down, wa_proj, clips, PAD_LEN, d_a, True)
    aud_emb, embed_raw, pooled, resid_out = got[:4]
    mid_i, h_two_i = out_norm(mixed_i, tokens, gains_i, wi_out, clips, IMG_LEN)

    if fast:
        h_two_i, aud_emb = fence(
            [(ci[2], "diag other near_twin"), (ci[3], "near"), (ci[4], "mine")], (h_two_i, aud_emb))
        ci[2].twin("diag", "other")
        ci[3].second()
        ci[3].twin("near")
        ci[4].first()
        gi.append(ci[2].group(twin_i))
        wi_up = Weight(d_i, ff_i, [(gi[1], d_i, half, 0, 0), (gi[2], 0, half, half, 0)])
        wi_proj = Weight(d_i, pj, [(gi[2], half, pj, 0, 0)])
    hidden_i = up_gelu(h_two_i, wi_up, clips, IMG_LEN, d_i, False)[0]

    if fast:
        (hidden_i,) = fence([(ci[3], "diag other near_twin"), (ci[4], "near")], (hidden_i,))
        ci[3].twin("diag", "other")
        ci[4].second()
        ci[4].twin("near")
        gi.append(ci[3].group(twin_i))
        wi_left = Weight(ff_i, dl, [(gi[3], j * dl, dl, 0, j) for j in range(sub_i)], sub=sub_i)
    left_i = down_left(hidden_i, mid_i, wi_left, clips, IMG_LEN, d_i)

    if fast:
        (left_i,) = fence([(ci[4], "diag other near_twin")], (left_i,))
        ci[4].twin("diag", "other")
        gi.append(ci[4].group(twin_i))
        dr = d_i - dl
        wi_right = Weight(ff_i, dr, [(gi[4], j * dr, dr, 0, j) for j in range(sub_i)], sub=sub_i)
    img_emb = down_embed(hidden_i, mid_i, left_i, gains_i, img_sizes, wi_right, wi_proj, clips, IMG_LEN, d_i, False)[0]

    ids_low = jnp.broadcast_to(to_low(video_ids.reshape(clips, 1)), (clips, 128))
    joined = jnp.concatenate([aud_emb, img_emb, ids_low], axis=1).reshape(MICRO, clip_dev, 2 * pj + 128)
    joined = lax.all_gather(lax.all_gather(joined, "rep", axis=1, tiled=True), "dp", axis=1, tiled=True)
    me = lax.axis_index("dp").astype(jnp.int32)
    first_row = lax.axis_index(AXES).astype(jnp.int32) * clip_dev
    place = jnp.stack([me % 2, first_row])
    got = down_backward(joined, embed_raw, pooled, resid_out, hidden, slope, gains_a, sizes, place, wa_down, wa_proj,
                        clips, PAD_LEN, fast)
    loss, d_pre, d_out, g_three = got[0][0, 0], *got[1:4]
    if fast:
        s_down = Sum(got[4], got[5], [(ff_a, d_a, d_a), (d_a, pj, d_a)], rep_size)
        s_down.core()
        (d_pre,) = go([s_down], d_pre)
    up = up_backward(d_pre, h_two, resid_mid, d_out, mixed, gains_a, place, wa_up, wa_out, clips, PAD_LEN, 1024, fast)
    d_mid, d_mixed, g_two = up[:3]
    if fast:
        (d_mixed,) = order([s_down], d_mixed)
        s_down.plane()
        s_up = Sum(up[3], up[4], [(d_a, ff_a, d_a), (d_a, d_a, d_a)], rep_size)
        s_up.core()
        (d_mixed,) = go([s_down, s_up], d_mixed)
    done, d_qkv = 0, None
    calls = [clip_dev, (clips - clip_dev) // 2, clips - clip_dev - (clips - clip_dev) // 2]
    for turn, count in enumerate(calls):
        if count:
            d_qkv = attn_backward(qkv, d_mixed, sizes, count, PAD_LEN, HEADS_A, done, d_qkv)
        done += count
        if fast:
            if turn == 0:
                d_qkv, d_mixed = order([s_down, s_up], d_qkv, d_mixed)
                s_down.plane_again()
                s_up.plane()
                d_qkv, d_mixed = go([s_down, s_up], d_qkv, d_mixed)
            elif turn == 1:
                d_qkv, d_mixed = order([s_down], d_qkv, d_mixed)
                s_down.pair()
                d_qkv, d_mixed = go([s_down], d_qkv, d_mixed)
            else:
                (d_qkv,) = order([s_down, s_up], d_qkv)
                s_down.across()
                s_up.plane_again()
                (d_qkv,) = go([s_down, s_up], d_qkv)
    last = qkv_backward(d_qkv, h_one, resid_in, d_mid, patches, gains_a, g_two, g_three, place, wa_qkv, clips, PAD_LEN,
                        fast)
    share = d_a // dp_size
    mine = lambda v: lax.dynamic_slice_in_dim(v[:3], me * share, share, 1)
    if fast:
        leave, stay = order([s_down, s_up], last[0], last[1])
        s_qkv = Sum(leave, stay, [(d_a, 3 * d_a, d_a), (w_patch.shape[0], d_a, d_a), (128, d_a, d_a)], rep_size)
        s_qkv.core()
        s_down.share()
        s_up.pair()
        go([s_qkv, s_up, s_down])
        order([s_qkv])
        s_qkv.plane()
        go([s_qkv])
        order([s_up])
        s_up.across()
        go([s_up])
        order([s_qkv])
        s_qkv.plane_again()
        go([s_qkv])
        order([s_qkv])
        s_qkv.pair()
        go([s_qkv])
        order([s_qkv, s_up])
        s_qkv.across()
        s_up.share()
        go([s_qkv, s_up])
        s_qkv.share()
        go([s_qkv])
        r_down, r_proj = s_down.result()
        r_up, r_out = s_up.result()
        r_qkv, r_patch, r_gain = s_qkv.result()
        summed = [r_patch, r_qkv, r_out, r_up, r_down, r_proj, mine(r_gain)]
    else:
        grads = (last[1], last[0], up[4], up[3], got[4], got[5])
        summed = [lax.psum(lax.psum_scatter(v, "dp", scatter_dimension=0, tiled=True), "rep") for v in grads]
        summed.append(mine(lax.psum(last[2], AXES)))
    local_squares = sum(jnp.sum(v * v) for v in summed)
    grad_norm = jnp.sqrt(lax.psum(local_squares, "dp"))
    factor = jnp.minimum(1.0, CLIP_NORM / grad_norm)
    results = []
    for index in range(7):
        step_rate = RATE_GAIN if index == 6 else RATE_MATRIX
        decay = 0.0 if index == 6 else WEIGHT_DECAY
        results.append(
            adam_step(masters[index], summed[index] * factor, firsts_in[index], seconds_in[index], step_rate, decay)
        )
    return (loss, grad_norm, *(r[0] for r in results), *(r[1] for r in results), *(r[2] for r in results))


def solution(mesh):
    batch4 = P(None, AXES, None, None)
    batch2 = P(None, AXES)
    split = P("dp", None)
    gain = P(None, "dp")
    weights = (split,) * 6 + (gain,)
    placed = (batch4, batch2, batch2, batch4) + (split,) * 5 + (gain,) + weights * 3
    return jax.shard_map(
        functools.partial(local, mesh.shape["dp"], mesh.shape["rep"]),
        mesh=mesh,
        in_specs=placed,
        out_specs=(P(), P()) + weights * 3,
        check_vma=False,
    )
```
